32 devices in a mesh: head: 4 (over x, core), blk: 8 (over z, y).
Axes of the slice: x: 2, y: 2, z: 4, core: 2. Of those that a mesh axis runs over, the one named last changes fastest.
Arguments:
- inputs: bfloat16 [4, 1024, 768], P('head', 'blk'), may hold values from -6 to 6
- segments: int32 [4, 1024], P('head', 'blk'), may hold values from 0 to 10, as said below
- w_query: bfloat16 [768, 768], P(('head', 'blk')), may hold values from -0.109375 to 0.109375
- w_key: bfloat16 [768, 768], P(('head', 'blk')), may hold values from -0.109375 to 0.109375
- w_value: bfloat16 [768, 768], P(('head', 'blk')), may hold values from -0.21875 to 0.21875
- w_out: bfloat16 [768, 768], P(('head', 'blk')), may hold values from -0.875 to 0.875
- w_in: bfloat16 [768, 3072], P(('head', 'blk')), may hold values from -0.21875 to 0.21875
- w_back: bfloat16 [3072, 768], P(('head', 'blk')), may hold values from -0.109375 to 0.109375
- w_proj: bfloat16 [768, 128], P(('head', 'blk')), may hold values from -0.21875 to 0.21875
- gain_attn: bfloat16 [768], P(('head', 'blk')), may hold values from 0.5 to 1.5
- gain_ffn: bfloat16 [768], P(('head', 'blk')), may hold values from 0.5 to 1.5
- gain_final: bfloat16 [768], P(('head', 'blk')), may hold values from 0.5 to 1.5
- rel_table: bfloat16 [32, 12], replicated, may hold values from -4 to 4
- cotangent: bfloat16 [4, 1024, 128], P('head', 'blk'), may hold values from -6 to 6
Outputs:
- states: bfloat16 [4, 1024, 128], P('head', 'blk')
- input_gradient_rows: float32 [4, 1024, 768], P('head', 'blk')
- grad_query: float32 [768, 768], P(('head', 'blk'))
- grad_key: float32 [768, 768], P(('head', 'blk'))
- grad_value: float32 [768, 768], P(('head', 'blk'))
- grad_out: float32 [768, 768], P(('head', 'blk'))
- grad_in: float32 [768, 3072], P(('head', 'blk'))
- grad_back: float32 [3072, 768], P(('head', 'blk'))
- grad_proj: float32 [768, 128], P(('head', 'blk'))
- grad_gain_attn: float32 [768], P(('head', 'blk'))
- grad_gain_ffn: float32 [768], P(('head', 'blk'))
- grad_gain_final: float32 [768], P(('head', 'blk'))
- grad_table: float32 [32, 12], replicated
The draws below stay inside these ranges and needn't reach their ends.
Inputs may be any that keep to these rules, and one draw needn't show every extreme that they name: `segments`: within each of the 4 sequences the numbers start at 0 at the first position and never fall; equal numbers mark one document. In one sequence, drawn from the seed, a single document covers all positions from 127 to 896.
All inputs are finite; a program needn't handle non-finite values.
Results may differ from the reference program's by a relative error of at most 0.014.
The reference program's roundings to bfloat16 on the way count: a program that leaves them out, or rounds other values in their place, can miss the bound.
Values may be sent and summed in bfloat16 or wider, within the bound.
No kernel may reach another device: no remote copies, remote signals or barrier semaphores. Data moves between devices by JAX's collectives and lax.ppermute only.
A program may use at most 192 MiB of HBM per device.

```python
import jax
import jax.numpy as jnp
from jax import lax

D = 768
FF = 3072
HEADS = 12
HEAD_DIM = 64
PROJ = 128
BUCKETS = 32
TOK_DEV = 128
SEQS = 4
SEQ_LEN = 1024


def draw_segments(key, part):
    picked = jax.random.randint(jax.random.fold_in(key, 1), (), 0, SEQS)
    cut_count = SEQ_LEN // 128 + 2
    uniform_ints = jax.random.randint(jax.random.fold_in(key, 2), (SEQS, cut_count), 0, 1024)
    cubed = uniform_ints * uniform_ints // 1024 * uniform_ints // 1024
    ordered = jnp.sort(cubed, axis=1)
    steps_index = jnp.arange(cut_count, dtype=jnp.int32)[None, :]
    location = 1 + ordered * (SEQ_LEN - 1 - cut_count) // 1024 + steps_index
    flipped = jax.random.randint(jax.random.fold_in(key, 3), (SEQS, 1), 0, 2)
    location = jnp.where(flipped == 1, SEQ_LEN - location, location)
    ending = jax.random.randint(jax.random.fold_in(key, 4), (SEQS, cut_count), 0, 2)
    nearby = 1 + location % (TOK_DEV - 1)
    nearby = jnp.where(ending == 1, SEQ_LEN - nearby, nearby)
    row_index = jnp.arange(SEQS, dtype=jnp.int32)[:, None]
    location = jnp.where(row_index == picked, nearby, location)
    starts = jnp.zeros((SEQS, SEQ_LEN), jnp.int32).at[jnp.broadcast_to(row_index, location.shape), location].set(1)
    return jnp.cumsum(starts, axis=1).astype(jnp.int32)


def spiked(values, key, source, target, blocks, factor):
    def block_of(axis_at):
        return (jnp.arange(values.shape[axis_at]) // (values.shape[axis_at] // blocks)).reshape((-1,) + (1,) * (values.ndim - 1 - axis_at))

    first = jax.random.permutation(key, blocks)[block_of(target)]
    far = (block_of(target) + blocks // 2) % blocks
    return jnp.where((block_of(source) == first) | (block_of(source) == far), factor * values, values)


def shard_levels(own_key, extent, cuts, smallest, top_value):
    def one(position, blocks):
        draws = jax.random.uniform(jax.random.fold_in(jax.random.fold_in(own_key, 6), position), (blocks,), jnp.float32, smallest / len(cuts), top_value / len(cuts))
        return jnp.repeat(jnp.exp(draws), extent[position] // blocks).reshape((-1,) + (1,) * (len(extent) - position - 1))

    gain = one(*cuts[0])
    for cut in cuts[1:]:
        gain = gain * one(*cut)
    return gain


def scatter_about(stream_key, extent, deviation, reach, cuts=(), kind=jnp.bfloat16):
    entries = deviation * jax.random.normal(stream_key, extent, jnp.float32)
    if cuts:
        entries = entries * shard_levels(stream_key, extent, cuts, -0.22, 0.18)
    return jnp.clip(entries, -reach, reach).astype(kind)


def bell_draw_with(key, dims, width, reach, shards, heavy, kind=jnp.bfloat16):
    values = width * jax.random.normal(key, dims, jnp.float32)
    if shards:
        values = values * shard_levels(key, dims, shards, -0.22, 0.18)
    return jnp.clip(spiked(values, jax.random.fold_in(key, 3), *heavy), -reach, reach).astype(kind)


def setup_inputs(seed: int = 0) -> dict:
    streams_of = jax.random.split(jax.random.key(seed), 15)
    inputs = bell_draw_with(streams_of[0], (SEQS, SEQ_LEN, D), 1.0, 6.0, ((0, 4), (1, 8)), (1, 2, 8, 2.0))
    segments = draw_segments(jax.random.fold_in(streams_of[14], 71), 0)
    w_query = scatter_about(streams_of[2], (D, D), (0.5 * D ** -0.5), 0.109375, ((0, 32),))
    w_key = scatter_about(streams_of[3], (D, D), (0.5 * D ** -0.5), 0.109375, ((0, 32),))
    w_value = scatter_about(streams_of[4], (D, D), D ** -0.5, 0.21875, ((0, 32),))
    w_out = scatter_about(streams_of[5], (D, D), (D // 16) ** -0.5, 0.875, ((0, 32),))
    w_in = scatter_about(streams_of[6], (D, FF), D ** -0.5, 0.21875, ((0, 32),))
    w_back = scatter_about(streams_of[7], (FF, D), FF ** -0.5, 0.109375, ((0, 32),))
    w_proj = scatter_about(streams_of[8], (D, PROJ), D ** -0.5, 0.21875, ((0, 32),))
    gain_attn = jnp.clip(1.0 + 0.1 * jax.random.normal(streams_of[9], (D,), jnp.float32), 0.5, 1.5).astype(jnp.bfloat16)
    gain_ffn = jnp.clip(1.0 + 0.1 * jax.random.normal(streams_of[10], (D,), jnp.float32), 0.5, 1.5).astype(jnp.bfloat16)
    gain_final = jnp.clip(1.0 + 0.1 * jax.random.normal(streams_of[11], (D,), jnp.float32), 0.5, 1.5).astype(jnp.bfloat16)
    rel_table = scatter_about(streams_of[12], (BUCKETS, HEADS), 1.0, 4.0)
    cotangent = scatter_about(streams_of[13], (SEQS, SEQ_LEN, PROJ), 1.0, 6.0, ((0, 4), (1, 8)))
    return dict(inputs=inputs, segments=segments, w_query=w_query, w_key=w_key, w_value=w_value, w_out=w_out, w_in=w_in, w_back=w_back, w_proj=w_proj, gain_attn=gain_attn, gain_ffn=gain_ffn, gain_final=gain_final, rel_table=rel_table, cotangent=cotangent)


@jax.custom_vjp
def low(v):
    return lax.optimization_barrier(v.astype(jnp.bfloat16)).astype(jnp.float32)

@jax.custom_vjp
def low_back(v):
    return v

def low_keep(v):
    return (low(v), None)

def low_pass(kept, grad):
    return (grad,)

def back_keep(v):
    return (v, None)

def back_low(kept, grad):
    return (low(grad),)
low.defvjp(low_keep, low_pass)
low_back.defvjp(back_keep, back_low)
bucket_borders = (12, 16, 23, 32, 46, 64, 91)
masked_value = -1e+30
highest_precision_flag = lax.Precision.HIGHEST

def bucket_of(offset):
    distance = jnp.abs(offset)
    beyond = 8 + sum(((distance >= border).astype(jnp.int32) for border in bucket_borders))
    within = jnp.minimum(jnp.where(distance < 8, distance, beyond), 15)
    return within + 16 * (offset > 0).astype(jnp.int32)

def norm_gain(value_vectors, weights):
    factor = lax.rsqrt(lax.optimization_barrier(jnp.mean(value_vectors * value_vectors, axis=-1, keepdims=True)) + 1e-06)
    return value_vectors * factor * weights

def attention(query, key, value, segments, table_heads):
    query_size = min(512, SEQ_LEN)
    query_count = SEQ_LEN // query_size
    positions = jnp.arange(SEQ_LEN, dtype=jnp.int32)
    query_blocks = query.reshape(SEQS * query_count, query_size, HEADS, HEAD_DIM)
    segment_blocks = segments.reshape(SEQS * query_count, query_size)
    position_blocks = jnp.tile(positions.reshape(query_count, query_size), (SEQS, 1))
    sequence_ids = jnp.repeat(jnp.arange(SEQS, dtype=jnp.int32), query_count)

    @jax.checkpoint
    def query_block(pieces):
        queries, query_seg, query_pos, sequence = pieces
        keys_seq = lax.dynamic_index_in_dim(key, sequence, 0, keepdims=False)
        values_seq = lax.dynamic_index_in_dim(value, sequence, 0, keepdims=False)
        key_seg = lax.dynamic_index_in_dim(segments, sequence, 0, keepdims=False)
        buckets = bucket_of(positions[None, :] - query_pos[:, None])
        logit_scores = jnp.einsum('ihe,jhe->hij', queries, keys_seq, precision=highest_precision_flag)
        logit_scores = low_back(logit_scores + jnp.take(table_heads, buckets, axis=1))
        allowed = query_seg[:, None] == key_seg[None, :]
        masked = jnp.where(allowed[None], logit_scores, masked_value)
        highest = lax.optimization_barrier(jnp.max(masked, axis=-1, keepdims=True))
        logsum = highest + jnp.log(lax.optimization_barrier(jnp.sum(jnp.exp(masked - highest), axis=-1, keepdims=True)))
        softmax = low(jnp.exp(masked - logsum))
        return jnp.einsum('hij,jhe->ihe', softmax, values_seq, precision=highest_precision_flag)
    attended = lax.map(query_block, (query_blocks, segment_blocks, position_blocks, sequence_ids))
    return attended.reshape(SEQS, SEQ_LEN, HEADS * HEAD_DIM)

def project(value_vectors, weight_matrix):
    return jnp.einsum('ztf,fy->zty', value_vectors, weight_matrix, precision=highest_precision_flag)

def forward(inputs, w_query, w_key, w_value, w_out, w_in, w_back, w_proj, gain_attn, gain_ffn, gain_final, rel_table, segments):
    hidden_one = low(norm_gain(inputs, gain_attn))
    query = low(low_back(project(hidden_one, w_query)))
    key = low(low_back(project(hidden_one, w_key)))
    value = low(low_back(project(hidden_one, w_value)))
    shape_heads = (SEQS, SEQ_LEN, HEADS, HEAD_DIM)
    attended = attention(query.reshape(shape_heads), key.reshape(shape_heads), value.reshape(shape_heads), segments, rel_table.T)
    attended = low(low_back(attended))
    resid_one = inputs + low_back(project(attended, w_out))
    hidden_two = low(norm_gain(resid_one, gain_ffn))
    upward = low_back(project(hidden_two, w_in))
    active = low(jax.nn.gelu(upward, approximate=True))
    resid_two = resid_one + low_back(project(active, w_back))
    final = low(norm_gain(resid_two, gain_final))
    return project(final, w_proj)

def reference(inputs, segments, w_query, w_key, w_value, w_out, w_in, w_back, w_proj, gain_attn, gain_ffn, gain_final, rel_table, cotangent):
    floats = [array.astype(jnp.float32) for array in (inputs, w_query, w_key, w_value, w_out, w_in, w_back, w_proj, gain_attn, gain_ffn, gain_final, rel_table)]

    def closed(*value_vectors):
        return forward(*value_vectors, segments)
    states, pullback = jax.vjp(closed, *floats)
    grads = pullback(cotangent.astype(jnp.float32))
    return (states.astype(jnp.bfloat16), grads[0], grads[1], grads[2], grads[3], grads[4], grads[5], grads[6], grads[7], grads[8], grads[9], grads[10], grads[11])
```

```python
import functools
import math

import jax
import jax.numpy as jnp
import numpy as np
from jax import lax
from jax.experimental import pallas as pl
from jax.experimental.pallas import tpu as pltpu
from jax.sharding import PartitionSpec as P

BORDERS = (12, 16, 23, 32, 46, 64, 91)
MASKED = -1e30
EPS = 1e-6
TILE = 128
WIN = 512
BF16 = jnp.bfloat16
F32 = jnp.float32
AXES = ("head", "blk")
VMEM_LIMIT = 56 * 1024 * 1024


def bucket_np(offset):
    distance = np.abs(offset)
    beyond = 8 + sum((distance >= border).astype(np.int64) for border in BORDERS)
    within = np.minimum(np.where(distance < 8, distance, beyond), 15)
    return within + 16 * (offset > 0)


def window_offsets():
    k = np.arange(WIN)
    return np.where(k < WIN - TILE, k - TILE, k - WIN - TILE)


def dot(a, b):
    return jnp.dot(a, b, preferred_element_type=F32)


def dot_nt(a, b):
    return lax.dot_general(a, b, (((1,), (1,)), ((), ())), preferred_element_type=F32)


def dot_tn(a, b):
    return lax.dot_general(a, b, (((0,), (0,)), ((), ())), preferred_element_type=F32)


class Links:
    def __init__(self):
        self.blocks = lax.axis_size("blk")
        self.total = lax.axis_size("head") * self.blocks
        self.me = lax.axis_index("head") * self.blocks + lax.axis_index("blk")
        self.bits = [1 << k for k in range(int(math.log2(self.total)))]
        self.blk_bits = [bit for bit in self.bits if bit < self.blocks]
        self.head_bits = [bit for bit in self.bits if bit >= self.blocks]

    def swap(self, value, bit):
        return lax.ppermute(value, AXES, [(i, i ^ bit) for i in range(self.total)])

    def mine(self, bit):
        return (self.me & bit) != 0


def gather_rows(links, shard, order, all_bits):
    high_first = sorted(all_bits, reverse=True)
    value = shard.reshape((1,) * len(high_first) + shard.shape)
    for bit in order:
        axis = high_first.index(bit)
        other = links.swap(value, bit)
        value = jnp.where(
            links.mine(bit),
            jnp.concatenate([other, value], axis),
            jnp.concatenate([value, other], axis),
        )
    return value.reshape((-1,) + shard.shape[1:])


def scatter_sum(links, whole, order, all_bits):
    high_first = sorted(all_bits, reverse=True)
    count = len(high_first)
    rows = whole.shape[0] >> count
    value = whole.reshape((2,) * count + (rows,) + whole.shape[1:])
    for bit in order:
        axis = high_first.index(bit)
        side = links.mine(bit).astype(jnp.int32)
        sent = lax.dynamic_slice_in_dim(value, 1 - side, 1, axis).astype(BF16)
        kept = lax.dynamic_slice_in_dim(value, side, 1, axis)
        value = kept.astype(F32) + links.swap(sent, bit).astype(F32)
    return value.reshape((rows,) + whole.shape[1:])


def bias_tiles(bias_ref, tiles_ref, head_row, side):
    row = bias_ref[pl.ds(head_row, 1), :]
    near = pltpu.roll(jnp.broadcast_to(row[:, :WIN], (TILE, WIN)), 0, 1, stride=1, stride_axis=0)
    rows = pl.ds(side * TILE, TILE)
    tiles_ref[0, rows, :] = jnp.broadcast_to(row[:, WIN : WIN + 1], (TILE, TILE))
    for t in range(3):
        tiles_ref[1 + t, rows, :] = near[:, t * TILE : (t + 1) * TILE]
    tiles_ref[4, rows, :] = jnp.broadcast_to(row[:, WIN + 1 : WIN + 2], (TILE, TILE))


def stacked(pair):
    lane = lax.broadcasted_iota(jnp.int32, pair.shape, 1)
    zero = jnp.zeros_like(pair)
    half = pair.shape[1] // 2
    return jnp.concatenate([jnp.where(lane < half, pair, zero), jnp.where(lane < half, zero, pair)], 0)


def unstacked(both):
    rows = both.shape[0] // 2
    lane = lax.broadcasted_iota(jnp.int32, (rows, both.shape[1]), 1)
    return jnp.where(lane < both.shape[1] // 2, both[:rows], both[rows:])


def tile_kind(key_tile, own_tile):
    return jnp.clip(key_tile - own_tile, -2, 2) + 2


def scores_into(chunk, chunk_tiles, own, q2, k_ref, qseg, kseg_ref, tiles_ref, s_ref):
    base = chunk * chunk_tiles * TILE
    raw = dot_nt(q2, k_ref[pl.ds(base, chunk_tiles * TILE), :])
    parts = []
    for t in range(chunk_tiles):
        at = base + t * TILE
        near = tiles_ref[tile_kind(chunk * chunk_tiles + t, own)]
        allowed = qseg == kseg_ref[:, pl.ds(at, TILE)]
        tile = jnp.where(allowed, raw[:, t * TILE : (t + 1) * TILE] + near, MASKED)
        s_ref[:, pl.ds(at, TILE)] = tile
        parts.append(tile)
    return parts


def attend_kernel(own_ref, q_ref, k_ref, v_ref, qseg_ref, kseg_ref, bias_ref, o_ref, low_ref, lse_ref, tiles_ref, s_ref, *, chunks, chunk_tiles):
    pair = pl.program_id(0)
    own = own_ref[0]
    for side in range(2):
        bias_tiles(bias_ref, tiles_ref, pair * 2 + side, side)
    q2 = stacked(q_ref[...])
    qseg = jnp.concatenate([qseg_ref[...], qseg_ref[...]], 0)

    def first(chunk, high):
        parts = scores_into(chunk, chunk_tiles, own, q2, k_ref, qseg, kseg_ref, tiles_ref, s_ref)
        return functools.reduce(jnp.maximum, parts, high)

    def second(chunk, total):
        for t in range(chunk_tiles):
            at = pl.ds((chunk * chunk_tiles + t) * TILE, TILE)
            powers = jnp.exp(s_ref[:, at] - high)
            s_ref[:, at] = powers
            total = total + powers
        return total

    def third(chunk, acc):
        base = chunk * chunk_tiles * TILE
        at = pl.ds(base, chunk_tiles * TILE)
        low = (s_ref[:, at] * inverse).astype(BF16)
        return acc + dot(low, v_ref[at, :])

    def loop(body, start):
        return body(0, start) if chunks == 1 else lax.fori_loop(0, chunks, body, start)

    high = loop(first, jnp.full((2 * TILE, TILE), MASKED, F32))
    high = jnp.max(high, axis=1, keepdims=True)
    total = jnp.sum(loop(second, jnp.zeros((2 * TILE, TILE), F32)), axis=1, keepdims=True)
    inverse = 1.0 / total
    out = unstacked(loop(third, jnp.zeros((2 * TILE, TILE), F32)))
    o_ref[...] = out
    low_ref[...] = out.astype(BF16)
    lse_ref[...] = jnp.broadcast_to(high + jnp.log(total), (2 * TILE, TILE))


def attend_back_kernel(own_ref, q_ref, k_ref, v_ref, do_ref, o_ref, lse_ref, qseg_ref, kseg_ref, bias_ref, dq_ref, dk_ref, dv_ref, sums_ref, tiles_ref, s_ref, near_ref, *, chunks, chunk_tiles):
    pair = pl.program_id(0)
    own = own_ref[0]
    for side in range(2):
        bias_tiles(bias_ref, tiles_ref, pair * 2 + side, side)
    q2 = stacked(q_ref[...])
    do2 = stacked(do_ref[...])
    delta = jnp.sum(stacked(do_ref[...].astype(F32) * o_ref[...]), axis=1, keepdims=True)
    lse = lse_ref[:, :1]
    qseg = jnp.concatenate([qseg_ref[...], qseg_ref[...]], 0)
    near_ref[...] = jnp.zeros_like(near_ref)

    def step(chunk, carried):
        acc, left, right = carried
        base = chunk * chunk_tiles * TILE
        at = pl.ds(base, chunk_tiles * TILE)
        scores_into(chunk, chunk_tiles, own, q2, k_ref, qseg, kseg_ref, tiles_ref, s_ref)
        probs = jnp.exp(s_ref[:, at] - lse)
        grad_probs = dot_nt(do2, v_ref[at, :])
        grads = (probs * (grad_probs - delta)).astype(BF16)
        acc = acc + dot(grads, k_ref[at, :])
        dk_ref[at, :] = dot_tn(grads, q2).astype(BF16)
        dv_ref[at, :] = dot_tn(probs.astype(BF16), do2).astype(BF16)
        wide = grads.astype(F32)
        for t in range(chunk_tiles):
            gap = chunk * chunk_tiles + t - own
            tile = wide[:, t * TILE : (t + 1) * TILE]
            left = left + jnp.where(gap < -1, tile, 0.0)
            right = right + jnp.where(gap > 1, tile, 0.0)

            @pl.when(jnp.abs(gap) <= 1)
            def _():
                near_ref[jnp.clip(gap + 1, 0, 2)] = tile

        return acc, left, right

    zero = jnp.zeros((2 * TILE, TILE), F32)
    start = (zero, zero, zero)
    acc, left, right = step(0, start) if chunks == 1 else lax.fori_loop(0, chunks, step, start)
    dq_ref[...] = unstacked(acc).astype(BF16)
    flip = (
        lax.broadcasted_iota(jnp.int32, (TILE, TILE), 0) + lax.broadcasted_iota(jnp.int32, (TILE, TILE), 1) == TILE - 1
    ).astype(BF16)
    for side in range(2):
        rows = slice(side * TILE, (side + 1) * TILE)
        window = jnp.concatenate([near_ref[t, rows, :] for t in range(4)], 1).astype(BF16)
        turned = pltpu.roll(dot(flip, window), 0, 1, stride=1, stride_axis=0)
        near_sum = jnp.sum(turned, axis=0, keepdims=True)
        far = [jnp.sum(jnp.sum(part[rows], axis=0, keepdims=True), axis=1, keepdims=True) for part in (left, right)]
        sums_ref[0, side : side + 1, :WIN] = near_sum
        lane = lax.broadcasted_iota(jnp.int32, (1, TILE), 1)
        sums_ref[0, side : side + 1, WIN:] = jnp.where(lane == 0, far[0], jnp.where(lane == 1, far[1], 0.0))


def attention_calls(length, width, heads):
    pairs = heads // 2
    tiles = length // TILE
    chunk_tiles = min(8, tiles)
    chunks = tiles // chunk_tiles
    wide = WIN + TILE
    lanes = width // pairs
    own_spec = pl.BlockSpec(memory_space=pltpu.SMEM)
    q_spec = pl.BlockSpec((TILE, lanes), lambda p: (0, p))
    k_spec = pl.BlockSpec((length, lanes), lambda p: (0, p))
    qseg_spec = pl.BlockSpec((TILE, 1), lambda p: (0, 0))
    kseg_spec = pl.BlockSpec((1, length), lambda p: (0, 0))
    bias_spec = pl.BlockSpec((heads, wide), lambda p: (0, 0))
    lse_spec = pl.BlockSpec((2 * TILE, TILE), lambda p: (p, 0))
    sums_spec = pl.BlockSpec((1, 2, wide), lambda p: (p, 0, 0))
    scratch = [pltpu.VMEM((5, 2 * TILE, TILE), F32), pltpu.VMEM((2 * TILE, length), F32)]
    params = pltpu.CompilerParams(vmem_limit_bytes=VMEM_LIMIT)

    def shape(dims, kind):
        return jax.ShapeDtypeStruct(dims, kind)

    forward = pl.pallas_call(
        functools.partial(attend_kernel, chunks=chunks, chunk_tiles=chunk_tiles),
        grid=(pairs,),
        in_specs=[own_spec, q_spec, k_spec, k_spec, qseg_spec, kseg_spec, bias_spec],
        out_specs=[q_spec, q_spec, lse_spec],
        out_shape=[shape((TILE, width), F32), shape((TILE, width), BF16), shape((pairs * 2 * TILE, TILE), F32)],
        scratch_shapes=scratch,
        compiler_params=params,
        name="attend",
    )
    backward = pl.pallas_call(
        functools.partial(attend_back_kernel, chunks=chunks, chunk_tiles=chunk_tiles),
        grid=(pairs,),
        in_specs=[own_spec, q_spec, k_spec, k_spec, q_spec, q_spec, lse_spec, qseg_spec, kseg_spec, bias_spec],
        out_specs=[q_spec, k_spec, k_spec, sums_spec],
        out_shape=[
            shape((TILE, width), BF16),
            shape((length, width), BF16),
            shape((length, width), BF16),
            shape((pairs, 2, wide), F32),
        ],
        scratch_shapes=scratch + [pltpu.VMEM((4, 2 * TILE, TILE), F32)],
        compiler_params=params,
        name="attend_back",
    )
    return forward, backward


def normed(rows):
    scale = lax.rsqrt(jnp.mean(rows * rows, axis=-1, keepdims=True) + EPS)
    return rows * scale, scale


def norm_back(grad, gain, unit, scale):
    scaled = grad * gain
    return (scaled - unit * jnp.mean(scaled * unit, axis=-1, keepdims=True)) * scale


def body(inputs, segments, w_query, w_key, w_value, w_out, w_in, w_back, w_proj, gain_attn, gain_ffn, gain_final, rel_table, cotangent):
    links = Links()
    bits = links.bits
    tokens, width = inputs.shape[1:]
    ff = w_in.shape[1]
    proj = w_proj.shape[1]
    buckets, heads = rel_table.shape
    length = tokens * links.blocks
    rows = w_query.shape[0]
    own = lax.axis_index("blk").reshape(1).astype(jnp.int32)

    gains = jnp.stack([gain_attn, gain_ffn, gain_final], 1)
    gains = jnp.pad(gains, ((0, 0), (0, TILE - gains.shape[1])))
    pack_qkv = jnp.concatenate([w_query, w_key, w_value, gains], 1)
    pack_mid = jnp.concatenate([w_out, w_in, w_proj], 1)
    blk_down = [b for b in links.blk_bits if b > 1] + [1]
    order_a = blk_down + links.head_bits[::-1]
    own_rows = inputs[0]
    all_rows = gather_rows(links, own_rows, blk_down, links.blk_bits)
    seg_all = gather_rows(links, segments, blk_down, links.blk_bits)
    full_qkv = gather_rows(links, pack_qkv, order_a, bits)
    full_mid = gather_rows(links, pack_mid, order_a, bits)
    full_back = gather_rows(links, w_back, order_a, bits)
    full_query, full_key, full_value = (full_qkv[:, i * width : (i + 1) * width] for i in range(3))
    gain_rows = full_qkv[:, 3 * width :].astype(F32).T
    gain_one, gain_two, gain_three = gain_rows[0], gain_rows[1], gain_rows[2]
    full_out = full_mid[:, :width]
    full_in = full_mid[:, width : width + ff]
    full_proj = full_mid[:, width + ff :]

    offsets = bucket_np(window_offsets())
    onehot = np.zeros((WIN + TILE, buckets), np.float32)
    onehot[np.arange(WIN), offsets] = 1.0
    onehot[WIN, 15] = 1.0
    onehot[WIN + 1, 31] = 1.0
    bias = lax.dot_general(
        rel_table, jnp.asarray(onehot, BF16), (((0,), (1,)), ((), ())), preferred_element_type=F32
    )

    states_in = own_rows.astype(F32)
    unit_all, scale_all = normed(all_rows.astype(F32))
    hidden_all = (unit_all * gain_one).astype(BF16)
    unit_one, scale_one = normed(states_in)
    hidden_one = (unit_one * gain_one).astype(BF16)
    query = dot(hidden_one, full_query).astype(BF16)
    key = dot(hidden_all, full_key).astype(BF16)
    value = dot(hidden_all, full_value).astype(BF16)
    attend, attend_back = attention_calls(length, width, heads)
    qseg = segments.reshape(tokens, 1)
    kseg = seg_all.reshape(1, length)
    attended, attended_low, lse = attend(own, query, key, value, qseg, kseg, bias)
    resid_one = states_in + dot(attended_low, full_out)
    unit_two, scale_two = normed(resid_one)
    hidden_two = (unit_two * gain_two).astype(BF16)
    upward = dot(hidden_two, full_in)
    active, back_gelu = jax.vjp(lambda u: jax.nn.gelu(u, approximate=True), upward)
    active_low = active.astype(BF16)
    resid_two = resid_one + dot(active_low, full_back)
    unit_three, scale_three = normed(resid_two)
    final_low = (unit_three * gain_three).astype(BF16)
    states = dot(final_low, full_proj).astype(BF16)

    arriving = cotangent[0]
    grad_proj = dot_tn(final_low, arriving)
    grad_final = dot_nt(arriving, full_proj)
    grad_gain_three = jnp.sum(grad_final * unit_three, axis=0)
    grad_two = norm_back(grad_final, gain_three, unit_three, scale_three)
    grad_branch = grad_two.astype(BF16)
    grad_back = dot_tn(active_low, grad_branch)
    grad_up = back_gelu(dot_nt(grad_branch, full_back))[0].astype(BF16)
    grad_in = dot_tn(hidden_two, grad_up)
    grad_hidden_two = dot_nt(grad_up, full_in)
    grad_gain_two = jnp.sum(grad_hidden_two * unit_two, axis=0)
    grad_one = grad_two + norm_back(grad_hidden_two, gain_two, unit_two, scale_two)
    grad_attn = grad_one.astype(BF16)
    grad_out = dot_tn(attended_low, grad_attn)
    grad_attended = dot_nt(grad_attn, full_out).astype(BF16)
    grad_q, grad_k, grad_v, sums = attend_back(
        own, query, key, value, grad_attended, attended, lse, qseg, kseg, bias
    )
    grad_query = dot_tn(hidden_one, grad_q)
    grad_key = dot_tn(hidden_all, grad_k)
    grad_value = dot_tn(hidden_all, grad_v)
    grad_rows = dot_nt(grad_k, full_key) + dot_nt(grad_v, full_value)
    own_part = dot_nt(grad_q, full_query)
    first = lax.axis_index("blk") * tokens
    grad_rows = lax.dynamic_update_slice_in_dim(
        grad_rows, lax.dynamic_slice_in_dim(grad_rows, first, tokens, 0) + own_part, first, 0
    )
    grad_gain_one = jnp.sum(grad_rows * unit_all, axis=0)

    up_order = links.head_bits + [1] + [b for b in links.blk_bits if b > 1][::-1]
    blk_up = [1] + [b for b in links.blk_bits if b > 1][::-1]
    reduced_back = scatter_sum(links, grad_back, up_order, bits)
    reduced_mid = scatter_sum(links, jnp.concatenate([grad_out, grad_in, grad_proj], 1), up_order, bits)
    gain_grads = jnp.stack([grad_gain_one, grad_gain_two, grad_gain_three], 1)
    gain_grads = jnp.pad(gain_grads, ((0, 0), (0, TILE - 3)))
    reduced_qkv = scatter_sum(
        links, jnp.concatenate([grad_query, grad_key, grad_value, gain_grads], 1), up_order, bits
    )
    grad_hidden_one = scatter_sum(links, grad_rows, blk_up, links.blk_bits)
    input_gradient_rows = grad_one + norm_back(grad_hidden_one, gain_one, unit_one, scale_one)

    per_head = sums.reshape(heads, WIN + TILE)
    lane = np.arange(WIN)
    diagonal = np.zeros((WIN + TILE, buckets), np.float32)
    reach = lane - (TILE - 1) - TILE
    diagonal[lane, bucket_np(reach)] = 1.0
    diagonal[WIN, 15] = 1.0
    diagonal[WIN + 1, 31] = 1.0
    table = lax.dot_general(
        jnp.asarray(diagonal), per_head, (((0,), (1,)), ((), ())), precision=lax.Precision.HIGHEST
    )
    table = jnp.pad(table, ((0, 0), (0, TILE - heads)))
    for bit in bits:
        table = table + links.swap(table, bit)
    return (
        states[None],
        input_gradient_rows[None],
        reduced_qkv[:, :width],
        reduced_qkv[:, width : 2 * width],
        reduced_qkv[:, 2 * width : 3 * width],
        reduced_mid[:, :width],
        reduced_mid[:, width : width + ff],
        reduced_back,
        reduced_mid[:, width + ff :],
        reduced_qkv[:, 3 * width],
        reduced_qkv[:, 3 * width + 1],
        reduced_qkv[:, 3 * width + 2],
        table[:, :heads],
    )


def solution(mesh):
    rows = P(("head", "blk"), None)
    line = P(("head", "blk"))
    tokens = P("head", "blk", None)
    in_specs = (tokens, P("head", "blk")) + (rows,) * 7 + (line,) * 3 + (P(), tokens)
    out_specs = (tokens, tokens) + (rows,) * 7 + (line,) * 3 + (P(),)
    return jax.shard_map(body, mesh=mesh, in_specs=in_specs, out_specs=out_specs, check_vma=False)
```

```python
import functools
import math

import jax
import jax.numpy as jnp
import numpy as np
from jax import lax
from jax.experimental import pallas as pl
from jax.experimental.pallas import tpu as pltpu
from jax.sharding import PartitionSpec as P

BORDERS = (12, 16, 23, 32, 46, 64, 91)
MASKED = -1e30
EPS = 1e-6
TILE = 128
WIN = 512
BF16 = jnp.bfloat16
F32 = jnp.float32
AXES = ("head", "blk")
VMEM_LIMIT = 56 * 1024 * 1024


def bucket_np(offset):
    distance = np.abs(offset)
    beyond = 8 + sum((distance >= border).astype(np.int64) for border in BORDERS)
    within = np.minimum(np.where(distance < 8, distance, beyond), 15)
    return within + 16 * (offset > 0)


def window_offsets():
    k = np.arange(WIN)
    return np.where(k < WIN - TILE, k - TILE, k - WIN - TILE)


def dot(a, b):
    return jnp.dot(a, b, preferred_element_type=F32)


def dot_nt(a, b):
    return lax.dot_general(a, b, (((1,), (1,)), ((), ())), preferred_element_type=F32)


def dot_tn(a, b):
    return lax.dot_general(a, b, (((0,), (0,)), ((), ())), preferred_element_type=F32)


class Links:
    def __init__(self):
        self.blocks = lax.axis_size("blk")
        self.total = lax.axis_size("head") * self.blocks
        self.me = lax.axis_index("head") * self.blocks + lax.axis_index("blk")
        self.bits = [1 << k for k in range(int(math.log2(self.total)))]
        self.blk_bits = [bit for bit in self.bits if bit < self.blocks]
        self.head_bits = [bit for bit in self.bits if bit >= self.blocks]

    def swap(self, value, bit):
        return lax.ppermute(value, AXES, [(i, i ^ bit) for i in range(self.total)])

    def mine(self, bit):
        return (self.me & bit) != 0


def gather_rows(links, shard, order, all_bits):
    high_first = sorted(all_bits, reverse=True)
    value = shard.reshape((1,) * len(high_first) + shard.shape)
    for bit in order:
        axis = high_first.index(bit)
        other = links.swap(value, bit)
        value = jnp.where(
            links.mine(bit),
            jnp.concatenate([other, value], axis),
            jnp.concatenate([value, other], axis),
        )
    return value.reshape((-1,) + shard.shape[1:])


def scatter_sum(links, whole, order, all_bits):
    high_first = sorted(all_bits, reverse=True)
    count = len(high_first)
    rows = whole.shape[0] >> count
    value = whole.reshape((2,) * count + (rows,) + whole.shape[1:])
    for bit in order:
        axis = high_first.index(bit)
        side = links.mine(bit).astype(jnp.int32)
        sent = lax.dynamic_slice_in_dim(value, 1 - side, 1, axis).astype(BF16)
        kept = lax.dynamic_slice_in_dim(value, side, 1, axis)
        value = kept.astype(F32) + links.swap(sent, bit).astype(F32)
    return value.reshape((rows,) + whole.shape[1:])


def bias_tiles(bias_ref, tiles_ref, head_row, side):
    row = bias_ref[pl.ds(head_row, 1), :]
    near = pltpu.roll(jnp.broadcast_to(row[:, :WIN], (TILE, WIN)), 0, 1, stride=1, stride_axis=0)
    rows = pl.ds(side * TILE, TILE)
    tiles_ref[0, rows, :] = jnp.broadcast_to(row[:, WIN : WIN + 1], (TILE, TILE))
    for t in range(3):
        tiles_ref[1 + t, rows, :] = near[:, t * TILE : (t + 1) * TILE]
    tiles_ref[4, rows, :] = jnp.broadcast_to(row[:, WIN + 1 : WIN + 2], (TILE, TILE))


def stacked(pair):
    lane = lax.broadcasted_iota(jnp.int32, pair.shape, 1)
    zero = jnp.zeros_like(pair)
    half = pair.shape[1] // 2
    return jnp.concatenate([jnp.where(lane < half, pair, zero), jnp.where(lane < half, zero, pair)], 0)


def unstacked(both):
    rows = both.shape[0] // 2
    lane = lax.broadcasted_iota(jnp.int32, (rows, both.shape[1]), 1)
    return jnp.where(lane < both.shape[1] // 2, both[:rows], both[rows:])


def tile_kind(key_tile, own_tile):
    return jnp.clip(key_tile - own_tile, -2, 2) + 2


def scores_into(chunk, chunk_tiles, own, q2, k_ref, qseg, kseg_ref, tiles_ref, s_ref):
    base = chunk * chunk_tiles * TILE
    raw = dot_nt(q2, k_ref[pl.ds(base, chunk_tiles * TILE), :])
    parts = []
    for t in range(chunk_tiles):
        at = base + t * TILE
        near = tiles_ref[tile_kind(chunk * chunk_tiles + t, own)]
        allowed = qseg == kseg_ref[pl.ds(chunk * chunk_tiles + t, 1), :]
        tile = jnp.where(allowed, raw[:, t * TILE : (t + 1) * TILE] + near, MASKED)
        s_ref[:, pl.ds(at, TILE)] = tile
        parts.append(tile)
    return parts


def attend_kernel(own_ref, q_ref, k_ref, v_ref, qseg_ref, kseg_ref, bias_ref, *refs, marks, chunks, chunk_tiles):
    o_ref, low_ref, lse_ref, tiles_ref, s_ref = refs[marks:]
    pair = pl.program_id(0)
    own = own_ref[0]
    for side in range(2):
        bias_tiles(bias_ref, tiles_ref, pair * 2 + side, side)
    q2 = stacked(q_ref[...])
    qseg = jnp.concatenate([qseg_ref[...], qseg_ref[...]], 0)

    def first(chunk, high):
        parts = scores_into(chunk, chunk_tiles, own, q2, k_ref, qseg, kseg_ref, tiles_ref, s_ref)
        return functools.reduce(jnp.maximum, parts, high)

    def second(chunk, total):
        for t in range(chunk_tiles):
            at = pl.ds((chunk * chunk_tiles + t) * TILE, TILE)
            powers = jnp.exp(s_ref[:, at] - high)
            s_ref[:, at] = powers
            total = total + powers
        return total

    def third(chunk, acc):
        base = chunk * chunk_tiles * TILE
        at = pl.ds(base, chunk_tiles * TILE)
        low = (s_ref[:, at] * inverse).astype(BF16)
        return acc + dot(low, v_ref[at, :])

    def loop(body, start):
        return body(0, start) if chunks == 1 else lax.fori_loop(0, chunks, body, start)

    high = loop(first, jnp.full((2 * TILE, TILE), MASKED, F32))
    high = jnp.max(high, axis=1, keepdims=True)
    total = jnp.sum(loop(second, jnp.zeros((2 * TILE, TILE), F32)), axis=1, keepdims=True)
    inverse = 1.0 / total
    out = unstacked(loop(third, jnp.zeros((2 * TILE, TILE), F32)))
    o_ref[...] = out
    low_ref[...] = out.astype(BF16)
    lse_ref[...] = jnp.broadcast_to(high + jnp.log(total), (2 * TILE, TILE))


def attend_back_kernel(own_ref, q_ref, k_ref, v_ref, do_ref, o_ref, lse_ref, qseg_ref, kseg_ref, bias_ref, *refs, first, marks, chunks, chunk_tiles):
    dq_ref, dk_ref, dv_ref, sums_ref, tiles_ref, s_ref, near_ref = refs[marks:]
    pair = pl.program_id(0) + first
    own = own_ref[0]
    for side in range(2):
        bias_tiles(bias_ref, tiles_ref, pair * 2 + side, side)
    q2 = stacked(q_ref[...])
    do2 = stacked(do_ref[...])
    delta = jnp.sum(stacked(do_ref[...].astype(F32) * o_ref[...]), axis=1, keepdims=True)
    lse = lse_ref[:, :1]
    qseg = jnp.concatenate([qseg_ref[...], qseg_ref[...]], 0)
    near_ref[...] = jnp.zeros_like(near_ref)

    def step(chunk, carried):
        acc, left, right = carried
        base = chunk * chunk_tiles * TILE
        at = pl.ds(base, chunk_tiles * TILE)
        scores_into(chunk, chunk_tiles, own, q2, k_ref, qseg, kseg_ref, tiles_ref, s_ref)
        probs = jnp.exp(s_ref[:, at] - lse)
        grad_probs = dot_nt(do2, v_ref[at, :])
        grads = (probs * (grad_probs - delta)).astype(BF16)
        acc = acc + dot(grads, k_ref[at, :])
        dk_ref[at, :] = dot_tn(grads, q2).astype(BF16)
        dv_ref[at, :] = dot_tn(probs.astype(BF16), do2).astype(BF16)
        wide = grads.astype(F32)
        for t in range(chunk_tiles):
            gap = chunk * chunk_tiles + t - own
            tile = wide[:, t * TILE : (t + 1) * TILE]
            left = left + jnp.where(gap < -1, tile, 0.0)
            right = right + jnp.where(gap > 1, tile, 0.0)

            @pl.when(jnp.abs(gap) <= 1)
            def _():
                near_ref[jnp.clip(gap + 1, 0, 2)] = tile

        return acc, left, right

    zero = jnp.zeros((2 * TILE, TILE), F32)
    start = (zero, zero, zero)
    acc, left, right = step(0, start) if chunks == 1 else lax.fori_loop(0, chunks, step, start)
    dq_ref[...] = unstacked(acc).astype(BF16)
    flip = (
        lax.broadcasted_iota(jnp.int32, (TILE, TILE), 0) + lax.broadcasted_iota(jnp.int32, (TILE, TILE), 1) == TILE - 1
    ).astype(BF16)
    for side in range(2):
        rows = slice(side * TILE, (side + 1) * TILE)
        window = jnp.concatenate([near_ref[t, rows, :] for t in range(4)], 1).astype(BF16)
        turned = pltpu.roll(dot(flip, window), 0, 1, stride=1, stride_axis=0)
        near_sum = jnp.sum(turned, axis=0, keepdims=True)
        far = [jnp.sum(jnp.sum(part[rows], axis=0, keepdims=True), axis=1, keepdims=True) for part in (left, right)]
        sums_ref[0, side : side + 1, :WIN] = near_sum
        lane = lax.broadcasted_iota(jnp.int32, (1, TILE), 1)
        sums_ref[0, side : side + 1, WIN:] = jnp.where(lane == 0, far[0], jnp.where(lane == 1, far[1], 0.0))


def attention_calls(length, width, heads, first=0, pairs=None, marks=0):
    total = heads // 2
    pairs = pairs or total
    tiles = length // TILE
    chunk_tiles = min(8, tiles)
    chunks = tiles // chunk_tiles
    wide = WIN + TILE
    lanes = width // total
    any_spec = pl.BlockSpec(memory_space=pl.ANY)
    own_spec = pl.BlockSpec(memory_space=pltpu.SMEM)
    q_spec = pl.BlockSpec((TILE, lanes), lambda p: (0, p + first))
    k_spec = pl.BlockSpec((length, lanes), lambda p: (0, p + first))
    dq_spec = pl.BlockSpec((TILE, lanes), lambda p: (0, p))
    dk_spec = pl.BlockSpec((length, lanes), lambda p: (0, p))
    qseg_spec = pl.BlockSpec((TILE, 1), lambda p: (0, 0))
    kseg_spec = pl.BlockSpec((tiles, TILE), lambda p: (0, 0))
    bias_spec = pl.BlockSpec((heads, wide), lambda p: (0, 0))
    lse_spec = pl.BlockSpec((2 * TILE, TILE), lambda p: (p + first, 0))
    sums_spec = pl.BlockSpec((1, 2, wide), lambda p: (p, 0, 0))
    scratch = [pltpu.VMEM((5, 2 * TILE, TILE), F32), pltpu.VMEM((2 * TILE, length), F32)]
    params = pltpu.CompilerParams(vmem_limit_bytes=VMEM_LIMIT)

    def shape(dims, kind):
        return jax.ShapeDtypeStruct(dims, kind)

    forward = pl.pallas_call(
        functools.partial(attend_kernel, marks=marks, chunks=chunks, chunk_tiles=chunk_tiles),
        grid=(pairs,),
        in_specs=[own_spec, q_spec, k_spec, k_spec, qseg_spec, kseg_spec, bias_spec] + [any_spec] * marks,
        out_specs=[q_spec, q_spec, lse_spec],
        out_shape=[shape((TILE, width), F32), shape((TILE, width), BF16), shape((pairs * 2 * TILE, TILE), F32)],
        scratch_shapes=scratch,
        compiler_params=params,
        cost_estimate=pl.CostEstimate(flops=0, transcendentals=0, bytes_accessed=30 << 20),
        name="attend",
    )
    backward = pl.pallas_call(
        functools.partial(attend_back_kernel, first=first, marks=marks, chunks=chunks, chunk_tiles=chunk_tiles),
        grid=(pairs,),
        in_specs=[own_spec, q_spec, k_spec, k_spec, q_spec, q_spec, lse_spec, qseg_spec, kseg_spec, bias_spec]
        + [any_spec] * marks,
        out_specs=[dq_spec, dk_spec, dk_spec, sums_spec],
        out_shape=[
            shape((TILE, pairs * lanes), BF16),
            shape((length, pairs * lanes), BF16),
            shape((length, pairs * lanes), BF16),
            shape((pairs, 2, wide), F32),
        ],
        scratch_shapes=scratch + [pltpu.VMEM((4, 2 * TILE, TILE), F32)],
        compiler_params=params,
        cost_estimate=pl.CostEstimate(flops=0, transcendentals=0, bytes_accessed=48 << 20),
        name="attend_back",
    )
    return forward, backward


def normed(rows):
    scale = lax.rsqrt(jnp.mean(rows * rows, axis=-1, keepdims=True) + EPS)
    return rows * scale, scale


def norm_back(grad, gain, unit, scale):
    scaled = grad * gain
    return (scaled - unit * jnp.mean(scaled * unit, axis=-1, keepdims=True)) * scale


def bias_rows(rel_table):
    onehot = np.zeros((WIN + TILE, rel_table.shape[0]), np.float32)
    onehot[np.arange(WIN), bucket_np(window_offsets())] = 1.0
    onehot[WIN, 15] = 1.0
    onehot[WIN + 1, 31] = 1.0
    return lax.dot_general(
        rel_table, jnp.asarray(onehot, BF16), (((0,), (1,)), ((), ())), preferred_element_type=F32
    )


def table_grad(sums, heads, buckets):
    lane = np.arange(WIN)
    diagonal = np.zeros((WIN + TILE, buckets), np.float32)
    diagonal[lane, bucket_np(lane - (2 * TILE - 1))] = 1.0
    diagonal[WIN, 15] = 1.0
    diagonal[WIN + 1, 31] = 1.0
    table = lax.dot_general(
        jnp.asarray(diagonal),
        sums.reshape(heads, WIN + TILE),
        (((0,), (1,)), ((), ())),
        precision=lax.Precision.HIGHEST,
    )
    return jnp.pad(table, ((0, 0), (0, TILE - heads)))


def outputs_of(states, input_gradient_rows, reduced_qkv, reduced_mid, reduced_back, table, width, ff, heads):
    return (
        states[None],
        input_gradient_rows[None],
        reduced_qkv[:, :width],
        reduced_qkv[:, width : 2 * width],
        reduced_qkv[:, 2 * width : 3 * width],
        reduced_mid[:, :width],
        reduced_mid[:, width : width + ff],
        reduced_back,
        reduced_mid[:, width + ff :],
        reduced_qkv[:, 3 * width],
        reduced_qkv[:, 3 * width + 1],
        reduced_qkv[:, 3 * width + 2],
        table[:, :heads],
    )


def general_body(inputs, segments, w_query, w_key, w_value, w_out, w_in, w_back, w_proj, gain_attn, gain_ffn, gain_final, rel_table, cotangent):
    links = Links()
    bits = links.bits
    tokens, width = inputs.shape[1:]
    ff = w_in.shape[1]
    proj = w_proj.shape[1]
    buckets, heads = rel_table.shape
    length = tokens * links.blocks
    rows = w_query.shape[0]
    own = lax.axis_index("blk").reshape(1).astype(jnp.int32)

    gains = jnp.stack([gain_attn, gain_ffn, gain_final], 1)
    gains = jnp.pad(gains, ((0, 0), (0, TILE - gains.shape[1])))
    pack_qkv = jnp.concatenate([w_query, w_key, w_value, gains], 1)
    pack_mid = jnp.concatenate([w_out, w_in, w_proj], 1)
    blk_down = [b for b in links.blk_bits if b > 1] + [1]
    order_a = blk_down + links.head_bits[::-1]
    own_rows = inputs[0]
    all_rows = gather_rows(links, own_rows, blk_down, links.blk_bits)
    seg_all = gather_rows(links, segments, blk_down, links.blk_bits)
    full_qkv = gather_rows(links, pack_qkv, order_a, bits)
    full_mid = gather_rows(links, pack_mid, order_a, bits)
    full_back = gather_rows(links, w_back, order_a, bits)
    full_query, full_key, full_value = (full_qkv[:, i * width : (i + 1) * width] for i in range(3))
    gain_rows = full_qkv[:, 3 * width :].astype(F32).T
    gain_one, gain_two, gain_three = gain_rows[0], gain_rows[1], gain_rows[2]
    full_out = full_mid[:, :width]
    full_in = full_mid[:, width : width + ff]
    full_proj = full_mid[:, width + ff :]

    bias = bias_rows(rel_table)

    states_in = own_rows.astype(F32)
    unit_all, scale_all = normed(all_rows.astype(F32))
    hidden_all = (unit_all * gain_one).astype(BF16)
    unit_one, scale_one = normed(states_in)
    hidden_one = (unit_one * gain_one).astype(BF16)
    query = dot(hidden_one, full_query).astype(BF16)
    key = dot(hidden_all, full_key).astype(BF16)
    value = dot(hidden_all, full_value).astype(BF16)
    attend, attend_back = attention_calls(length, width, heads)
    qseg = segments.reshape(tokens, 1)
    kseg = seg_all
    attended, attended_low, lse = attend(own, query, key, value, qseg, kseg, bias)
    resid_one = states_in + dot(attended_low, full_out)
    unit_two, scale_two = normed(resid_one)
    hidden_two = (unit_two * gain_two).astype(BF16)
    upward = dot(hidden_two, full_in)
    active, back_gelu = jax.vjp(lambda u: jax.nn.gelu(u, approximate=True), upward)
    active_low = active.astype(BF16)
    resid_two = resid_one + dot(active_low, full_back)
    unit_three, scale_three = normed(resid_two)
    final_low = (unit_three * gain_three).astype(BF16)
    states = dot(final_low, full_proj).astype(BF16)

    arriving = cotangent[0]
    grad_proj = dot_tn(final_low, arriving)
    grad_final = dot_nt(arriving, full_proj)
    grad_gain_three = jnp.sum(grad_final * unit_three, axis=0)
    grad_two = norm_back(grad_final, gain_three, unit_three, scale_three)
    grad_branch = grad_two.astype(BF16)
    grad_back = dot_tn(active_low, grad_branch)
    grad_up = back_gelu(dot_nt(grad_branch, full_back))[0].astype(BF16)
    grad_in = dot_tn(hidden_two, grad_up)
    grad_hidden_two = dot_nt(grad_up, full_in)
    grad_gain_two = jnp.sum(grad_hidden_two * unit_two, axis=0)
    grad_one = grad_two + norm_back(grad_hidden_two, gain_two, unit_two, scale_two)
    grad_attn = grad_one.astype(BF16)
    grad_out = dot_tn(attended_low, grad_attn)
    grad_attended = dot_nt(grad_attn, full_out).astype(BF16)
    grad_q, grad_k, grad_v, sums = attend_back(
        own, query, key, value, grad_attended, attended, lse, qseg, kseg, bias
    )
    grad_query = dot_tn(hidden_one, grad_q)
    grad_key = dot_tn(hidden_all, grad_k)
    grad_value = dot_tn(hidden_all, grad_v)
    grad_rows = dot_nt(grad_k, full_key) + dot_nt(grad_v, full_value)
    own_part = dot_nt(grad_q, full_query)
    first = lax.axis_index("blk") * tokens
    grad_rows = lax.dynamic_update_slice_in_dim(
        grad_rows, lax.dynamic_slice_in_dim(grad_rows, first, tokens, 0) + own_part, first, 0
    )
    grad_gain_one = jnp.sum(grad_rows * unit_all, axis=0)

    up_order = links.head_bits + [1] + [b for b in links.blk_bits if b > 1][::-1]
    blk_up = [1] + [b for b in links.blk_bits if b > 1][::-1]
    reduced_back = scatter_sum(links, grad_back, up_order, bits)
    reduced_mid = scatter_sum(links, jnp.concatenate([grad_out, grad_in, grad_proj], 1), up_order, bits)
    gain_grads = jnp.stack([grad_gain_one, grad_gain_two, grad_gain_three], 1)
    gain_grads = jnp.pad(gain_grads, ((0, 0), (0, TILE - 3)))
    reduced_qkv = scatter_sum(
        links, jnp.concatenate([grad_query, grad_key, grad_value, gain_grads], 1), up_order, bits
    )
    grad_hidden_one = scatter_sum(links, grad_rows, blk_up, links.blk_bits)
    input_gradient_rows = grad_one + norm_back(grad_hidden_one, gain_one, unit_one, scale_one)

    table = table_grad(sums, heads, rel_table.shape[0])
    for bit in bits:
        table = table + links.swap(table, bit)
    return outputs_of(states, input_gradient_rows, reduced_qkv, reduced_mid, reduced_back, table, width, ff, heads)


X_BIT, CORE_BIT, Y_BIT = 16, 8, 1
NEAR_BIT, OVER_BIT = 2, 4
DEPTH = 4
PEERS = 32


def swap(value, mask, other_mask=None):
    masks = (mask, mask if other_mask is None else other_mask)
    return lax.ppermute(value, AXES, [(i, i ^ masks[(i // CORE_BIT) % 2]) for i in range(PEERS)])


def depth_mask(place, core):
    return (0, NEAR_BIT + core * (OVER_BIT - NEAR_BIT), OVER_BIT - core * (OVER_BIT - NEAR_BIT), NEAR_BIT | OVER_BIT)[place]


def side_masks(core):
    return Y_BIT + core * (X_BIT - Y_BIT), X_BIT - core * (X_BIT - Y_BIT)


def tied(value, *earlier):
    whole = functools.reduce(jnp.logical_and, [mark[(0,) * mark.ndim] == mark[(0,) * mark.ndim] for mark in earlier])
    return jnp.where(whole, value, jnp.zeros_like(value))


def gather_depth(own, first=None):
    first = swap(own, NEAR_BIT, OVER_BIT) if first is None else first
    pair = jnp.stack([own, first])
    return jnp.concatenate([pair, swap(pair, OVER_BIT, NEAR_BIT)], 0)


def gather_plane(column):
    half = jnp.concatenate([column, swap(column, Y_BIT, X_BIT)], 0)
    return half, swap(half, X_BIT, Y_BIT)


def y_pairs(half, rest):
    second = (lax.axis_index("head") % 2) == 1
    high = (lax.axis_index("blk") % 2) == 1
    pairs = (
        (half[:DEPTH], jnp.where(second, rest[:DEPTH], half[DEPTH:])),
        (jnp.where(second, half[DEPTH:], rest[:DEPTH]), rest[DEPTH:]),
    )
    return [
        jnp.where(high, jnp.concatenate([other, mine], 1), jnp.concatenate([mine, other], 1)) for mine, other in pairs
    ]


def gathered_items(core, paired):
    items = []
    for c in range(2):
        here = core if c == 0 else 1 - core
        first, second = side_masks(here)
        for b in range(2):
            for k in range(DEPTH):
                depth = depth_mask(k, here)
                if paired:
                    items.append((2 * c + b, k, (c * CORE_BIT + b * X_BIT) | depth))
                else:
                    items += [
                        (2 * c + b, a * DEPTH + k, (c * CORE_BIT) | (a * first) | (b * second) | depth) for a in range(2)
                    ]
    return items


def sent_items(core):
    items = []
    for c in range(2):
        here = core if c == 0 else 1 - core
        minor, major = side_masks(here)
        for a in range(2):
            for b in range(2):
                for k in range(DEPTH):
                    place = a * 2 * DEPTH + b * DEPTH + k
                    items.append((c, place, (c * CORE_BIT) | (a * major) | (b * minor) | depth_mask(k, here)))
    return items


def wide(value):
    return value.astype(F32)


def part_of(terms, first, last):
    return sum(wide(term[first:last]) for term in terms)


def next_sent(terms):
    half = terms[-1].shape[0] // 2
    return part_of(terms, half, 2 * half).astype(BF16)


def halved(terms, masks, sent=None):
    half = terms[-1].shape[0] // 2
    return [term[:half] for term in terms] + [swap(next_sent(terms) if sent is None else sent, *masks)]


FIRST_SIDE, SECOND_SIDE = (X_BIT, Y_BIT), (Y_BIT, X_BIT)
FIRST_DEPTH, SECOND_DEPTH = (OVER_BIT, NEAR_BIT), (NEAR_BIT, OVER_BIT)


ANY = pl.BlockSpec(memory_space=pl.ANY)
SMEM = pl.BlockSpec(memory_space=pltpu.SMEM)
WHOLE = pl.BlockSpec(memory_space=pltpu.VMEM)


def load_shards(parts, me, target, sems, rows, paired):
    copies = []
    rows = 2 * rows if paired else rows
    core = lax.rem(me // CORE_BIT, 2)
    for n, (buffer, place, relative) in enumerate(gathered_items(core, paired)):
        index = (me ^ relative) // 2 if paired else me ^ relative
        at = pl.multiple_of(index * rows, 16)
        copies.append(pltpu.make_async_copy(parts[buffer].at[place], target.at[pl.ds(at, rows), :], sems.at[n]))
    for copy in copies:
        copy.start()
    return copies


def store_blocks(source, me, targets, sems):
    copies = []
    for n, (side, place, relative) in enumerate(sent_items(lax.rem(me // CORE_BIT, 2))):
        copies.append(pltpu.make_async_copy(source.at[me ^ relative], targets[side].at[place], sems.at[n]))
    for copy in copies:
        copy.start()
    return copies


def put_blocks(target, lanes, value):
    rows = target.shape[1]
    for p in range(PEERS):
        target[p, :, lanes] = value[p * rows : (p + 1) * rows, :].astype(BF16)


def wait_all(copies):
    for copy in copies:
        copy.wait()


def project_kernel(me_ref, *refs, blocks, rows):
    xs = refs[:2]
    parts = refs[2:6]
    h_ref, k_ref, v_ref, q_ref, gains_ref, seg_ref, w_ref, sems = refs[-8:]
    me = me_ref[0]
    own = lax.rem(me, blocks)
    copies = load_shards(parts, me, w_ref, sems, rows, True)
    width = h_ref.shape[1]
    wait_all(copies)
    gains_ref[...] = wide(w_ref[:, 3 * width :]).T[:8]
    gain = gains_ref[0:1, :]
    core = lax.rem(me // CORE_BIT, 2)
    for r in range(blocks):
        x_ref = xs[r // 4].at[r % 4]
        unit, scale = normed(wide(x_ref[:TILE, :]))
        hidden = (unit * gain).astype(BF16)
        block = own ^ ((r & 1) * Y_BIT | depth_mask(r >> 1, core))
        at = pl.multiple_of(block * TILE, TILE)
        h_ref[pl.ds(at, TILE), :] = hidden
        seg_ref[pl.ds(block, 1), :] = wide(x_ref[TILE : TILE + 1, :TILE])
        if r == 0:
            q_ref[...] = dot(hidden, w_ref[:, :width]).astype(BF16)
    step = 512
    for start in range(0, h_ref.shape[0], step):
        at = slice(start, start + step)
        k_ref[at, :] = dot(h_ref[at, :], w_ref[:, width : 2 * width]).astype(BF16)
        v_ref[at, :] = dot(h_ref[at, :], w_ref[:, 2 * width : 3 * width]).astype(BF16)


GELU_C = math.sqrt(2.0 / math.pi)


def ffn_kernel(me_ref, att_ref, x_ref, cot_ref, gains_ref, *refs, ff):
    mid_parts, back_parts = refs[:4], refs[4:8]
    states_ref, one_ref, do_ref, gain_grads_ref, back_keep, back_send, mid_keep, mid_send = refs[8:16]
    mid_ref, back_ref, dmid_ref, dback_ref, mid_sems, back_sems, mid_out_sems, back_out_sems = refs[16:]
    me = me_ref[0]
    width = att_ref.shape[1]
    mid_rows = width // PEERS
    back_rows = ff // PEERS
    mid_copies = load_shards(mid_parts, me, mid_ref, mid_sems, mid_rows, True)
    back_copies = load_shards(back_parts, me, back_ref, back_sems, back_rows, False)
    gain_two = gains_ref[1:2, :]
    gain_three = gains_ref[2:3, :]
    w_out = slice(0, width)
    w_in = slice(width, width + ff)
    w_proj = slice(width + ff, mid_ref.shape[1])
    wait_all(mid_copies)
    resid_one = wide(x_ref[:TILE, :]) + dot(att_ref[...], mid_ref[:, w_out])
    unit_two, scale_two = normed(resid_one)
    hidden_two = (unit_two * gain_two).astype(BF16)
    up = dot(hidden_two, mid_ref[:, w_in])
    inner = GELU_C * (up + 0.044715 * (up * up * up))
    bent = jnp.tanh(inner)
    active = (0.5 * up * (1.0 + bent)).astype(BF16)
    slope = 0.5 * (1.0 + bent) + 0.5 * up * (1.0 - bent * bent) * (GELU_C * (1.0 + 3.0 * 0.044715 * (up * up)))
    wait_all(back_copies)
    resid_two = resid_one + dot(active, back_ref[...])
    unit_three, scale_three = normed(resid_two)
    final = (unit_three * gain_three).astype(BF16)
    states_ref[...] = dot(final, mid_ref[:, w_proj]).astype(BF16)
    grad_final = dot_nt(cot_ref[...], mid_ref[:, w_proj])
    grad_two = norm_back(grad_final, gain_three, unit_three, scale_three)
    branch = grad_two.astype(BF16)
    put_blocks(dback_ref, slice(None), dot_tn(active, branch))
    back_out = store_blocks(dback_ref, me, (back_keep, back_send), back_out_sems)
    grad_up = (dot_nt(branch, back_ref[...]) * slope).astype(BF16)
    grad_hidden = dot_nt(grad_up, mid_ref[:, w_in])
    grad_one = grad_two + norm_back(grad_hidden, gain_two, unit_two, scale_two)
    one_ref[...] = grad_one
    grad_attn = grad_one.astype(BF16)
    do_ref[...] = dot_nt(grad_attn, mid_ref[:, w_out]).astype(BF16)
    put_blocks(dmid_ref, w_out, dot_tn(att_ref[...], grad_attn))
    put_blocks(dmid_ref, w_in, dot_tn(hidden_two, grad_up))
    put_blocks(dmid_ref, w_proj, dot_tn(final, cot_ref[...]))
    mid_out = store_blocks(dmid_ref, me, (mid_keep, mid_send), mid_out_sems)
    gain_grads_ref[...] = jnp.zeros_like(gain_grads_ref)
    gain_grads_ref[1:2, :] = jnp.sum(grad_hidden * unit_two, axis=0, keepdims=True)
    gain_grads_ref[2:3, :] = jnp.sum(grad_final * unit_three, axis=0, keepdims=True)
    wait_all(back_out)
    wait_all(mid_out)


def rows_grad_kernel(me_ref, x_ref, rest_ref, *refs, blocks, rows):
    halves = [refs[3 * i : 3 * i + 3] for i in range(2)]
    parts = refs[6:10]
    dh_ref, gain_grad_ref, w_ref, grad_ref, sems = refs[-5:]
    me = me_ref[0]
    own = lax.rem(me, blocks)
    width = grad_ref.shape[1]
    span = width // 2
    own_at = pl.ds(pl.multiple_of(own * TILE, TILE), TILE)
    wait_all(load_shards(parts, me, w_ref, sems, rows, True))
    for i, (dq_ref, dk_ref, dv_ref) in enumerate(halves):
        grad = dot_nt(dk_ref[...], w_ref[:, width + i * span : width + (i + 1) * span])
        grad = grad + dot_nt(dv_ref[...], w_ref[:, 2 * width + i * span : 2 * width + (i + 1) * span])
        grad_ref[...] = grad if i == 0 else grad_ref[...] + grad
        grad_ref[own_at, :] = grad_ref[own_at, :] + dot_nt(dq_ref[...], w_ref[:, i * span : (i + 1) * span])
    gain_grad = jnp.zeros((1, width), F32)
    core = lax.rem(me // CORE_BIT, 2)
    for r in range(blocks):
        block = own ^ ((r & 1) * Y_BIT | depth_mask(r >> 1, core))
        at = pl.ds(pl.multiple_of(block * TILE, TILE), TILE)
        grad = grad_ref[at, :]
        source = rest_ref if r // 4 else x_ref
        unit, scale = normed(wide(source[r % 4, :TILE, :]))
        gain_grad = gain_grad + jnp.sum(grad * unit, axis=0, keepdims=True)
        dh_ref[r] = grad.astype(BF16)
    gain_grad_ref[...] = jnp.broadcast_to(gain_grad, gain_grad_ref.shape)


def qkv_grad_kernel(me_ref, h_ref, gain_grads_ref, gain_grad_ref, *refs, marks, blocks):
    halves = [refs[3 * i : 3 * i + 3] for i in range(2)]
    keep, send, dw_ref, out_sems = refs[6 + marks :]
    me = me_ref[0]
    own = lax.rem(me, blocks)
    width = h_ref.shape[1]
    span = width // 2
    own_at = pl.ds(pl.multiple_of(own * TILE, TILE), TILE)
    for i, (dq_ref, dk_ref, dv_ref) in enumerate(halves):
        put_blocks(dw_ref, slice(i * span, (i + 1) * span), dot_tn(h_ref[own_at, :], dq_ref[...]))
        put_blocks(dw_ref, slice(width + i * span, width + (i + 1) * span), dot_tn(h_ref[...], dk_ref[...]))
        put_blocks(dw_ref, slice(2 * width + i * span, 2 * width + (i + 1) * span), dot_tn(h_ref[...], dv_ref[...]))
    row = lax.broadcasted_iota(jnp.int32, (TILE, width), 0)
    rows_of = jnp.where(row == 0, gain_grad_ref[:1, :], jnp.where(row == 1, gain_grads_ref[1:2, :], gain_grads_ref[2:3, :]))
    put_blocks(dw_ref, slice(3 * width, 3 * width + TILE), rows_of.T)
    wait_all(store_blocks(dw_ref, me, (keep, send), out_sems))


def shaped(dims, kind):
    return jax.ShapeDtypeStruct(dims, kind)


def cube_body(inputs, segments, w_query, w_key, w_value, w_out, w_in, w_back, w_proj, gain_attn, gain_ffn, gain_final, rel_table, cotangent):
    blocks = lax.axis_size("blk")
    tokens, width = inputs.shape[1:]
    ff = w_in.shape[1]
    proj = w_proj.shape[1]
    heads = rel_table.shape[1]
    length = tokens * blocks
    rows = w_query.shape[0]
    back_rows = w_back.shape[0]
    own = lax.axis_index("blk").reshape(1).astype(jnp.int32)
    me = (lax.axis_index("head") * blocks + lax.axis_index("blk")).reshape(1).astype(jnp.int32)
    params = pltpu.CompilerParams(vmem_limit_bytes=VMEM_LIMIT)
    dma = pltpu.SemaphoreType.DMA((PEERS,))

    gains = jnp.stack([gain_attn, gain_ffn, gain_final], 1)
    gains = jnp.pad(gains, ((0, 0), (0, TILE - gains.shape[1])))
    pack_qkv = jnp.concatenate([w_query, w_key, w_value, gains], 1)
    pack_mid = jnp.concatenate([w_out, w_in, w_proj], 1)
    qkv_lanes = pack_qkv.shape[1]
    mid_lanes = pack_mid.shape[1]
    seg_row = jnp.pad(segments.astype(BF16), ((0, 7), (0, width - tokens)))
    own_x = jnp.concatenate([inputs[0], seg_row], 0)
    x_pair = jnp.stack([own_x, swap(own_x, Y_BIT)])
    qkv_first = swap(pack_qkv, NEAR_BIT, OVER_BIT)
    qkv_column = gather_depth(pack_qkv, qkv_first)
    x_half = jnp.concatenate([x_pair, swap(x_pair, NEAR_BIT, OVER_BIT)], 0)
    x_rest = swap(x_half, OVER_BIT, NEAR_BIT)
    qkv_parts = y_pairs(*gather_plane(qkv_column))
    qkv_parts = qkv_parts + [swap(part, CORE_BIT) for part in qkv_parts]
    pack_mid = tied(pack_mid, qkv_column)
    mid_first = swap(pack_mid, NEAR_BIT, OVER_BIT)
    mid_plane = gather_plane(gather_depth(pack_mid, mid_first))
    back_column = gather_depth(tied(w_back, mid_first))
    back_plane = gather_plane(back_column)
    hidden, key, value, query, gain_rows, kseg = pl.pallas_call(
        functools.partial(project_kernel, blocks=blocks, rows=rows),
        in_specs=[SMEM] + [WHOLE] * 2 + [ANY] * 6,
        out_specs=[WHOLE] * 6,
        out_shape=[
            shaped((length, width), BF16),
            shaped((length, width), BF16),
            shaped((length, width), BF16),
            shaped((tokens, width), BF16),
            shaped((8, width), F32),
            shaped((blocks, TILE), F32),
        ],
        scratch_shapes=[pltpu.VMEM((width, qkv_lanes), BF16), dma],
        compiler_params=params,
        cost_estimate=pl.CostEstimate(flops=2 * length * width * 2 * width, transcendentals=0, bytes_accessed=30 << 20),
        name="project",
    )(me, x_half, x_rest, *qkv_parts, mid_plane[0], back_column)
    bias = bias_rows(rel_table)
    attend, _ = attention_calls(length, width, heads, marks=1)
    qseg = segments.reshape(tokens, 1).astype(F32)
    attended, attended_low, lse = attend(own, query, key, value, qseg, kseg, bias, back_plane[0])
    mid_parts = y_pairs(*(tied(part, attended_low) for part in mid_plane))
    mid_parts = mid_parts + [swap(part, CORE_BIT) for part in mid_parts]
    back_parts = [*back_plane, *(swap(part, CORE_BIT) for part in back_plane)]
    states, grad_one, grad_attended, gain_grads, back_keep, back_send, mid_keep, mid_send = pl.pallas_call(
        functools.partial(ffn_kernel, ff=ff),
        in_specs=[SMEM] + [WHOLE] * 4 + [ANY] * 8,
        out_specs=[WHOLE] * 4 + [ANY] * 4,
        out_shape=[
            shaped((tokens, proj), BF16),
            shaped((tokens, width), F32),
            shaped((tokens, width), BF16),
            shaped((8, width), F32),
            shaped((PEERS // 2, back_rows, width), BF16),
            shaped((PEERS // 2, back_rows, width), BF16),
            shaped((PEERS // 2, rows, mid_lanes), BF16),
            shaped((PEERS // 2, rows, mid_lanes), BF16),
        ],
        scratch_shapes=[
            pltpu.VMEM((width, mid_lanes), BF16),
            pltpu.VMEM((ff, width), BF16),
            pltpu.VMEM((PEERS, rows, mid_lanes), BF16),
            pltpu.VMEM((PEERS, back_rows, width), BF16),
            dma,
            dma,
            dma,
            dma,
        ],
        compiler_params=params,
        cost_estimate=pl.CostEstimate(flops=6 * 2 * tokens * width * (ff + width), transcendentals=0, bytes_accessed=70 << 20),
        name="ffn",
    )(me, attended_low, own_x, cotangent[0], gain_rows, *mid_parts, *back_parts)
    back_terms = [back_keep, swap(back_send, CORE_BIT)]
    mid_terms = [mid_keep, swap(mid_send, CORE_BIT)]
    common = (own, query, key, value, grad_attended, attended, lse, qseg, kseg, bias)
    _, attend_back = attention_calls(length, width, heads, 0, heads // 4)
    *first_grads, first_sums = attend_back(*common)
    back_sent, mid_sent = next_sent(back_terms), next_sent(mid_terms)
    _, attend_back = attention_calls(length, width, heads, heads // 4, heads // 4, marks=2)
    *second_grads, second_sums = attend_back(*common, back_sent, mid_sent)
    back_terms = halved(back_terms, FIRST_SIDE, back_sent)
    mid_terms = halved(mid_terms, FIRST_SIDE, mid_sent)
    back_sent, mid_sent = next_sent(back_terms), next_sent(mid_terms)
    grad_parts = (*first_grads, *second_grads)
    grad_rows, gain_grad = pl.pallas_call(
        functools.partial(rows_grad_kernel, blocks=blocks, rows=rows),
        in_specs=[SMEM] + [WHOLE] * 8 + [ANY] * 5,
        out_specs=[WHOLE] * 2,
        out_shape=[shaped((blocks, tokens, width), BF16), shaped((8, width), F32)],
        scratch_shapes=[pltpu.VMEM((width, qkv_lanes), BF16), pltpu.VMEM((length, width), F32), dma],
        compiler_params=params,
        cost_estimate=pl.CostEstimate(flops=2 * 2 * length * width * width, transcendentals=0, bytes_accessed=30 << 20),
        name="rows_grad",
    )(me, x_half, x_rest, *grad_parts, *qkv_parts, back_sent)
    back_terms = halved(back_terms, SECOND_SIDE, back_sent)
    back_sent = next_sent(back_terms)
    marks = (mid_sent, back_sent)
    qkv_keep, qkv_send = pl.pallas_call(
        functools.partial(qkv_grad_kernel, marks=len(marks), blocks=blocks),
        in_specs=[SMEM] + [WHOLE] * 9 + [ANY] * len(marks),
        out_specs=[ANY, ANY],
        out_shape=[shaped((PEERS // 2, rows, qkv_lanes), BF16), shaped((PEERS // 2, rows, qkv_lanes), BF16)],
        scratch_shapes=[pltpu.VMEM((PEERS, rows, qkv_lanes), BF16), dma],
        compiler_params=params,
        cost_estimate=pl.CostEstimate(flops=2 * 2 * length * width * width, transcendentals=0, bytes_accessed=30 << 20),
        name="qkv_grad",
    )(me, hidden, gain_grads, gain_grad, *grad_parts, *marks)
    mid_terms = halved(mid_terms, SECOND_SIDE, mid_sent)
    mid_sent = next_sent(mid_terms)
    back_terms = halved(back_terms, FIRST_DEPTH, back_sent)
    back_sent = next_sent(back_terms)
    row_terms = halved([grad_rows], FIRST_DEPTH)
    row_sent = next_sent(row_terms)
    qkv_terms = [qkv_keep, swap(qkv_send, CORE_BIT)]
    qkv_terms = halved(qkv_terms, FIRST_SIDE, tied(next_sent(qkv_terms), mid_sent, back_sent, row_sent))
    mid_terms = halved(mid_terms, FIRST_DEPTH, mid_sent)
    mid_sent = next_sent(mid_terms)
    reduced_back = part_of(halved(back_terms, SECOND_DEPTH, back_sent), 0, 1)[0]
    row_terms = halved(row_terms, SECOND_DEPTH, row_sent)
    row_sent = next_sent(row_terms)
    qkv_terms = halved(qkv_terms, SECOND_SIDE, tied(next_sent(qkv_terms), mid_sent, row_sent))
    qkv_terms = halved(halved(qkv_terms, FIRST_DEPTH), SECOND_DEPTH)
    reduced_mid = part_of(halved(mid_terms, SECOND_DEPTH, mid_sent), 0, 1)[0]
    reduced_qkv = part_of(qkv_terms, 0, 1)[0]
    grad_hidden = part_of(halved(row_terms, (Y_BIT,), row_sent), 0, 1)[0]
    sums = jnp.concatenate([first_sums, second_sums], 0)
    unit, scale = normed(wide(inputs[0]))
    input_gradient_rows = grad_one + norm_back(grad_hidden, gain_rows[0], unit, scale)
    table = table_grad(sums, heads, rel_table.shape[0])
    every = lax.all_to_all(jnp.broadcast_to(table, (PEERS,) + table.shape), AXES, 0, 0)
    table = jnp.sum(every, axis=0)
    return outputs_of(states, input_gradient_rows, reduced_qkv, reduced_mid, reduced_back, table, width, ff, heads)


def body(*args):
    cube = lax.axis_size("head") == 4 and lax.axis_size("blk") == 8
    return (cube_body if cube else general_body)(*args)


def solution(mesh):
    rows = P(("head", "blk"), None)
    line = P(("head", "blk"))
    tokens = P("head", "blk", None)
    in_specs = (tokens, P("head", "blk")) + (rows,) * 7 + (line,) * 3 + (P(), tokens)
    out_specs = (tokens, tokens) + (rows,) * 7 + (line,) * 3 + (P(),)
    return jax.shard_map(body, mesh=mesh, in_specs=in_specs, out_specs=out_specs, check_vma=False)
```

```python
import functools
import math

import jax
import jax.numpy as jnp
import numpy as np
from jax import lax
from jax.experimental import pallas as pl
from jax.experimental.pallas import tpu as pltpu
from jax.sharding import PartitionSpec as P

BORDERS = (12, 16, 23, 32, 46, 64, 91)
MASKED = -1e30
EPS = 1e-6
TILE = 128
WIN = 512
BF16 = jnp.bfloat16
F32 = jnp.float32
AXES = ("head", "blk")
MIB = 1024 * 1024


def bucket_np(offset):
    distance = np.abs(offset)
    beyond = 8 + sum((distance >= border).astype(np.int64) for border in BORDERS)
    within = np.minimum(np.where(distance < 8, distance, beyond), 15)
    return within + 16 * (offset > 0)


def window_offsets():
    k = np.arange(WIN)
    return np.where(k < WIN - TILE, k - TILE, k - WIN - TILE)


def dot(a, b):
    return jnp.dot(a, b, preferred_element_type=F32)


def dot_nt(a, b):
    return lax.dot_general(a, b, (((1,), (1,)), ((), ())), preferred_element_type=F32)


def dot_tn(a, b):
    return lax.dot_general(a, b, (((0,), (0,)), ((), ())), preferred_element_type=F32)


class Links:
    def __init__(self):
        self.blocks = lax.axis_size("blk")
        self.total = lax.axis_size("head") * self.blocks
        self.me = lax.axis_index("head") * self.blocks + lax.axis_index("blk")
        self.bits = [1 << k for k in range(int(math.log2(self.total)))]
        self.blk_bits = [bit for bit in self.bits if bit < self.blocks]
        self.head_bits = [bit for bit in self.bits if bit >= self.blocks]

    def swap(self, value, bit):
        return lax.ppermute(value, AXES, [(i, i ^ bit) for i in range(self.total)])

    def mine(self, bit):
        return (self.me & bit) != 0


def gather_rows(links, shard, order, all_bits):
    high_first = sorted(all_bits, reverse=True)
    value = shard.reshape((1,) * len(high_first) + shard.shape)
    for bit in order:
        axis = high_first.index(bit)
        other = links.swap(value, bit)
        value = jnp.where(
            links.mine(bit),
            jnp.concatenate([other, value], axis),
            jnp.concatenate([value, other], axis),
        )
    return value.reshape((-1,) + shard.shape[1:])


def scatter_sum(links, whole, order, all_bits):
    high_first = sorted(all_bits, reverse=True)
    count = len(high_first)
    rows = whole.shape[0] >> count
    value = whole.reshape((2,) * count + (rows,) + whole.shape[1:])
    for bit in order:
        axis = high_first.index(bit)
        side = links.mine(bit).astype(jnp.int32)
        sent = lax.dynamic_slice_in_dim(value, 1 - side, 1, axis).astype(BF16)
        kept = lax.dynamic_slice_in_dim(value, side, 1, axis)
        value = kept.astype(F32) + links.swap(sent, bit).astype(F32)
    return value.reshape((rows,) + whole.shape[1:])


def bias_tiles(bias_ref, tiles_ref, head_row, side):
    row = bias_ref[pl.ds(head_row, 1), :]
    near = pltpu.roll(jnp.broadcast_to(row[:, :WIN], (TILE, WIN)), 0, 1, stride=1, stride_axis=0)
    rows = pl.ds(side * TILE, TILE)
    tiles_ref[0, rows, :] = jnp.broadcast_to(row[:, WIN : WIN + 1], (TILE, TILE))
    for t in range(3):
        tiles_ref[1 + t, rows, :] = near[:, t * TILE : (t + 1) * TILE]
    tiles_ref[4, rows, :] = jnp.broadcast_to(row[:, WIN + 1 : WIN + 2], (TILE, TILE))


def stacked(pair):
    lane = lax.broadcasted_iota(jnp.int32, pair.shape, 1)
    zero = jnp.zeros_like(pair)
    half = pair.shape[1] // 2
    return jnp.concatenate([jnp.where(lane < half, pair, zero), jnp.where(lane < half, zero, pair)], 0)


def unstacked(both):
    rows = both.shape[0] // 2
    lane = lax.broadcasted_iota(jnp.int32, (rows, both.shape[1]), 1)
    return jnp.where(lane < both.shape[1] // 2, both[:rows], both[rows:])


def tile_kind(key_tile, own_tile):
    return jnp.clip(key_tile - own_tile, -2, 2) + 2


def scores_into(chunk, chunk_tiles, own, q2, k_ref, qseg, kseg_ref, tiles_ref, s_ref):
    base = chunk * chunk_tiles * TILE
    raw = dot_nt(q2, k_ref[pl.ds(base, chunk_tiles * TILE), :])
    parts = []
    for t in range(chunk_tiles):
        at = base + t * TILE
        near = tiles_ref[tile_kind(chunk * chunk_tiles + t, own)]
        allowed = qseg == kseg_ref[pl.ds(chunk * chunk_tiles + t, 1), :]
        tile = jnp.where(allowed, raw[:, t * TILE : (t + 1) * TILE] + near, MASKED)
        s_ref[:, pl.ds(at, TILE)] = tile
        parts.append(tile)
    return parts


def attend_kernel(own_ref, q_ref, k_ref, v_ref, qseg_ref, kseg_ref, bias_ref, *refs, marks, chunks, chunk_tiles):
    o_ref, low_ref, lse_ref, tiles_ref, s_ref = refs[marks:]
    pair = pl.program_id(0)
    own = own_ref[0]
    for side in range(2):
        bias_tiles(bias_ref, tiles_ref, pair * 2 + side, side)
    q2 = stacked(q_ref[...])
    qseg = jnp.concatenate([qseg_ref[...], qseg_ref[...]], 0)

    def first(chunk, high):
        parts = scores_into(chunk, chunk_tiles, own, q2, k_ref, qseg, kseg_ref, tiles_ref, s_ref)
        return functools.reduce(jnp.maximum, parts, high)

    def second(chunk, total):
        for t in range(chunk_tiles):
            at = pl.ds((chunk * chunk_tiles + t) * TILE, TILE)
            powers = jnp.exp(s_ref[:, at] - high)
            s_ref[:, at] = powers
            total = total + powers
        return total

    def third(chunk, acc):
        base = chunk * chunk_tiles * TILE
        at = pl.ds(base, chunk_tiles * TILE)
        low = (s_ref[:, at] * inverse).astype(BF16)
        return acc + dot(low, v_ref[at, :])

    def loop(body, start):
        return body(0, start) if chunks == 1 else lax.fori_loop(0, chunks, body, start)

    high = loop(first, jnp.full((2 * TILE, TILE), MASKED, F32))
    high = jnp.max(high, axis=1, keepdims=True)
    total = jnp.sum(loop(second, jnp.zeros((2 * TILE, TILE), F32)), axis=1, keepdims=True)
    inverse = 1.0 / total
    out = unstacked(loop(third, jnp.zeros((2 * TILE, TILE), F32)))
    o_ref[...] = out
    low_ref[...] = out.astype(BF16)
    lse_ref[...] = jnp.broadcast_to(high + jnp.log(total), (2 * TILE, TILE))


def attend_back_kernel(own_ref, q_ref, k_ref, v_ref, do_ref, o_ref, lse_ref, qseg_ref, kseg_ref, bias_ref, *refs, first, marks, chunks, chunk_tiles):
    dq_ref, dk_ref, dv_ref, sums_ref, tiles_ref, s_ref, near_ref = refs[marks:]
    pair = pl.program_id(0) + first
    own = own_ref[0]
    for side in range(2):
        bias_tiles(bias_ref, tiles_ref, pair * 2 + side, side)
    q2 = stacked(q_ref[...])
    do2 = stacked(do_ref[...])
    delta = jnp.sum(stacked(do_ref[...].astype(F32) * o_ref[...]), axis=1, keepdims=True)
    lse = lse_ref[:, :1]
    qseg = jnp.concatenate([qseg_ref[...], qseg_ref[...]], 0)
    near_ref[...] = jnp.zeros_like(near_ref)

    def step(chunk, carried):
        acc, left, right = carried
        base = chunk * chunk_tiles * TILE
        at = pl.ds(base, chunk_tiles * TILE)
        scores_into(chunk, chunk_tiles, own, q2, k_ref, qseg, kseg_ref, tiles_ref, s_ref)
        probs = jnp.exp(s_ref[:, at] - lse)
        grad_probs = dot_nt(do2, v_ref[at, :])
        grads = (probs * (grad_probs - delta)).astype(BF16)
        acc = acc + dot(grads, k_ref[at, :])
        dk_ref[at, :] = dot_tn(grads, q2).astype(BF16)
        dv_ref[at, :] = dot_tn(probs.astype(BF16), do2).astype(BF16)
        wide = grads.astype(F32)
        for t in range(chunk_tiles):
            gap = chunk * chunk_tiles + t - own
            tile = wide[:, t * TILE : (t + 1) * TILE]
            left = left + jnp.where(gap < -1, tile, 0.0)
            right = right + jnp.where(gap > 1, tile, 0.0)

            @pl.when(jnp.abs(gap) <= 1)
            def _():
                near_ref[jnp.clip(gap + 1, 0, 2)] = tile

        return acc, left, right

    zero = jnp.zeros((2 * TILE, TILE), F32)
    start = (zero, zero, zero)
    acc, left, right = step(0, start) if chunks == 1 else lax.fori_loop(0, chunks, step, start)
    dq_ref[...] = unstacked(acc).astype(BF16)
    flip = (
        lax.broadcasted_iota(jnp.int32, (TILE, TILE), 0) + lax.broadcasted_iota(jnp.int32, (TILE, TILE), 1) == TILE - 1
    ).astype(BF16)
    for side in range(2):
        rows = slice(side * TILE, (side + 1) * TILE)
        window = jnp.concatenate([near_ref[t, rows, :] for t in range(4)], 1).astype(BF16)
        turned = pltpu.roll(dot(flip, window), 0, 1, stride=1, stride_axis=0)
        near_sum = jnp.sum(turned, axis=0, keepdims=True)
        far = [jnp.sum(jnp.sum(part[rows], axis=0, keepdims=True), axis=1, keepdims=True) for part in (left, right)]
        sums_ref[0, side : side + 1, :WIN] = near_sum
        lane = lax.broadcasted_iota(jnp.int32, (1, TILE), 1)
        sums_ref[0, side : side + 1, WIN:] = jnp.where(lane == 0, far[0], jnp.where(lane == 1, far[1], 0.0))


def attention_calls(length, width, heads, first=0, pairs=None, marks=0):
    total = heads // 2
    pairs = pairs or total
    tiles = length // TILE
    chunk_tiles = min(8, tiles)
    chunks = tiles // chunk_tiles
    wide = WIN + TILE
    lanes = width // total
    any_spec = pl.BlockSpec(memory_space=pl.ANY)
    own_spec = pl.BlockSpec(memory_space=pltpu.SMEM)
    q_spec = pl.BlockSpec((TILE, lanes), lambda p: (0, p + first))
    k_spec = pl.BlockSpec((length, lanes), lambda p: (0, p + first))
    dq_spec = pl.BlockSpec((TILE, lanes), lambda p: (0, p))
    dk_spec = pl.BlockSpec((length, lanes), lambda p: (0, p))
    qseg_spec = pl.BlockSpec((TILE, 1), lambda p: (0, 0))
    kseg_spec = pl.BlockSpec((tiles, TILE), lambda p: (0, 0))
    bias_spec = pl.BlockSpec((heads, wide), lambda p: (0, 0))
    lse_spec = pl.BlockSpec((2 * TILE, TILE), lambda p: (p + first, 0))
    sums_spec = pl.BlockSpec((1, 2, wide), lambda p: (p, 0, 0))
    scratch = [pltpu.VMEM((5, 2 * TILE, TILE), F32), pltpu.VMEM((2 * TILE, length), F32)]
    params = pltpu.CompilerParams(vmem_limit_bytes=(14 + length // 256) * MIB)

    def shape(dims, kind):
        return jax.ShapeDtypeStruct(dims, kind)

    forward = pl.pallas_call(
        functools.partial(attend_kernel, marks=marks, chunks=chunks, chunk_tiles=chunk_tiles),
        grid=(pairs,),
        in_specs=[own_spec, q_spec, k_spec, k_spec, qseg_spec, kseg_spec, bias_spec] + [any_spec] * marks,
        out_specs=[q_spec, q_spec, lse_spec],
        out_shape=[shape((TILE, width), F32), shape((TILE, width), BF16), shape((pairs * 2 * TILE, TILE), F32)],
        scratch_shapes=scratch,
        compiler_params=params,
        cost_estimate=pl.CostEstimate(flops=0, transcendentals=0, bytes_accessed=30 << 20),
        name="attend",
    )
    backward = pl.pallas_call(
        functools.partial(attend_back_kernel, first=first, marks=marks, chunks=chunks, chunk_tiles=chunk_tiles),
        grid=(pairs,),
        in_specs=[own_spec, q_spec, k_spec, k_spec, q_spec, q_spec, lse_spec, qseg_spec, kseg_spec, bias_spec]
        + [any_spec] * marks,
        out_specs=[dq_spec, dk_spec, dk_spec, sums_spec],
        out_shape=[
            shape((TILE, pairs * lanes), BF16),
            shape((length, pairs * lanes), BF16),
            shape((length, pairs * lanes), BF16),
            shape((pairs, 2, wide), F32),
        ],
        scratch_shapes=scratch + [pltpu.VMEM((4, 2 * TILE, TILE), F32)],
        compiler_params=params,
        cost_estimate=pl.CostEstimate(flops=0, transcendentals=0, bytes_accessed=48 << 20),
        name="attend_back",
    )
    return forward, backward


def normed(rows):
    scale = lax.rsqrt(jnp.mean(rows * rows, axis=-1, keepdims=True) + EPS)
    return rows * scale, scale


def norm_back(grad, gain, unit, scale):
    scaled = grad * gain
    return (scaled - unit * jnp.mean(scaled * unit, axis=-1, keepdims=True)) * scale


def bias_rows(rel_table):
    onehot = np.zeros((WIN + TILE, rel_table.shape[0]), np.float32)
    onehot[np.arange(WIN), bucket_np(window_offsets())] = 1.0
    onehot[WIN, 15] = 1.0
    onehot[WIN + 1, 31] = 1.0
    return lax.dot_general(
        rel_table, jnp.asarray(onehot, BF16), (((0,), (1,)), ((), ())), preferred_element_type=F32
    )


def table_grad(sums, heads, buckets):
    lane = np.arange(WIN)
    diagonal = np.zeros((WIN + TILE, buckets), np.float32)
    diagonal[lane, bucket_np(lane - (2 * TILE - 1))] = 1.0
    diagonal[WIN, 15] = 1.0
    diagonal[WIN + 1, 31] = 1.0
    table = lax.dot_general(
        jnp.asarray(diagonal),
        sums.reshape(heads, WIN + TILE),
        (((0,), (1,)), ((), ())),
        precision=lax.Precision.HIGHEST,
    )
    return jnp.pad(table, ((0, 0), (0, TILE - heads)))


def outputs_of(states, input_gradient_rows, reduced_qkv, reduced_mid, reduced_back, gain_grads, table, width, ff):
    return (
        states[None],
        input_gradient_rows[None],
        reduced_qkv[:, :width],
        reduced_qkv[:, width : 2 * width],
        reduced_qkv[:, 2 * width : 3 * width],
        reduced_mid[:, :width],
        reduced_mid[:, width : width + ff],
        reduced_back,
        reduced_mid[:, width + ff :],
        gain_grads[0],
        gain_grads[1],
        gain_grads[2],
        table,
    )


def general_body(inputs, segments, w_query, w_key, w_value, w_out, w_in, w_back, w_proj, gain_attn, gain_ffn, gain_final, rel_table, cotangent):
    links = Links()
    bits = links.bits
    tokens, width = inputs.shape[1:]
    ff = w_in.shape[1]
    proj = w_proj.shape[1]
    buckets, heads = rel_table.shape
    length = tokens * links.blocks
    rows = w_query.shape[0]
    own = lax.axis_index("blk").reshape(1).astype(jnp.int32)

    gains = jnp.stack([gain_attn, gain_ffn, gain_final], 1)
    gains = jnp.pad(gains, ((0, 0), (0, TILE - gains.shape[1])))
    pack_qkv = jnp.concatenate([w_query, w_key, w_value, gains], 1)
    pack_mid = jnp.concatenate([w_out, w_in, w_proj], 1)
    blk_down = [b for b in links.blk_bits if b > 1] + [1]
    order_a = blk_down + links.head_bits[::-1]
    own_rows = inputs[0]
    all_rows = gather_rows(links, own_rows, blk_down, links.blk_bits)
    seg_all = gather_rows(links, segments, blk_down, links.blk_bits)
    full_qkv = gather_rows(links, pack_qkv, order_a, bits)
    full_mid = gather_rows(links, pack_mid, order_a, bits)
    full_back = gather_rows(links, w_back, order_a, bits)
    full_query, full_key, full_value = (full_qkv[:, i * width : (i + 1) * width] for i in range(3))
    gain_rows = full_qkv[:, 3 * width :].astype(F32).T
    gain_one, gain_two, gain_three = gain_rows[0], gain_rows[1], gain_rows[2]
    full_out = full_mid[:, :width]
    full_in = full_mid[:, width : width + ff]
    full_proj = full_mid[:, width + ff :]

    bias = bias_rows(rel_table)

    states_in = own_rows.astype(F32)
    unit_all, scale_all = normed(all_rows.astype(F32))
    hidden_all = (unit_all * gain_one).astype(BF16)
    unit_one, scale_one = normed(states_in)
    hidden_one = (unit_one * gain_one).astype(BF16)
    query = dot(hidden_one, full_query).astype(BF16)
    key = dot(hidden_all, full_key).astype(BF16)
    value = dot(hidden_all, full_value).astype(BF16)
    attend, attend_back = attention_calls(length, width, heads)
    qseg = segments.reshape(tokens, 1)
    kseg = seg_all
    attended, attended_low, lse = attend(own, query, key, value, qseg, kseg, bias)
    resid_one = states_in + dot(attended_low, full_out)
    unit_two, scale_two = normed(resid_one)
    hidden_two = (unit_two * gain_two).astype(BF16)
    upward = dot(hidden_two, full_in)
    active, back_gelu = jax.vjp(lambda u: jax.nn.gelu(u, approximate=True), upward)
    active_low = active.astype(BF16)
    resid_two = resid_one + dot(active_low, full_back)
    unit_three, scale_three = normed(resid_two)
    final_low = (unit_three * gain_three).astype(BF16)
    states = dot(final_low, full_proj).astype(BF16)

    arriving = cotangent[0]
    grad_proj = dot_tn(final_low, arriving)
    grad_final = dot_nt(arriving, full_proj)
    grad_gain_three = jnp.sum(grad_final * unit_three, axis=0)
    grad_two = norm_back(grad_final, gain_three, unit_three, scale_three)
    grad_branch = grad_two.astype(BF16)
    grad_back = dot_tn(active_low, grad_branch)
    grad_up = back_gelu(dot_nt(grad_branch, full_back))[0].astype(BF16)
    grad_in = dot_tn(hidden_two, grad_up)
    grad_hidden_two = dot_nt(grad_up, full_in)
    grad_gain_two = jnp.sum(grad_hidden_two * unit_two, axis=0)
    grad_one = grad_two + norm_back(grad_hidden_two, gain_two, unit_two, scale_two)
    grad_attn = grad_one.astype(BF16)
    grad_out = dot_tn(attended_low, grad_attn)
    grad_attended = dot_nt(grad_attn, full_out).astype(BF16)
    grad_q, grad_k, grad_v, sums = attend_back(
        own, query, key, value, grad_attended, attended, lse, qseg, kseg, bias
    )
    grad_query = dot_tn(hidden_one, grad_q)
    grad_key = dot_tn(hidden_all, grad_k)
    grad_value = dot_tn(hidden_all, grad_v)
    grad_rows = dot_nt(grad_k, full_key) + dot_nt(grad_v, full_value)
    own_part = dot_nt(grad_q, full_query)
    first = lax.axis_index("blk") * tokens
    grad_rows = lax.dynamic_update_slice_in_dim(
        grad_rows, lax.dynamic_slice_in_dim(grad_rows, first, tokens, 0) + own_part, first, 0
    )
    grad_gain_one = jnp.sum(grad_rows * unit_all, axis=0)

    up_order = links.head_bits + [1] + [b for b in links.blk_bits if b > 1][::-1]
    blk_up = [1] + [b for b in links.blk_bits if b > 1][::-1]
    reduced_back = scatter_sum(links, grad_back, up_order, bits)
    reduced_mid = scatter_sum(links, jnp.concatenate([grad_out, grad_in, grad_proj], 1), up_order, bits)
    gain_grads = jnp.stack([grad_gain_one, grad_gain_two, grad_gain_three], 1)
    gain_grads = jnp.pad(gain_grads, ((0, 0), (0, TILE - 3)))
    reduced_qkv = scatter_sum(
        links, jnp.concatenate([grad_query, grad_key, grad_value, gain_grads], 1), up_order, bits
    )
    grad_hidden_one = scatter_sum(links, grad_rows, blk_up, links.blk_bits)
    input_gradient_rows = grad_one + norm_back(grad_hidden_one, gain_one, unit_one, scale_one)

    table = table_grad(sums, heads, rel_table.shape[0])
    for bit in bits:
        table = table + links.swap(table, bit)
    gain_grads = reduced_qkv[:, 3 * width :].T
    return outputs_of(
        states, input_gradient_rows, reduced_qkv, reduced_mid, reduced_back, gain_grads, table[:, :heads], width, ff
    )


X_BIT, CORE_BIT, Y_BIT = 16, 8, 1
NEAR_BIT, OVER_BIT = 2, 4
DEPTH = 4
PEERS = 32


def swap(value, mask, other_mask=None):
    masks = (mask, mask if other_mask is None else other_mask)
    return lax.ppermute(value, AXES, [(i, i ^ masks[(i // CORE_BIT) % 2]) for i in range(PEERS)])


def depth_mask(place, core):
    return (0, NEAR_BIT + core * (OVER_BIT - NEAR_BIT), OVER_BIT - core * (OVER_BIT - NEAR_BIT), NEAR_BIT | OVER_BIT)[place]


def side_masks(core):
    return Y_BIT + core * (X_BIT - Y_BIT), X_BIT - core * (X_BIT - Y_BIT)


def tied(value, *earlier):
    whole = functools.reduce(jnp.logical_and, [mark[(0,) * mark.ndim] == mark[(0,) * mark.ndim] for mark in earlier])
    return jnp.where(whole, value, jnp.zeros_like(value))


def gather_depth(own, first=None):
    first = swap(own, NEAR_BIT, OVER_BIT) if first is None else first
    pair = jnp.stack([own, first])
    return jnp.concatenate([pair, swap(pair, OVER_BIT, NEAR_BIT)], 0)


def gather_plane(column):
    half = jnp.concatenate([column, swap(column, Y_BIT, X_BIT)], 0)
    return half, swap(half, X_BIT, Y_BIT)


def y_pairs(half, rest):
    second = (lax.axis_index("head") % 2) == 1
    high = (lax.axis_index("blk") % 2) == 1
    pairs = (
        (half[:DEPTH], jnp.where(second, rest[:DEPTH], half[DEPTH:])),
        (jnp.where(second, half[DEPTH:], rest[:DEPTH]), rest[DEPTH:]),
    )
    return [
        jnp.where(high, jnp.concatenate([other, mine], 1), jnp.concatenate([mine, other], 1)) for mine, other in pairs
    ]


def gathered_items(core, paired):
    items = []
    for c in range(2):
        here = core if c == 0 else 1 - core
        first, second = side_masks(here)
        for b in range(2):
            for k in range(DEPTH):
                depth = depth_mask(k, here)
                if paired:
                    items.append((2 * c + b, k, (c * CORE_BIT + b * X_BIT) | depth))
                else:
                    items += [
                        (2 * c + b, a * DEPTH + k, (c * CORE_BIT) | (a * first) | (b * second) | depth) for a in range(2)
                    ]
    return items


def sent_items(core):
    items = []
    for c in range(2):
        here = core if c == 0 else 1 - core
        minor, major = side_masks(here)
        for a in range(2):
            for b in range(2):
                for k in range(DEPTH):
                    place = a * 2 * DEPTH + b * DEPTH + k
                    items.append((c, place, (c * CORE_BIT) | (a * major) | (b * minor) | depth_mask(k, here)))
    return items


def wide(value):
    return value.astype(F32)


def part_of(terms, first, last):
    return sum(wide(term[first:last]) for term in terms)


def next_sent(terms):
    half = terms[-1].shape[0] // 2
    return part_of(terms, half, 2 * half).astype(BF16)


def halved(terms, masks, sent=None):
    half = terms[-1].shape[0] // 2
    return [term[:half] for term in terms] + [swap(next_sent(terms) if sent is None else sent, *masks)]


FIRST_SIDE, SECOND_SIDE = (X_BIT, Y_BIT), (Y_BIT, X_BIT)
FIRST_DEPTH, SECOND_DEPTH = (OVER_BIT, NEAR_BIT), (NEAR_BIT, OVER_BIT)


ANY = pl.BlockSpec(memory_space=pl.ANY)
SMEM = pl.BlockSpec(memory_space=pltpu.SMEM)
WHOLE = pl.BlockSpec(memory_space=pltpu.VMEM)


def load_shards(parts, me, target, sems, rows, paired):
    copies = []
    rows = 2 * rows if paired else rows
    core = lax.rem(me // CORE_BIT, 2)
    for n, (buffer, place, relative) in enumerate(gathered_items(core, paired)):
        index = (me ^ relative) // 2 if paired else me ^ relative
        at = pl.multiple_of(index * rows, 16)
        copies.append(pltpu.make_async_copy(parts[buffer].at[place], target.at[pl.ds(at, rows), :], sems.at[n]))
    for copy in copies:
        copy.start()
    return copies


def store_blocks(source, me, targets, sems):
    copies = []
    for n, (side, place, relative) in enumerate(sent_items(lax.rem(me // CORE_BIT, 2))):
        copies.append(pltpu.make_async_copy(source.at[me ^ relative], targets[side].at[place], sems.at[n]))
    for copy in copies:
        copy.start()
    return copies


def put_blocks(target, lanes, value):
    rows = target.shape[1]
    for p in range(PEERS):
        target[p, :, lanes] = value[p * rows : (p + 1) * rows, :].astype(BF16)


def wait_all(copies):
    for copy in copies:
        copy.wait()


def project_kernel(me_ref, *refs, blocks, rows):
    xs = refs[:2]
    parts = refs[2:6]
    h_ref, k_ref, v_ref, q_ref, gains_ref, seg_ref, w_ref, sems = refs[-8:]
    me = me_ref[0]
    own = lax.rem(me, blocks)
    copies = load_shards(parts, me, w_ref, sems, rows, True)
    width = h_ref.shape[1]
    wait_all(copies)
    gains_ref[...] = wide(w_ref[:, 3 * width :]).T[:8]
    gain = gains_ref[0:1, :]
    core = lax.rem(me // CORE_BIT, 2)
    for r in range(blocks):
        x_ref = xs[r // 4].at[r % 4]
        unit, scale = normed(wide(x_ref[:TILE, :]))
        hidden = (unit * gain).astype(BF16)
        block = own ^ ((r & 1) * Y_BIT | depth_mask(r >> 1, core))
        at = pl.multiple_of(block * TILE, TILE)
        h_ref[pl.ds(at, TILE), :] = hidden
        seg_ref[pl.ds(block, 1), :] = wide(x_ref[TILE : TILE + 1, :TILE])
        if r == 0:
            q_ref[...] = dot(hidden, w_ref[:, :width]).astype(BF16)
    step = 512
    for start in range(0, h_ref.shape[0], step):
        at = slice(start, start + step)
        k_ref[at, :] = dot(h_ref[at, :], w_ref[:, width : 2 * width]).astype(BF16)
        v_ref[at, :] = dot(h_ref[at, :], w_ref[:, 2 * width : 3 * width]).astype(BF16)


GELU_C = math.sqrt(2.0 / math.pi)


def ffn_kernel(me_ref, att_ref, x_ref, cot_ref, gains_ref, *refs, ff):
    mid_parts, back_parts = refs[:4], refs[4:8]
    states_ref, one_ref, do_ref, gain_grads_ref, back_keep, back_send, mid_keep, mid_send = refs[8:16]
    mid_ref, back_ref, dmid_ref, dback_ref, mid_sems, back_sems, mid_out_sems, back_out_sems = refs[16:]
    me = me_ref[0]
    width = att_ref.shape[1]
    mid_rows = width // PEERS
    back_rows = ff // PEERS
    mid_copies = load_shards(mid_parts, me, mid_ref, mid_sems, mid_rows, True)
    back_copies = load_shards(back_parts, me, back_ref, back_sems, back_rows, False)
    gain_two = gains_ref[1:2, :]
    gain_three = gains_ref[2:3, :]
    w_out = slice(0, width)
    w_in = slice(width, width + ff)
    w_proj = slice(width + ff, mid_ref.shape[1])
    wait_all(mid_copies)
    resid_one = wide(x_ref[:TILE, :]) + dot(att_ref[...], mid_ref[:, w_out])
    unit_two, scale_two = normed(resid_one)
    hidden_two = (unit_two * gain_two).astype(BF16)
    up = dot(hidden_two, mid_ref[:, w_in])
    inner = GELU_C * (up + 0.044715 * (up * up * up))
    bent = jnp.tanh(inner)
    active = (0.5 * up * (1.0 + bent)).astype(BF16)
    slope = 0.5 * (1.0 + bent) + 0.5 * up * (1.0 - bent * bent) * (GELU_C * (1.0 + 3.0 * 0.044715 * (up * up)))
    wait_all(back_copies)
    resid_two = resid_one + dot(active, back_ref[...])
    unit_three, scale_three = normed(resid_two)
    final = (unit_three * gain_three).astype(BF16)
    states_ref[...] = dot(final, mid_ref[:, w_proj]).astype(BF16)
    grad_final = dot_nt(cot_ref[...], mid_ref[:, w_proj])
    grad_two = norm_back(grad_final, gain_three, unit_three, scale_three)
    branch = grad_two.astype(BF16)
    put_blocks(dback_ref, slice(None), dot_tn(active, branch))
    back_out = store_blocks(dback_ref, me, (back_keep, back_send), back_out_sems)
    grad_up = (dot_nt(branch, back_ref[...]) * slope).astype(BF16)
    grad_hidden = dot_nt(grad_up, mid_ref[:, w_in])
    grad_one = grad_two + norm_back(grad_hidden, gain_two, unit_two, scale_two)
    one_ref[...] = grad_one
    grad_attn = grad_one.astype(BF16)
    do_ref[...] = dot_nt(grad_attn, mid_ref[:, w_out]).astype(BF16)
    put_blocks(dmid_ref, w_out, dot_tn(att_ref[...], grad_attn))
    put_blocks(dmid_ref, w_in, dot_tn(hidden_two, grad_up))
    put_blocks(dmid_ref, w_proj, dot_tn(final, cot_ref[...]))
    mid_out = store_blocks(dmid_ref, me, (mid_keep, mid_send), mid_out_sems)
    gain_grads_ref[...] = jnp.zeros_like(gain_grads_ref)
    gain_grads_ref[1:2, :] = jnp.sum(grad_hidden * unit_two, axis=0, keepdims=True)
    gain_grads_ref[2:3, :] = jnp.sum(grad_final * unit_three, axis=0, keepdims=True)
    wait_all(back_out)
    wait_all(mid_out)


def rows_grad_kernel(me_ref, x_ref, rest_ref, *refs, blocks, rows):
    halves = [refs[3 * i : 3 * i + 3] for i in range(2)]
    parts = refs[6:10]
    *dh_refs, gain_grad_ref, w_ref, grad_ref, sems = refs[-6:]
    me = me_ref[0]
    own = lax.rem(me, blocks)
    width = grad_ref.shape[1]
    span = width // 2
    own_at = pl.ds(pl.multiple_of(own * TILE, TILE), TILE)
    wait_all(load_shards(parts, me, w_ref, sems, rows, True))
    for i, (dq_ref, dk_ref, dv_ref) in enumerate(halves):
        grad = dot_nt(dk_ref[...], w_ref[:, width + i * span : width + (i + 1) * span])
        grad = grad + dot_nt(dv_ref[...], w_ref[:, 2 * width + i * span : 2 * width + (i + 1) * span])
        grad_ref[...] = grad if i == 0 else grad_ref[...] + grad
        grad_ref[own_at, :] = grad_ref[own_at, :] + dot_nt(dq_ref[...], w_ref[:, i * span : (i + 1) * span])
    gain_grad = jnp.zeros((1, width), F32)
    core = lax.rem(me // CORE_BIT, 2)
    for r in range(blocks):
        block = own ^ ((r & 1) * Y_BIT | depth_mask(r >> 1, core))
        at = pl.ds(pl.multiple_of(block * TILE, TILE), TILE)
        grad = grad_ref[at, :]
        source = rest_ref if r // 4 else x_ref
        unit, scale = normed(wide(source[r % 4, :TILE, :]))
        gain_grad = gain_grad + jnp.sum(grad * unit, axis=0, keepdims=True)
        dh_refs[r & 1][r >> 1] = grad.astype(BF16)
    gain_grad_ref[...] = jnp.broadcast_to(gain_grad, gain_grad_ref.shape)


def qkv_grad_kernel(me_ref, h_ref, *refs, marks, blocks):
    halves = [refs[3 * i : 3 * i + 3] for i in range(2)]
    keep, send, dw_ref, out_sems = refs[6 + marks :]
    me = me_ref[0]
    own = lax.rem(me, blocks)
    width = h_ref.shape[1]
    span = width // 2
    own_at = pl.ds(pl.multiple_of(own * TILE, TILE), TILE)
    for i, (dq_ref, dk_ref, dv_ref) in enumerate(halves):
        put_blocks(dw_ref, slice(i * span, (i + 1) * span), dot_tn(h_ref[own_at, :], dq_ref[...]))
        put_blocks(dw_ref, slice(width + i * span, width + (i + 1) * span), dot_tn(h_ref[...], dk_ref[...]))
        put_blocks(dw_ref, slice(2 * width + i * span, 2 * width + (i + 1) * span), dot_tn(h_ref[...], dv_ref[...]))
    wait_all(store_blocks(dw_ref, me, (keep, send), out_sems))


def shaped(dims, kind):
    return jax.ShapeDtypeStruct(dims, kind)


def cube_body(inputs, segments, w_query, w_key, w_value, w_out, w_in, w_back, w_proj, gain_attn, gain_ffn, gain_final, rel_table, cotangent):
    blocks = lax.axis_size("blk")
    tokens, width = inputs.shape[1:]
    ff = w_in.shape[1]
    proj = w_proj.shape[1]
    heads = rel_table.shape[1]
    length = tokens * blocks
    rows = w_query.shape[0]
    back_rows = w_back.shape[0]
    own = lax.axis_index("blk").reshape(1).astype(jnp.int32)
    me = (lax.axis_index("head") * blocks + lax.axis_index("blk")).reshape(1).astype(jnp.int32)
    dma = pltpu.SemaphoreType.DMA((PEERS,))

    gains = jnp.stack([gain_attn, gain_ffn, gain_final], 1)
    gains = jnp.pad(gains, ((0, 0), (0, TILE - gains.shape[1])))
    pack_qkv = jnp.concatenate([w_query, w_key, w_value, gains], 1)
    pack_mid = jnp.concatenate([w_out, w_in, w_proj], 1)
    qkv_lanes = pack_qkv.shape[1]
    mid_lanes = pack_mid.shape[1]
    seg_row = jnp.pad(segments.astype(BF16), ((0, 7), (0, width - tokens)))
    own_x = jnp.concatenate([inputs[0], seg_row], 0)
    x_pair = jnp.stack([own_x, swap(own_x, Y_BIT)])
    qkv_first = swap(pack_qkv, NEAR_BIT, OVER_BIT)
    qkv_column = gather_depth(pack_qkv, qkv_first)
    x_half = jnp.concatenate([x_pair, swap(x_pair, NEAR_BIT, OVER_BIT)], 0)
    x_rest = swap(x_half, OVER_BIT, NEAR_BIT)
    qkv_parts = y_pairs(*gather_plane(qkv_column))
    qkv_parts = qkv_parts + [swap(part, CORE_BIT) for part in qkv_parts]
    pack_mid = tied(pack_mid, qkv_column)
    mid_first = swap(pack_mid, NEAR_BIT, OVER_BIT)
    mid_plane = gather_plane(gather_depth(pack_mid, mid_first))
    back_column = gather_depth(tied(w_back, mid_first))
    back_plane = gather_plane(back_column)
    hidden, key, value, query, gain_rows, kseg = pl.pallas_call(
        functools.partial(project_kernel, blocks=blocks, rows=rows),
        in_specs=[SMEM] + [WHOLE] * 2 + [ANY] * 6,
        out_specs=[WHOLE] * 6,
        out_shape=[
            shaped((length, width), BF16),
            shaped((length, width), BF16),
            shaped((length, width), BF16),
            shaped((tokens, width), BF16),
            shaped((8, width), F32),
            shaped((blocks, TILE), F32),
        ],
        scratch_shapes=[pltpu.VMEM((width, qkv_lanes), BF16), dma],
        compiler_params=pltpu.CompilerParams(vmem_limit_bytes=24 * MIB),
        cost_estimate=pl.CostEstimate(flops=2 * length * width * 2 * width, transcendentals=0, bytes_accessed=30 << 20),
        name="project",
    )(me, x_half, x_rest, *qkv_parts, mid_plane[0], back_column)
    bias = bias_rows(rel_table)
    attend, _ = attention_calls(length, width, heads, marks=1)
    qseg = segments.reshape(tokens, 1).astype(F32)
    attended, attended_low, lse = attend(own, query, key, value, qseg, kseg, bias, back_plane[0])
    mid_parts = y_pairs(*(tied(part, attended_low) for part in mid_plane))
    mid_parts = mid_parts + [swap(part, CORE_BIT) for part in mid_parts]
    back_parts = [*back_plane, *(swap(part, CORE_BIT) for part in back_plane)]
    states, grad_one, grad_attended, gain_grads, back_keep, back_send, mid_keep, mid_send = pl.pallas_call(
        functools.partial(ffn_kernel, ff=ff),
        in_specs=[SMEM] + [WHOLE] * 4 + [ANY] * 8,
        out_specs=[WHOLE] * 4 + [ANY] * 4,
        out_shape=[
            shaped((tokens, proj), BF16),
            shaped((tokens, width), F32),
            shaped((tokens, width), BF16),
            shaped((8, width), F32),
            shaped((PEERS // 2, back_rows, width), BF16),
            shaped((PEERS // 2, back_rows, width), BF16),
            shaped((PEERS // 2, rows, mid_lanes), BF16),
            shaped((PEERS // 2, rows, mid_lanes), BF16),
        ],
        scratch_shapes=[
            pltpu.VMEM((width, mid_lanes), BF16),
            pltpu.VMEM((ff, width), BF16),
            pltpu.VMEM((PEERS, rows, mid_lanes), BF16),
            pltpu.VMEM((PEERS, back_rows, width), BF16),
            dma,
            dma,
            dma,
            dma,
        ],
        compiler_params=pltpu.CompilerParams(vmem_limit_bytes=56 * MIB),
        cost_estimate=pl.CostEstimate(flops=6 * 2 * tokens * width * (ff + width), transcendentals=0, bytes_accessed=70 << 20),
        name="ffn",
    )(me, attended_low, own_x, cotangent[0], gain_rows, *mid_parts, *back_parts)
    back_terms = [back_keep, swap(back_send, CORE_BIT)]
    mid_terms = [mid_keep, swap(mid_send, CORE_BIT)]
    common = (own, query, key, value, grad_attended, attended, lse, qseg, kseg, bias)
    _, attend_back = attention_calls(length, width, heads, 0, heads // 4)
    *first_grads, first_sums = attend_back(*common)
    back_sent, mid_sent = next_sent(back_terms), next_sent(mid_terms)
    _, attend_back = attention_calls(length, width, heads, heads // 4, heads // 4, marks=2)
    *second_grads, second_sums = attend_back(*common, back_sent, mid_sent)
    back_terms = halved(back_terms, FIRST_SIDE, back_sent)
    mid_terms = halved(mid_terms, FIRST_SIDE, mid_sent)
    grad_parts = (*first_grads, *second_grads)
    lanes = 3 * width
    qkv_keep, qkv_send = pl.pallas_call(
        functools.partial(qkv_grad_kernel, marks=0, blocks=blocks),
        in_specs=[SMEM] + [WHOLE] * 7,
        out_specs=[ANY, ANY],
        out_shape=[shaped((PEERS // 2, rows, lanes), BF16), shaped((PEERS // 2, rows, lanes), BF16)],
        scratch_shapes=[pltpu.VMEM((PEERS, rows, lanes), BF16), dma],
        compiler_params=pltpu.CompilerParams(vmem_limit_bytes=26 * MIB),
        cost_estimate=pl.CostEstimate(flops=2 * 2 * length * width * width, transcendentals=0, bytes_accessed=30 << 20),
        name="qkv_grad",
    )(me, hidden, *grad_parts)
    qkv_terms = [qkv_keep, swap(qkv_send, CORE_BIT)]
    back_sent, mid_sent = tied(next_sent(back_terms), qkv_keep), tied(next_sent(mid_terms), qkv_keep)
    qkv_sent = next_sent(qkv_terms)
    rows_keep, rows_send, gain_grad = pl.pallas_call(
        functools.partial(rows_grad_kernel, blocks=blocks, rows=rows),
        in_specs=[SMEM] + [WHOLE] * 8 + [ANY] * 7,
        out_specs=[WHOLE] * 3,
        out_shape=[shaped((blocks // 2, tokens, width), BF16)] * 2 + [shaped((8, width), F32)],
        scratch_shapes=[pltpu.VMEM((width, qkv_lanes), BF16), pltpu.VMEM((length, width), F32), dma],
        compiler_params=pltpu.CompilerParams(vmem_limit_bytes=30 * MIB),
        cost_estimate=pl.CostEstimate(flops=2 * 2 * length * width * width, transcendentals=0, bytes_accessed=30 << 20),
        name="rows_grad",
    )(me, x_half, x_rest, *grad_parts, *qkv_parts, back_sent, mid_sent, qkv_sent)
    qkv_terms = halved(qkv_terms, FIRST_SIDE, qkv_sent)
    back_terms = halved(back_terms, SECOND_SIDE, back_sent)
    mid_terms = halved(mid_terms, SECOND_SIDE, mid_sent)
    row_terms = [rows_keep, swap(rows_send, Y_BIT)]
    back_terms = halved(back_terms, FIRST_DEPTH)
    mid_terms = halved(mid_terms, FIRST_DEPTH)
    qkv_sent = next_sent(qkv_terms)
    qkv_terms = halved(qkv_terms, SECOND_SIDE, qkv_sent)
    row_terms = halved(row_terms, FIRST_DEPTH, tied(next_sent(row_terms), qkv_sent))
    back_terms = halved(back_terms, SECOND_DEPTH, tied(next_sent(back_terms), qkv_sent))
    mid_terms = halved(mid_terms, SECOND_DEPTH, tied(next_sent(mid_terms), qkv_sent))
    qkv_sent = next_sent(qkv_terms)
    after_sides = qkv_sent
    qkv_terms = halved(qkv_terms, FIRST_DEPTH, qkv_sent)
    row_terms = halved(row_terms, SECOND_DEPTH)
    qkv_terms = halved(qkv_terms, SECOND_DEPTH)
    reduced_back, reduced_mid, reduced_qkv, grad_hidden = (
        part_of(terms, 0, 1)[0] for terms in (back_terms, mid_terms, qkv_terms, row_terms)
    )
    sums = jnp.concatenate([first_sums, second_sums], 0)
    unit, scale = normed(wide(inputs[0]))
    input_gradient_rows = grad_one + norm_back(grad_hidden, gain_rows[0], unit, scale)
    buckets = rel_table.shape[0]
    table = table_grad(sums, heads, buckets)[:, :heads].reshape(1, -1, TILE)
    gain_grads = jnp.stack([gain_grad[0], gain_grads[1], gain_grads[2]]).reshape(3, PEERS, rows)
    gain_grads = jnp.pad(gain_grads.transpose(1, 0, 2), ((0, 0), (0, 8 - 3 - table.shape[1]), (0, TILE - rows)))
    small = jnp.concatenate([jnp.broadcast_to(table, (PEERS,) + table.shape[1:]), gain_grads], 1)
    small = tied(small, after_sides)
    small = jnp.sum(lax.all_to_all(small, AXES, 0, 0), axis=0)
    first = table.shape[1]
    table = small[:first].reshape(buckets, heads)
    return outputs_of(
        states, input_gradient_rows, reduced_qkv, reduced_mid, reduced_back, small[first : first + 3, :rows], table, width, ff
    )


def body(*args):
    cube = lax.axis_size("head") == 4 and lax.axis_size("blk") == 8
    return (cube_body if cube else general_body)(*args)


def solution(mesh):
    rows = P(("head", "blk"), None)
    line = P(("head", "blk"))
    tokens = P("head", "blk", None)
    in_specs = (tokens, P("head", "blk")) + (rows,) * 7 + (line,) * 3 + (P(), tokens)
    out_specs = (tokens, tokens) + (rows,) * 7 + (line,) * 3 + (P(),)
    return jax.shard_map(body, mesh=mesh, in_specs=in_specs, out_specs=out_specs, check_vma=False)
```

```python
import functools
import math

import jax
import jax.numpy as jnp
import numpy as np
from jax import lax
from jax.experimental import pallas as pl
from jax.experimental.pallas import tpu as pltpu
from jax.sharding import PartitionSpec as P

BORDERS = (12, 16, 23, 32, 46, 64, 91)
MASKED = -1e30
EPS = 1e-6
TILE = 128
WIN = 512
BF16 = jnp.bfloat16
F32 = jnp.float32
AXES = ("head", "blk")
MIB = 1024 * 1024


def bucket_np(offset):
    distance = np.abs(offset)
    beyond = 8 + sum((distance >= border).astype(np.int64) for border in BORDERS)
    within = np.minimum(np.where(distance < 8, distance, beyond), 15)
    return within + 16 * (offset > 0)


def window_offsets():
    k = np.arange(WIN)
    return np.where(k < WIN - TILE, k - TILE, k - WIN - TILE)


def dot(a, b):
    return jnp.dot(a, b, preferred_element_type=F32)


def dot_nt(a, b):
    return lax.dot_general(a, b, (((1,), (1,)), ((), ())), preferred_element_type=F32)


def dot_tn(a, b):
    return lax.dot_general(a, b, (((0,), (0,)), ((), ())), preferred_element_type=F32)


class Links:
    def __init__(self):
        self.blocks = lax.axis_size("blk")
        self.total = lax.axis_size("head") * self.blocks
        self.me = lax.axis_index("head") * self.blocks + lax.axis_index("blk")
        self.bits = [1 << k for k in range(int(math.log2(self.total)))]
        self.blk_bits = [bit for bit in self.bits if bit < self.blocks]
        self.head_bits = [bit for bit in self.bits if bit >= self.blocks]

    def swap(self, value, bit):
        return lax.ppermute(value, AXES, [(i, i ^ bit) for i in range(self.total)])

    def mine(self, bit):
        return (self.me & bit) != 0


def gather_rows(links, shard, order, all_bits):
    high_first = sorted(all_bits, reverse=True)
    value = shard.reshape((1,) * len(high_first) + shard.shape)
    for bit in order:
        axis = high_first.index(bit)
        other = links.swap(value, bit)
        value = jnp.where(
            links.mine(bit),
            jnp.concatenate([other, value], axis),
            jnp.concatenate([value, other], axis),
        )
    return value.reshape((-1,) + shard.shape[1:])


def scatter_sum(links, whole, order, all_bits):
    high_first = sorted(all_bits, reverse=True)
    count = len(high_first)
    rows = whole.shape[0] >> count
    value = whole.reshape((2,) * count + (rows,) + whole.shape[1:])
    for bit in order:
        axis = high_first.index(bit)
        side = links.mine(bit).astype(jnp.int32)
        sent = lax.dynamic_slice_in_dim(value, 1 - side, 1, axis).astype(BF16)
        kept = lax.dynamic_slice_in_dim(value, side, 1, axis)
        value = kept.astype(F32) + links.swap(sent, bit).astype(F32)
    return value.reshape((rows,) + whole.shape[1:])


def bias_tiles(bias_ref, tiles_ref, head_row, side):
    row = bias_ref[pl.ds(head_row, 1), :]
    near = pltpu.roll(jnp.broadcast_to(row[:, :WIN], (TILE, WIN)), 0, 1, stride=1, stride_axis=0)
    rows = pl.ds(side * TILE, TILE)
    tiles_ref[0, rows, :] = jnp.broadcast_to(row[:, WIN : WIN + 1], (TILE, TILE))
    for t in range(3):
        tiles_ref[1 + t, rows, :] = near[:, t * TILE : (t + 1) * TILE]
    tiles_ref[4, rows, :] = jnp.broadcast_to(row[:, WIN + 1 : WIN + 2], (TILE, TILE))


def stacked(pair):
    lane = lax.broadcasted_iota(jnp.int32, pair.shape, 1)
    zero = jnp.zeros_like(pair)
    half = pair.shape[1] // 2
    return jnp.concatenate([jnp.where(lane < half, pair, zero), jnp.where(lane < half, zero, pair)], 0)


def unstacked(both):
    rows = both.shape[0] // 2
    lane = lax.broadcasted_iota(jnp.int32, (rows, both.shape[1]), 1)
    return jnp.where(lane < both.shape[1] // 2, both[:rows], both[rows:])


def tile_kind(key_tile, own_tile):
    return jnp.clip(key_tile - own_tile, -2, 2) + 2


def scores_into(chunk, chunk_tiles, own, q2, k_ref, qseg, kseg_ref, tiles_ref, s_ref):
    base = chunk * chunk_tiles * TILE
    raw = dot_nt(q2, k_ref[pl.ds(base, chunk_tiles * TILE), :])
    parts = []
    for t in range(chunk_tiles):
        at = base + t * TILE
        near = tiles_ref[tile_kind(chunk * chunk_tiles + t, own)]
        allowed = qseg == kseg_ref[pl.ds(chunk * chunk_tiles + t, 1), :]
        tile = jnp.where(allowed, raw[:, t * TILE : (t + 1) * TILE] + near, MASKED)
        s_ref[:, pl.ds(at, TILE)] = tile
        parts.append(tile)
    return parts


def attend_kernel(own_ref, q_ref, k_ref, v_ref, qseg_ref, kseg_ref, bias_ref, *refs, marks, chunks, chunk_tiles):
    o_ref, low_ref, lse_ref, tiles_ref, s_ref = refs[marks:]
    pair = pl.program_id(0)
    own = own_ref[0]
    for side in range(2):
        bias_tiles(bias_ref, tiles_ref, pair * 2 + side, side)
    q2 = stacked(q_ref[...])
    qseg = jnp.concatenate([qseg_ref[...], qseg_ref[...]], 0)

    def first(chunk, high):
        parts = scores_into(chunk, chunk_tiles, own, q2, k_ref, qseg, kseg_ref, tiles_ref, s_ref)
        return functools.reduce(jnp.maximum, parts, high)

    def second(chunk, total):
        for t in range(chunk_tiles):
            at = pl.ds((chunk * chunk_tiles + t) * TILE, TILE)
            powers = jnp.exp(s_ref[:, at] - high)
            s_ref[:, at] = powers
            total = total + powers
        return total

    def third(chunk, acc):
        base = chunk * chunk_tiles * TILE
        at = pl.ds(base, chunk_tiles * TILE)
        low = (s_ref[:, at] * inverse).astype(BF16)
        return acc + dot(low, v_ref[at, :])

    def loop(body, start):
        return body(0, start) if chunks == 1 else lax.fori_loop(0, chunks, body, start)

    high = loop(first, jnp.full((2 * TILE, TILE), MASKED, F32))
    high = jnp.max(high, axis=1, keepdims=True)
    total = jnp.sum(loop(second, jnp.zeros((2 * TILE, TILE), F32)), axis=1, keepdims=True)
    inverse = 1.0 / total
    out = unstacked(loop(third, jnp.zeros((2 * TILE, TILE), F32)))
    o_ref[...] = out
    low_ref[...] = out.astype(BF16)
    lse_ref[...] = jnp.broadcast_to(high + jnp.log(total), (2 * TILE, TILE))


def attend_back_kernel(own_ref, q_ref, k_ref, v_ref, do_ref, o_ref, lse_ref, qseg_ref, kseg_ref, bias_ref, *refs, first, marks, chunks, chunk_tiles):
    dq_ref, dk_ref, dv_ref, sums_ref, tiles_ref, s_ref, near_ref = refs[marks:]
    pair = pl.program_id(0) + first
    own = own_ref[0]
    for side in range(2):
        bias_tiles(bias_ref, tiles_ref, pair * 2 + side, side)
    q2 = stacked(q_ref[...])
    do2 = stacked(do_ref[...])
    delta = jnp.sum(stacked(do_ref[...].astype(F32) * o_ref[...]), axis=1, keepdims=True)
    lse = lse_ref[:, :1]
    qseg = jnp.concatenate([qseg_ref[...], qseg_ref[...]], 0)
    near_ref[...] = jnp.zeros_like(near_ref)

    def step(chunk, carried):
        acc, left, right = carried
        base = chunk * chunk_tiles * TILE
        at = pl.ds(base, chunk_tiles * TILE)
        scores_into(chunk, chunk_tiles, own, q2, k_ref, qseg, kseg_ref, tiles_ref, s_ref)
        probs = jnp.exp(s_ref[:, at] - lse)
        grad_probs = dot_nt(do2, v_ref[at, :])
        grads = (probs * (grad_probs - delta)).astype(BF16)
        acc = acc + dot(grads, k_ref[at, :])
        dk_ref[at, :] = dot_tn(grads, q2).astype(BF16)
        dv_ref[at, :] = dot_tn(probs.astype(BF16), do2).astype(BF16)
        wide = grads.astype(F32)
        for t in range(chunk_tiles):
            gap = chunk * chunk_tiles + t - own
            tile = wide[:, t * TILE : (t + 1) * TILE]
            left = left + jnp.where(gap < -1, tile, 0.0)
            right = right + jnp.where(gap > 1, tile, 0.0)

            @pl.when(jnp.abs(gap) <= 1)
            def _():
                near_ref[jnp.clip(gap + 1, 0, 2)] = tile

        return acc, left, right

    zero = jnp.zeros((2 * TILE, TILE), F32)
    start = (zero, zero, zero)
    acc, left, right = step(0, start) if chunks == 1 else lax.fori_loop(0, chunks, step, start)
    dq_ref[...] = unstacked(acc).astype(BF16)
    flip = (
        lax.broadcasted_iota(jnp.int32, (TILE, TILE), 0) + lax.broadcasted_iota(jnp.int32, (TILE, TILE), 1) == TILE - 1
    ).astype(BF16)
    for side in range(2):
        rows = slice(side * TILE, (side + 1) * TILE)
        window = jnp.concatenate([near_ref[t, rows, :] for t in range(4)], 1).astype(BF16)
        turned = pltpu.roll(dot(flip, window), 0, 1, stride=1, stride_axis=0)
        near_sum = jnp.sum(turned, axis=0, keepdims=True)
        far = [jnp.sum(jnp.sum(part[rows], axis=0, keepdims=True), axis=1, keepdims=True) for part in (left, right)]
        sums_ref[0, side : side + 1, :WIN] = near_sum
        lane = lax.broadcasted_iota(jnp.int32, (1, TILE), 1)
        sums_ref[0, side : side + 1, WIN:] = jnp.where(lane == 0, far[0], jnp.where(lane == 1, far[1], 0.0))


def attention_calls(length, width, heads, first=0, pairs=None, marks=0):
    total = heads // 2
    pairs = pairs or total
    tiles = length // TILE
    chunk_tiles = min(8, tiles)
    chunks = tiles // chunk_tiles
    wide = WIN + TILE
    lanes = width // total
    any_spec = pl.BlockSpec(memory_space=pl.ANY)
    own_spec = pl.BlockSpec(memory_space=pltpu.SMEM)
    q_spec = pl.BlockSpec((TILE, lanes), lambda p: (0, p + first))
    k_spec = pl.BlockSpec((length, lanes), lambda p: (0, p + first))
    dq_spec = pl.BlockSpec((TILE, lanes), lambda p: (0, p))
    dk_spec = pl.BlockSpec((length, lanes), lambda p: (0, p))
    qseg_spec = pl.BlockSpec((TILE, 1), lambda p: (0, 0))
    kseg_spec = pl.BlockSpec((tiles, TILE), lambda p: (0, 0))
    bias_spec = pl.BlockSpec((heads, wide), lambda p: (0, 0))
    lse_spec = pl.BlockSpec((2 * TILE, TILE), lambda p: (p + first, 0))
    sums_spec = pl.BlockSpec((1, 2, wide), lambda p: (p, 0, 0))
    scratch = [pltpu.VMEM((5, 2 * TILE, TILE), F32), pltpu.VMEM((2 * TILE, length), F32)]
    params = pltpu.CompilerParams(vmem_limit_bytes=(14 + length // 256) * MIB)

    def shape(dims, kind):
        return jax.ShapeDtypeStruct(dims, kind)

    forward = pl.pallas_call(
        functools.partial(attend_kernel, marks=marks, chunks=chunks, chunk_tiles=chunk_tiles),
        grid=(pairs,),
        in_specs=[own_spec, q_spec, k_spec, k_spec, qseg_spec, kseg_spec, bias_spec] + [any_spec] * marks,
        out_specs=[q_spec, q_spec, lse_spec],
        out_shape=[shape((TILE, width), F32), shape((TILE, width), BF16), shape((pairs * 2 * TILE, TILE), F32)],
        scratch_shapes=scratch,
        compiler_params=params,
        cost_estimate=pl.CostEstimate(flops=0, transcendentals=0, bytes_accessed=30 << 20),
        name="attend",
    )
    backward = pl.pallas_call(
        functools.partial(attend_back_kernel, first=first, marks=marks, chunks=chunks, chunk_tiles=chunk_tiles),
        grid=(pairs,),
        in_specs=[own_spec, q_spec, k_spec, k_spec, q_spec, q_spec, lse_spec, qseg_spec, kseg_spec, bias_spec]
        + [any_spec] * marks,
        out_specs=[dq_spec, dk_spec, dk_spec, sums_spec],
        out_shape=[
            shape((TILE, pairs * lanes), BF16),
            shape((length, pairs * lanes), BF16),
            shape((length, pairs * lanes), BF16),
            shape((pairs, 2, wide), F32),
        ],
        scratch_shapes=scratch + [pltpu.VMEM((4, 2 * TILE, TILE), F32)],
        compiler_params=params,
        cost_estimate=pl.CostEstimate(flops=0, transcendentals=0, bytes_accessed=48 << 20),
        name="attend_back",
    )
    return forward, backward


def normed(rows):
    scale = lax.rsqrt(jnp.mean(rows * rows, axis=-1, keepdims=True) + EPS)
    return rows * scale, scale


def norm_back(grad, gain, unit, scale):
    scaled = grad * gain
    return (scaled - unit * jnp.mean(scaled * unit, axis=-1, keepdims=True)) * scale


def bias_rows(rel_table):
    onehot = np.zeros((WIN + TILE, rel_table.shape[0]), np.float32)
    onehot[np.arange(WIN), bucket_np(window_offsets())] = 1.0
    onehot[WIN, 15] = 1.0
    onehot[WIN + 1, 31] = 1.0
    return lax.dot_general(
        rel_table, jnp.asarray(onehot, BF16), (((0,), (1,)), ((), ())), preferred_element_type=F32
    )


def table_grad(sums, heads, buckets):
    lane = np.arange(WIN)
    diagonal = np.zeros((WIN + TILE, buckets), np.float32)
    diagonal[lane, bucket_np(lane - (2 * TILE - 1))] = 1.0
    diagonal[WIN, 15] = 1.0
    diagonal[WIN + 1, 31] = 1.0
    table = lax.dot_general(
        jnp.asarray(diagonal),
        sums.reshape(heads, WIN + TILE),
        (((0,), (1,)), ((), ())),
        precision=lax.Precision.HIGHEST,
    )
    return jnp.pad(table, ((0, 0), (0, TILE - heads)))


def outputs_of(states, input_gradient_rows, reduced_qkv, reduced_mid, reduced_back, gain_grads, table, width, ff):
    return (
        states[None],
        input_gradient_rows[None],
        reduced_qkv[:, :width],
        reduced_qkv[:, width : 2 * width],
        reduced_qkv[:, 2 * width : 3 * width],
        reduced_mid[:, :width],
        reduced_mid[:, width : width + ff],
        reduced_back,
        reduced_mid[:, width + ff :],
        gain_grads[0],
        gain_grads[1],
        gain_grads[2],
        table,
    )


def general_body(inputs, segments, w_query, w_key, w_value, w_out, w_in, w_back, w_proj, gain_attn, gain_ffn, gain_final, rel_table, cotangent):
    links = Links()
    bits = links.bits
    tokens, width = inputs.shape[1:]
    ff = w_in.shape[1]
    proj = w_proj.shape[1]
    buckets, heads = rel_table.shape
    length = tokens * links.blocks
    rows = w_query.shape[0]
    own = lax.axis_index("blk").reshape(1).astype(jnp.int32)

    gains = jnp.stack([gain_attn, gain_ffn, gain_final], 1)
    gains = jnp.pad(gains, ((0, 0), (0, TILE - gains.shape[1])))
    pack_qkv = jnp.concatenate([w_query, w_key, w_value, gains], 1)
    pack_mid = jnp.concatenate([w_out, w_in, w_proj], 1)
    blk_down = [b for b in links.blk_bits if b > 1] + [1]
    order_a = blk_down + links.head_bits[::-1]
    own_rows = inputs[0]
    all_rows = gather_rows(links, own_rows, blk_down, links.blk_bits)
    seg_all = gather_rows(links, segments, blk_down, links.blk_bits)
    full_qkv = gather_rows(links, pack_qkv, order_a, bits)
    full_mid = gather_rows(links, pack_mid, order_a, bits)
    full_back = gather_rows(links, w_back, order_a, bits)
    full_query, full_key, full_value = (full_qkv[:, i * width : (i + 1) * width] for i in range(3))
    gain_rows = full_qkv[:, 3 * width :].astype(F32).T
    gain_one, gain_two, gain_three = gain_rows[0], gain_rows[1], gain_rows[2]
    full_out = full_mid[:, :width]
    full_in = full_mid[:, width : width + ff]
    full_proj = full_mid[:, width + ff :]

    bias = bias_rows(rel_table)

    states_in = own_rows.astype(F32)
    unit_all, scale_all = normed(all_rows.astype(F32))
    hidden_all = (unit_all * gain_one).astype(BF16)
    unit_one, scale_one = normed(states_in)
    hidden_one = (unit_one * gain_one).astype(BF16)
    query = dot(hidden_one, full_query).astype(BF16)
    key = dot(hidden_all, full_key).astype(BF16)
    value = dot(hidden_all, full_value).astype(BF16)
    attend, attend_back = attention_calls(length, width, heads)
    qseg = segments.reshape(tokens, 1)
    kseg = seg_all
    attended, attended_low, lse = attend(own, query, key, value, qseg, kseg, bias)
    resid_one = states_in + dot(attended_low, full_out)
    unit_two, scale_two = normed(resid_one)
    hidden_two = (unit_two * gain_two).astype(BF16)
    upward = dot(hidden_two, full_in)
    active, back_gelu = jax.vjp(lambda u: jax.nn.gelu(u, approximate=True), upward)
    active_low = active.astype(BF16)
    resid_two = resid_one + dot(active_low, full_back)
    unit_three, scale_three = normed(resid_two)
    final_low = (unit_three * gain_three).astype(BF16)
    states = dot(final_low, full_proj).astype(BF16)

    arriving = cotangent[0]
    grad_proj = dot_tn(final_low, arriving)
    grad_final = dot_nt(arriving, full_proj)
    grad_gain_three = jnp.sum(grad_final * unit_three, axis=0)
    grad_two = norm_back(grad_final, gain_three, unit_three, scale_three)
    grad_branch = grad_two.astype(BF16)
    grad_back = dot_tn(active_low, grad_branch)
    grad_up = back_gelu(dot_nt(grad_branch, full_back))[0].astype(BF16)
    grad_in = dot_tn(hidden_two, grad_up)
    grad_hidden_two = dot_nt(grad_up, full_in)
    grad_gain_two = jnp.sum(grad_hidden_two * unit_two, axis=0)
    grad_one = grad_two + norm_back(grad_hidden_two, gain_two, unit_two, scale_two)
    grad_attn = grad_one.astype(BF16)
    grad_out = dot_tn(attended_low, grad_attn)
    grad_attended = dot_nt(grad_attn, full_out).astype(BF16)
    grad_q, grad_k, grad_v, sums = attend_back(
        own, query, key, value, grad_attended, attended, lse, qseg, kseg, bias
    )
    grad_query = dot_tn(hidden_one, grad_q)
    grad_key = dot_tn(hidden_all, grad_k)
    grad_value = dot_tn(hidden_all, grad_v)
    grad_rows = dot_nt(grad_k, full_key) + dot_nt(grad_v, full_value)
    own_part = dot_nt(grad_q, full_query)
    first = lax.axis_index("blk") * tokens
    grad_rows = lax.dynamic_update_slice_in_dim(
        grad_rows, lax.dynamic_slice_in_dim(grad_rows, first, tokens, 0) + own_part, first, 0
    )
    grad_gain_one = jnp.sum(grad_rows * unit_all, axis=0)

    up_order = links.head_bits + [1] + [b for b in links.blk_bits if b > 1][::-1]
    blk_up = [1] + [b for b in links.blk_bits if b > 1][::-1]
    reduced_back = scatter_sum(links, grad_back, up_order, bits)
    reduced_mid = scatter_sum(links, jnp.concatenate([grad_out, grad_in, grad_proj], 1), up_order, bits)
    gain_grads = jnp.stack([grad_gain_one, grad_gain_two, grad_gain_three], 1)
    gain_grads = jnp.pad(gain_grads, ((0, 0), (0, TILE - 3)))
    reduced_qkv = scatter_sum(
        links, jnp.concatenate([grad_query, grad_key, grad_value, gain_grads], 1), up_order, bits
    )
    grad_hidden_one = scatter_sum(links, grad_rows, blk_up, links.blk_bits)
    input_gradient_rows = grad_one + norm_back(grad_hidden_one, gain_one, unit_one, scale_one)

    table = table_grad(sums, heads, rel_table.shape[0])
    for bit in bits:
        table = table + links.swap(table, bit)
    gain_grads = reduced_qkv[:, 3 * width :].T
    return outputs_of(
        states, input_gradient_rows, reduced_qkv, reduced_mid, reduced_back, gain_grads, table[:, :heads], width, ff
    )


X_BIT, CORE_BIT, Y_BIT = 16, 8, 1
NEAR_BIT, OVER_BIT = 2, 4
DEPTH = 4
PEERS = 32


def swap(value, mask, other_mask=None):
    masks = (mask, mask if other_mask is None else other_mask)
    return lax.ppermute(value, AXES, [(i, i ^ masks[(i // CORE_BIT) % 2]) for i in range(PEERS)])


def depth_mask(place, core):
    return (0, NEAR_BIT + core * (OVER_BIT - NEAR_BIT), OVER_BIT - core * (OVER_BIT - NEAR_BIT), NEAR_BIT | OVER_BIT)[place]


def side_masks(core):
    return Y_BIT + core * (X_BIT - Y_BIT), X_BIT - core * (X_BIT - Y_BIT)


def tied(value, *earlier):
    whole = functools.reduce(jnp.logical_and, [mark[(0,) * mark.ndim] == mark[(0,) * mark.ndim] for mark in earlier])
    return jnp.where(whole, value, jnp.zeros_like(value))


def gather_depth(own, first=None):
    first = swap(own, NEAR_BIT, OVER_BIT) if first is None else first
    pair = jnp.stack([own, first])
    return jnp.concatenate([pair, swap(pair, OVER_BIT, NEAR_BIT)], 0)


def gather_plane(column):
    half = jnp.concatenate([column, swap(column, Y_BIT, X_BIT)], 0)
    return half, swap(half, X_BIT, Y_BIT)


def y_pairs(half, rest):
    second = (lax.axis_index("head") % 2) == 1
    high = (lax.axis_index("blk") % 2) == 1
    pairs = (
        (half[:DEPTH], jnp.where(second, rest[:DEPTH], half[DEPTH:])),
        (jnp.where(second, half[DEPTH:], rest[:DEPTH]), rest[DEPTH:]),
    )
    return [
        jnp.where(high, jnp.concatenate([other, mine], 1), jnp.concatenate([mine, other], 1)) for mine, other in pairs
    ]


def gathered_items(core, paired):
    items = []
    for c in range(2):
        here = core if c == 0 else 1 - core
        first, second = side_masks(here)
        for b in range(2):
            for k in range(DEPTH):
                depth = depth_mask(k, here)
                if paired:
                    items.append((2 * c + b, k, (c * CORE_BIT + b * X_BIT) | depth))
                else:
                    items += [
                        (2 * c + b, a * DEPTH + k, (c * CORE_BIT) | (a * first) | (b * second) | depth) for a in range(2)
                    ]
    return items


def sent_items(core):
    items = []
    for c in range(2):
        here = core if c == 0 else 1 - core
        minor, major = side_masks(here)
        for a in range(2):
            for b in range(2):
                for k in range(DEPTH):
                    place = a * 2 * DEPTH + b * DEPTH + k
                    items.append((c, place, (c * CORE_BIT) | (a * major) | (b * minor) | depth_mask(k, here)))
    return items


def wide(value):
    return value.astype(F32)


def part_of(terms, first, last):
    return sum(wide(term[first:last]) for term in terms)


def next_sent(terms):
    half = terms[-1].shape[0] // 2
    return part_of(terms, half, 2 * half).astype(BF16)


def halved(terms, masks, sent=None):
    half = terms[-1].shape[0] // 2
    return [term[:half] for term in terms] + [swap(next_sent(terms) if sent is None else sent, *masks)]


FIRST_SIDE, SECOND_SIDE = (X_BIT, Y_BIT), (Y_BIT, X_BIT)
FIRST_DEPTH, SECOND_DEPTH = (OVER_BIT, NEAR_BIT), (NEAR_BIT, OVER_BIT)


ANY = pl.BlockSpec(memory_space=pl.ANY)
SMEM = pl.BlockSpec(memory_space=pltpu.SMEM)
WHOLE = pl.BlockSpec(memory_space=pltpu.VMEM)


def load_shards(parts, me, target, sems, rows, paired):
    copies = []
    rows = 2 * rows if paired else rows
    core = lax.rem(me // CORE_BIT, 2)
    for n, (buffer, place, relative) in enumerate(gathered_items(core, paired)):
        index = (me ^ relative) // 2 if paired else me ^ relative
        at = pl.multiple_of(index * rows, 16)
        copies.append(pltpu.make_async_copy(parts[buffer].at[place], target.at[pl.ds(at, rows), :], sems.at[n]))
    for copy in copies:
        copy.start()
    return copies


def store_blocks(source, me, targets, sems):
    copies = []
    for n, (side, place, relative) in enumerate(sent_items(lax.rem(me // CORE_BIT, 2))):
        copies.append(pltpu.make_async_copy(source.at[me ^ relative], targets[side].at[place], sems.at[n]))
    for copy in copies:
        copy.start()
    return copies


def put_blocks(target, lanes, value):
    rows = target.shape[1]
    for p in range(PEERS):
        target[p, :, lanes] = value[p * rows : (p + 1) * rows, :].astype(BF16)


def wait_all(copies):
    for copy in copies:
        copy.wait()


def project_kernel(me_ref, *refs, blocks, rows):
    xs = refs[:2]
    parts = refs[2:6]
    h_ref, k_ref, v_ref, q_ref, gains_ref, seg_ref, w_ref, sems = refs[-8:]
    me = me_ref[0]
    own = lax.rem(me, blocks)
    copies = load_shards(parts, me, w_ref, sems, rows, True)
    width = h_ref.shape[1]
    wait_all(copies)
    gains_ref[...] = wide(w_ref[:, 3 * width :]).T[:8]
    gain = gains_ref[0:1, :]
    core = lax.rem(me // CORE_BIT, 2)
    for r in range(blocks):
        x_ref = xs[r // 4].at[r % 4]
        unit, scale = normed(wide(x_ref[:TILE, :]))
        hidden = (unit * gain).astype(BF16)
        block = own ^ ((r & 1) * Y_BIT | depth_mask(r >> 1, core))
        at = pl.multiple_of(block * TILE, TILE)
        h_ref[pl.ds(at, TILE), :] = hidden
        seg_ref[pl.ds(block, 1), :] = wide(x_ref[TILE : TILE + 1, :TILE])
        if r == 0:
            q_ref[...] = dot(hidden, w_ref[:, :width]).astype(BF16)
    step = 512
    for start in range(0, h_ref.shape[0], step):
        at = slice(start, start + step)
        k_ref[at, :] = dot(h_ref[at, :], w_ref[:, width : 2 * width]).astype(BF16)
        v_ref[at, :] = dot(h_ref[at, :], w_ref[:, 2 * width : 3 * width]).astype(BF16)


GELU_C = math.sqrt(2.0 / math.pi)


def ffn_kernel(me_ref, att_ref, x_ref, cot_ref, gains_ref, *refs, ff):
    mid_parts, back_parts = refs[:4], refs[4:8]
    states_ref, one_ref, do_ref, gain_grads_ref, back_keep, back_send, mid_keep, mid_send = refs[8:16]
    mid_ref, back_ref, dmid_ref, dback_ref, mid_sems, back_sems, mid_out_sems, back_out_sems = refs[16:]
    me = me_ref[0]
    width = att_ref.shape[1]
    mid_rows = width // PEERS
    back_rows = ff // PEERS
    mid_copies = load_shards(mid_parts, me, mid_ref, mid_sems, mid_rows, True)
    back_copies = load_shards(back_parts, me, back_ref, back_sems, back_rows, False)
    gain_two = gains_ref[1:2, :]
    gain_three = gains_ref[2:3, :]
    w_out = slice(0, width)
    w_in = slice(width, width + ff)
    w_proj = slice(width + ff, mid_ref.shape[1])
    wait_all(mid_copies)
    resid_one = wide(x_ref[:TILE, :]) + dot(att_ref[...], mid_ref[:, w_out])
    unit_two, scale_two = normed(resid_one)
    hidden_two = (unit_two * gain_two).astype(BF16)
    up = dot(hidden_two, mid_ref[:, w_in])
    inner = GELU_C * (up + 0.044715 * (up * up * up))
    bent = jnp.tanh(inner)
    active = (0.5 * up * (1.0 + bent)).astype(BF16)
    slope = 0.5 * (1.0 + bent) + 0.5 * up * (1.0 - bent * bent) * (GELU_C * (1.0 + 3.0 * 0.044715 * (up * up)))
    wait_all(back_copies)
    resid_two = resid_one + dot(active, back_ref[...])
    unit_three, scale_three = normed(resid_two)
    final = (unit_three * gain_three).astype(BF16)
    states_ref[...] = dot(final, mid_ref[:, w_proj]).astype(BF16)
    grad_final = dot_nt(cot_ref[...], mid_ref[:, w_proj])
    grad_two = norm_back(grad_final, gain_three, unit_three, scale_three)
    branch = grad_two.astype(BF16)
    put_blocks(dback_ref, slice(None), dot_tn(active, branch))
    back_out = store_blocks(dback_ref, me, (back_keep, back_send), back_out_sems)
    grad_up = (dot_nt(branch, back_ref[...]) * slope).astype(BF16)
    grad_hidden = dot_nt(grad_up, mid_ref[:, w_in])
    grad_one = grad_two + norm_back(grad_hidden, gain_two, unit_two, scale_two)
    one_ref[...] = grad_one
    grad_attn = grad_one.astype(BF16)
    do_ref[...] = dot_nt(grad_attn, mid_ref[:, w_out]).astype(BF16)
    put_blocks(dmid_ref, w_out, dot_tn(att_ref[...], grad_attn))
    put_blocks(dmid_ref, w_in, dot_tn(hidden_two, grad_up))
    put_blocks(dmid_ref, w_proj, dot_tn(final, cot_ref[...]))
    mid_out = store_blocks(dmid_ref, me, (mid_keep, mid_send), mid_out_sems)
    gain_grads_ref[...] = jnp.zeros_like(gain_grads_ref)
    gain_grads_ref[1:2, :] = jnp.sum(grad_hidden * unit_two, axis=0, keepdims=True)
    gain_grads_ref[2:3, :] = jnp.sum(grad_final * unit_three, axis=0, keepdims=True)
    wait_all(back_out)
    wait_all(mid_out)


def rows_grad_kernel(me_ref, x_ref, rest_ref, *refs, blocks, rows):
    halves = [refs[3 * i : 3 * i + 3] for i in range(2)]
    parts = refs[6:10]
    *dh_refs, gain_grad_ref, w_ref, grad_ref, sems = refs[-6:]
    me = me_ref[0]
    own = lax.rem(me, blocks)
    width = grad_ref.shape[1]
    span = width // 2
    own_at = pl.ds(pl.multiple_of(own * TILE, TILE), TILE)
    wait_all(load_shards(parts, me, w_ref, sems, rows, True))
    for i, (dq_ref, dk_ref, dv_ref) in enumerate(halves):
        grad = dot_nt(dk_ref[...], w_ref[:, width + i * span : width + (i + 1) * span])
        grad = grad + dot_nt(dv_ref[...], w_ref[:, 2 * width + i * span : 2 * width + (i + 1) * span])
        grad_ref[...] = grad if i == 0 else grad_ref[...] + grad
        grad_ref[own_at, :] = grad_ref[own_at, :] + dot_nt(dq_ref[...], w_ref[:, i * span : (i + 1) * span])
    gain_grad = jnp.zeros((1, width), F32)
    core = lax.rem(me // CORE_BIT, 2)
    for r in range(blocks):
        block = own ^ ((r & 1) * Y_BIT | depth_mask(r >> 1, core))
        at = pl.ds(pl.multiple_of(block * TILE, TILE), TILE)
        grad = grad_ref[at, :]
        source = rest_ref if r // 4 else x_ref
        unit, scale = normed(wide(source[r % 4, :TILE, :]))
        gain_grad = gain_grad + jnp.sum(grad * unit, axis=0, keepdims=True)
        dh_refs[r & 1][r >> 1] = grad.astype(BF16)
    gain_grad_ref[...] = jnp.broadcast_to(gain_grad, gain_grad_ref.shape)


def qkv_grad_kernel(me_ref, h_ref, *refs, marks, blocks):
    halves = [refs[3 * i : 3 * i + 3] for i in range(2)]
    keep, send, dw_ref, out_sems = refs[6 + marks :]
    me = me_ref[0]
    own = lax.rem(me, blocks)
    width = h_ref.shape[1]
    span = width // 2
    own_at = pl.ds(pl.multiple_of(own * TILE, TILE), TILE)
    for i, (dq_ref, dk_ref, dv_ref) in enumerate(halves):
        put_blocks(dw_ref, slice(i * span, (i + 1) * span), dot_tn(h_ref[own_at, :], dq_ref[...]))
        put_blocks(dw_ref, slice(width + i * span, width + (i + 1) * span), dot_tn(h_ref[...], dk_ref[...]))
        put_blocks(dw_ref, slice(2 * width + i * span, 2 * width + (i + 1) * span), dot_tn(h_ref[...], dv_ref[...]))
    wait_all(store_blocks(dw_ref, me, (keep, send), out_sems))


def shaped(dims, kind):
    return jax.ShapeDtypeStruct(dims, kind)


def cube_body(inputs, segments, w_query, w_key, w_value, w_out, w_in, w_back, w_proj, gain_attn, gain_ffn, gain_final, rel_table, cotangent):
    blocks = lax.axis_size("blk")
    tokens, width = inputs.shape[1:]
    ff = w_in.shape[1]
    proj = w_proj.shape[1]
    heads = rel_table.shape[1]
    length = tokens * blocks
    rows = w_query.shape[0]
    back_rows = w_back.shape[0]
    own = lax.axis_index("blk").reshape(1).astype(jnp.int32)
    me = (lax.axis_index("head") * blocks + lax.axis_index("blk")).reshape(1).astype(jnp.int32)
    dma = pltpu.SemaphoreType.DMA((PEERS,))

    gains = jnp.stack([gain_attn, gain_ffn, gain_final], 1)
    gains = jnp.pad(gains, ((0, 0), (0, TILE - gains.shape[1])))
    pack_qkv = jnp.concatenate([w_query, w_key, w_value, gains], 1)
    pack_mid = jnp.concatenate([w_out, w_in, w_proj], 1)
    qkv_lanes = pack_qkv.shape[1]
    mid_lanes = pack_mid.shape[1]
    seg_row = jnp.pad(segments.astype(BF16), ((0, 7), (0, width - tokens)))
    own_x = jnp.concatenate([inputs[0], seg_row], 0)
    x_pair = jnp.stack([own_x, swap(own_x, Y_BIT)])
    qkv_first = swap(pack_qkv, NEAR_BIT, OVER_BIT)
    qkv_column = gather_depth(pack_qkv, qkv_first)
    x_half = jnp.concatenate([x_pair, swap(x_pair, NEAR_BIT, OVER_BIT)], 0)
    x_rest = swap(x_half, OVER_BIT, NEAR_BIT)
    qkv_parts = y_pairs(*gather_plane(qkv_column))
    qkv_parts = qkv_parts + [swap(part, CORE_BIT) for part in qkv_parts]
    pack_mid = tied(pack_mid, qkv_column)
    mid_first = swap(pack_mid, NEAR_BIT, OVER_BIT)
    mid_plane = gather_plane(gather_depth(pack_mid, mid_first))
    back_column = gather_depth(tied(w_back, mid_first))
    back_plane = gather_plane(back_column)
    hidden, key, value, query, gain_rows, kseg = pl.pallas_call(
        functools.partial(project_kernel, blocks=blocks, rows=rows),
        in_specs=[SMEM] + [WHOLE] * 2 + [ANY] * 6,
        out_specs=[WHOLE] * 6,
        out_shape=[
            shaped((length, width), BF16),
            shaped((length, width), BF16),
            shaped((length, width), BF16),
            shaped((tokens, width), BF16),
            shaped((8, width), F32),
            shaped((blocks, TILE), F32),
        ],
        scratch_shapes=[pltpu.VMEM((width, qkv_lanes), BF16), dma],
        compiler_params=pltpu.CompilerParams(vmem_limit_bytes=24 * MIB),
        cost_estimate=pl.CostEstimate(flops=2 * length * width * 2 * width, transcendentals=0, bytes_accessed=30 << 20),
        name="project",
    )(me, x_half, x_rest, *qkv_parts, mid_plane[0], back_column)
    bias = bias_rows(rel_table)
    attend, _ = attention_calls(length, width, heads, marks=1)
    qseg = segments.reshape(tokens, 1).astype(F32)
    attended, attended_low, lse = attend(own, query, key, value, qseg, kseg, bias, back_plane[0])
    mid_parts = y_pairs(*(tied(part, attended_low) for part in mid_plane))
    mid_parts = mid_parts + [swap(part, CORE_BIT) for part in mid_parts]
    back_parts = [*back_plane, *(swap(part, CORE_BIT) for part in back_plane)]
    states, grad_one, grad_attended, gain_grads, back_keep, back_send, mid_keep, mid_send = pl.pallas_call(
        functools.partial(ffn_kernel, ff=ff),
        in_specs=[SMEM] + [WHOLE] * 4 + [ANY] * 8,
        out_specs=[WHOLE] * 4 + [ANY] * 4,
        out_shape=[
            shaped((tokens, proj), BF16),
            shaped((tokens, width), F32),
            shaped((tokens, width), BF16),
            shaped((8, width), F32),
            shaped((PEERS // 2, back_rows, width), BF16),
            shaped((PEERS // 2, back_rows, width), BF16),
            shaped((PEERS // 2, rows, mid_lanes), BF16),
            shaped((PEERS // 2, rows, mid_lanes), BF16),
        ],
        scratch_shapes=[
            pltpu.VMEM((width, mid_lanes), BF16),
            pltpu.VMEM((ff, width), BF16),
            pltpu.VMEM((PEERS, rows, mid_lanes), BF16),
            pltpu.VMEM((PEERS, back_rows, width), BF16),
            dma,
            dma,
            dma,
            dma,
        ],
        compiler_params=pltpu.CompilerParams(vmem_limit_bytes=56 * MIB),
        cost_estimate=pl.CostEstimate(flops=6 * 2 * tokens * width * (ff + width), transcendentals=0, bytes_accessed=70 << 20),
        name="ffn",
    )(me, attended_low, own_x, cotangent[0], gain_rows, *mid_parts, *back_parts)
    back_terms = [back_keep, swap(back_send, CORE_BIT)]
    mid_terms = [mid_keep, swap(mid_send, CORE_BIT)]
    common = (own, query, key, value, grad_attended, attended, lse, qseg, kseg, bias)
    _, attend_back = attention_calls(length, width, heads, 0, heads // 4)
    *first_grads, first_sums = attend_back(*common)
    back_sent, mid_sent = next_sent(back_terms), next_sent(mid_terms)
    _, attend_back = attention_calls(length, width, heads, heads // 4, heads // 4, marks=2)
    *second_grads, second_sums = attend_back(*common, back_sent, mid_sent)
    back_terms = halved(back_terms, FIRST_SIDE, back_sent)
    mid_terms = halved(mid_terms, FIRST_SIDE, mid_sent)
    back_sent = next_sent(back_terms)
    grad_parts = (*first_grads, *second_grads)
    lanes = 3 * width
    qkv_keep, qkv_send = pl.pallas_call(
        functools.partial(qkv_grad_kernel, marks=1, blocks=blocks),
        in_specs=[SMEM] + [WHOLE] * 7 + [ANY],
        out_specs=[ANY, ANY],
        out_shape=[shaped((PEERS // 2, rows, lanes), BF16), shaped((PEERS // 2, rows, lanes), BF16)],
        scratch_shapes=[pltpu.VMEM((PEERS, rows, lanes), BF16), dma],
        compiler_params=pltpu.CompilerParams(vmem_limit_bytes=26 * MIB),
        cost_estimate=pl.CostEstimate(flops=2 * 2 * length * width * width, transcendentals=0, bytes_accessed=30 << 20),
        name="qkv_grad",
    )(me, hidden, *grad_parts, back_sent)
    back_terms = halved(back_terms, SECOND_SIDE, back_sent)
    back_sent = next_sent(back_terms)
    qkv_terms = [qkv_keep, swap(qkv_send, CORE_BIT)]
    mid_sent = tied(next_sent(mid_terms), qkv_keep)
    qkv_sent = next_sent(qkv_terms)
    rows_keep, rows_send, gain_grad = pl.pallas_call(
        functools.partial(rows_grad_kernel, blocks=blocks, rows=rows),
        in_specs=[SMEM] + [WHOLE] * 8 + [ANY] * 7,
        out_specs=[WHOLE] * 3,
        out_shape=[shaped((blocks // 2, tokens, width), BF16)] * 2 + [shaped((8, width), F32)],
        scratch_shapes=[pltpu.VMEM((width, qkv_lanes), BF16), pltpu.VMEM((length, width), F32), dma],
        compiler_params=pltpu.CompilerParams(vmem_limit_bytes=30 * MIB),
        cost_estimate=pl.CostEstimate(flops=2 * 2 * length * width * width, transcendentals=0, bytes_accessed=30 << 20),
        name="rows_grad",
    )(me, x_half, x_rest, *grad_parts, *qkv_parts, back_sent, mid_sent, qkv_sent)
    qkv_terms = halved(qkv_terms, FIRST_SIDE, qkv_sent)
    mid_terms = halved(mid_terms, SECOND_SIDE, mid_sent)
    row_terms = [rows_keep, swap(rows_send, Y_BIT)]
    back_terms = halved(back_terms, FIRST_DEPTH, back_sent)
    mid_terms = halved(mid_terms, FIRST_DEPTH)
    qkv_sent = next_sent(qkv_terms)
    qkv_terms = halved(qkv_terms, SECOND_SIDE, qkv_sent)
    row_terms = halved(row_terms, FIRST_DEPTH, tied(next_sent(row_terms), qkv_sent))
    back_terms = halved(back_terms, SECOND_DEPTH, tied(next_sent(back_terms), qkv_sent))
    mid_terms = halved(mid_terms, SECOND_DEPTH, tied(next_sent(mid_terms), qkv_sent))
    qkv_sent = next_sent(qkv_terms)
    after_sides = qkv_sent
    qkv_terms = halved(qkv_terms, FIRST_DEPTH, qkv_sent)
    row_terms = halved(row_terms, SECOND_DEPTH)
    qkv_terms = halved(qkv_terms, SECOND_DEPTH)
    reduced_back, reduced_mid, reduced_qkv, grad_hidden = (
        part_of(terms, 0, 1)[0] for terms in (back_terms, mid_terms, qkv_terms, row_terms)
    )
    sums = jnp.concatenate([first_sums, second_sums], 0)
    unit, scale = normed(wide(inputs[0]))
    input_gradient_rows = grad_one + norm_back(grad_hidden, gain_rows[0], unit, scale)
    buckets = rel_table.shape[0]
    table = table_grad(sums, heads, buckets)[:, :heads].reshape(1, -1, TILE)
    gain_grads = jnp.stack([gain_grad[0], gain_grads[1], gain_grads[2]]).reshape(3, PEERS, rows)
    gain_grads = jnp.pad(gain_grads.transpose(1, 0, 2), ((0, 0), (0, 8 - 3 - table.shape[1]), (0, TILE - rows)))
    small = jnp.concatenate([jnp.broadcast_to(table, (PEERS,) + table.shape[1:]), gain_grads], 1)
    small = tied(small, after_sides)
    small = jnp.sum(lax.all_to_all(small, AXES, 0, 0), axis=0)
    first = table.shape[1]
    table = small[:first].reshape(buckets, heads)
    return outputs_of(
        states, input_gradient_rows, reduced_qkv, reduced_mid, reduced_back, small[first : first + 3, :rows], table, width, ff
    )


def body(*args):
    cube = lax.axis_size("head") == 4 and lax.axis_size("blk") == 8
    return (cube_body if cube else general_body)(*args)


def solution(mesh):
    rows = P(("head", "blk"), None)
    line = P(("head", "blk"))
    tokens = P("head", "blk", None)
    in_specs = (tokens, P("head", "blk")) + (rows,) * 7 + (line,) * 3 + (P(), tokens)
    out_specs = (tokens, tokens) + (rows,) * 7 + (line,) * 3 + (P(),)
    return jax.shard_map(body, mesh=mesh, in_specs=in_specs, out_specs=out_specs, check_vma=False)
```

```python
import functools
import math

import jax
import jax.numpy as jnp
import numpy as np
from jax import lax
from jax.experimental import pallas as pl
from jax.experimental.pallas import tpu as pltpu
from jax.sharding import PartitionSpec as P

BORDERS = (12, 16, 23, 32, 46, 64, 91)
MASKED = -1e30
EPS = 1e-6
TILE = 128
WIN = 512
BF16 = jnp.bfloat16
F32 = jnp.float32
AXES = ("head", "blk")
MIB = 1024 * 1024


def bucket_np(offset):
    distance = np.abs(offset)
    beyond = 8 + sum((distance >= border).astype(np.int64) for border in BORDERS)
    within = np.minimum(np.where(distance < 8, distance, beyond), 15)
    return within + 16 * (offset > 0)


def window_offsets():
    k = np.arange(WIN)
    return np.where(k < WIN - TILE, k - TILE, k - WIN - TILE)


def dot(a, b):
    return jnp.dot(a, b, preferred_element_type=F32)


def dot_nt(a, b):
    return lax.dot_general(a, b, (((1,), (1,)), ((), ())), preferred_element_type=F32)


def dot_tn(a, b):
    return lax.dot_general(a, b, (((0,), (0,)), ((), ())), preferred_element_type=F32)


class Links:
    def __init__(self):
        self.blocks = lax.axis_size("blk")
        self.total = lax.axis_size("head") * self.blocks
        self.me = lax.axis_index("head") * self.blocks + lax.axis_index("blk")
        self.bits = [1 << k for k in range(int(math.log2(self.total)))]
        self.blk_bits = [bit for bit in self.bits if bit < self.blocks]
        self.head_bits = [bit for bit in self.bits if bit >= self.blocks]

    def swap(self, value, bit):
        return lax.ppermute(value, AXES, [(i, i ^ bit) for i in range(self.total)])

    def mine(self, bit):
        return (self.me & bit) != 0


def gather_rows(links, shard, order, all_bits):
    high_first = sorted(all_bits, reverse=True)
    value = shard.reshape((1,) * len(high_first) + shard.shape)
    for bit in order:
        axis = high_first.index(bit)
        other = links.swap(value, bit)
        value = jnp.where(
            links.mine(bit),
            jnp.concatenate([other, value], axis),
            jnp.concatenate([value, other], axis),
        )
    return value.reshape((-1,) + shard.shape[1:])


def scatter_sum(links, whole, order, all_bits):
    high_first = sorted(all_bits, reverse=True)
    count = len(high_first)
    rows = whole.shape[0] >> count
    value = whole.reshape((2,) * count + (rows,) + whole.shape[1:])
    for bit in order:
        axis = high_first.index(bit)
        side = links.mine(bit).astype(jnp.int32)
        sent = lax.dynamic_slice_in_dim(value, 1 - side, 1, axis).astype(BF16)
        kept = lax.dynamic_slice_in_dim(value, side, 1, axis)
        value = kept.astype(F32) + links.swap(sent, bit).astype(F32)
    return value.reshape((rows,) + whole.shape[1:])


def bias_tiles(bias_ref, tiles_ref, head_row, side):
    row = bias_ref[pl.ds(head_row, 1), :]
    near = pltpu.roll(jnp.broadcast_to(row[:, :WIN], (TILE, WIN)), 0, 1, stride=1, stride_axis=0)
    rows = pl.ds(side * TILE, TILE)
    tiles_ref[0, rows, :] = jnp.broadcast_to(row[:, WIN : WIN + 1], (TILE, TILE))
    for t in range(3):
        tiles_ref[1 + t, rows, :] = near[:, t * TILE : (t + 1) * TILE]
    tiles_ref[4, rows, :] = jnp.broadcast_to(row[:, WIN + 1 : WIN + 2], (TILE, TILE))


def stacked(pair):
    lane = lax.broadcasted_iota(jnp.int32, pair.shape, 1)
    zero = jnp.zeros_like(pair)
    half = pair.shape[1] // 2
    return jnp.concatenate([jnp.where(lane < half, pair, zero), jnp.where(lane < half, zero, pair)], 0)


def unstacked(both):
    rows = both.shape[0] // 2
    lane = lax.broadcasted_iota(jnp.int32, (rows, both.shape[1]), 1)
    return jnp.where(lane < both.shape[1] // 2, both[:rows], both[rows:])


def tile_kind(key_tile, own_tile):
    return jnp.clip(key_tile - own_tile, -2, 2) + 2


def scores_into(chunk, chunk_tiles, own, q2, k_ref, qseg, kseg_ref, tiles_ref, s_ref):
    base = chunk * chunk_tiles * TILE
    raw = dot_nt(q2, k_ref[pl.ds(base, chunk_tiles * TILE), :])
    parts = []
    for t in range(chunk_tiles):
        at = base + t * TILE
        near = tiles_ref[tile_kind(chunk * chunk_tiles + t, own)]
        allowed = qseg == kseg_ref[pl.ds(chunk * chunk_tiles + t, 1), :]
        tile = jnp.where(allowed, raw[:, t * TILE : (t + 1) * TILE] + near, MASKED)
        s_ref[:, pl.ds(at, TILE)] = tile
        parts.append(tile)
    return parts


def attend_kernel(own_ref, q_ref, k_ref, v_ref, qseg_ref, kseg_ref, bias_ref, *refs, marks, chunks, chunk_tiles):
    o_ref, low_ref, lse_ref, tiles_ref, s_ref = refs[marks:]
    pair = pl.program_id(0)
    own = own_ref[0]
    for side in range(2):
        bias_tiles(bias_ref, tiles_ref, pair * 2 + side, side)
    q2 = stacked(q_ref[...])
    qseg = jnp.concatenate([qseg_ref[...], qseg_ref[...]], 0)

    def first(chunk, high):
        parts = scores_into(chunk, chunk_tiles, own, q2, k_ref, qseg, kseg_ref, tiles_ref, s_ref)
        return functools.reduce(jnp.maximum, parts, high)

    def second(chunk, total):
        for t in range(chunk_tiles):
            at = pl.ds((chunk * chunk_tiles + t) * TILE, TILE)
            powers = jnp.exp(s_ref[:, at] - high)
            s_ref[:, at] = powers
            total = total + powers
        return total

    def third(chunk, acc):
        base = chunk * chunk_tiles * TILE
        at = pl.ds(base, chunk_tiles * TILE)
        low = (s_ref[:, at] * inverse).astype(BF16)
        return acc + dot(low, v_ref[at, :])

    def loop(body, start):
        return body(0, start) if chunks == 1 else lax.fori_loop(0, chunks, body, start)

    high = loop(first, jnp.full((2 * TILE, TILE), MASKED, F32))
    high = jnp.max(high, axis=1, keepdims=True)
    total = jnp.sum(loop(second, jnp.zeros((2 * TILE, TILE), F32)), axis=1, keepdims=True)
    inverse = 1.0 / total
    out = unstacked(loop(third, jnp.zeros((2 * TILE, TILE), F32)))
    o_ref[...] = out
    low_ref[...] = out.astype(BF16)
    lse_ref[...] = jnp.broadcast_to(high + jnp.log(total), (2 * TILE, TILE))


def attend_back_kernel(own_ref, q_ref, k_ref, v_ref, do_ref, o_ref, lse_ref, qseg_ref, kseg_ref, bias_ref, *refs, first, marks, chunks, chunk_tiles):
    dq_ref, dk_ref, dv_ref, sums_ref, tiles_ref, s_ref, near_ref = refs[marks:]
    pair = pl.program_id(0) + first
    own = own_ref[0]
    for side in range(2):
        bias_tiles(bias_ref, tiles_ref, pair * 2 + side, side)
    q2 = stacked(q_ref[...])
    do2 = stacked(do_ref[...])
    delta = jnp.sum(stacked(do_ref[...].astype(F32) * o_ref[...]), axis=1, keepdims=True)
    lse = lse_ref[:, :1]
    qseg = jnp.concatenate([qseg_ref[...], qseg_ref[...]], 0)
    near_ref[...] = jnp.zeros_like(near_ref)

    def step(chunk, carried):
        acc, left, right = carried
        base = chunk * chunk_tiles * TILE
        at = pl.ds(base, chunk_tiles * TILE)
        scores_into(chunk, chunk_tiles, own, q2, k_ref, qseg, kseg_ref, tiles_ref, s_ref)
        probs = jnp.exp(s_ref[:, at] - lse)
        grad_probs = dot_nt(do2, v_ref[at, :])
        grads = (probs * (grad_probs - delta)).astype(BF16)
        acc = acc + dot(grads, k_ref[at, :])
        dk_ref[at, :] = dot_tn(grads, q2).astype(BF16)
        dv_ref[at, :] = dot_tn(probs.astype(BF16), do2).astype(BF16)
        wide = grads.astype(F32)
        for t in range(chunk_tiles):
            gap = chunk * chunk_tiles + t - own
            tile = wide[:, t * TILE : (t + 1) * TILE]
            left = left + jnp.where(gap < -1, tile, 0.0)
            right = right + jnp.where(gap > 1, tile, 0.0)

            @pl.when(jnp.abs(gap) <= 1)
            def _():
                near_ref[jnp.clip(gap + 1, 0, 2)] = tile

        return acc, left, right

    zero = jnp.zeros((2 * TILE, TILE), F32)
    start = (zero, zero, zero)
    acc, left, right = step(0, start) if chunks == 1 else lax.fori_loop(0, chunks, step, start)
    dq_ref[...] = unstacked(acc).astype(BF16)
    flip = (
        lax.broadcasted_iota(jnp.int32, (TILE, TILE), 0) + lax.broadcasted_iota(jnp.int32, (TILE, TILE), 1) == TILE - 1
    ).astype(BF16)
    for side in range(2):
        rows = slice(side * TILE, (side + 1) * TILE)
        window = jnp.concatenate([near_ref[t, rows, :] for t in range(4)], 1).astype(BF16)
        turned = pltpu.roll(dot(flip, window), 0, 1, stride=1, stride_axis=0)
        near_sum = jnp.sum(turned, axis=0, keepdims=True)
        far = [jnp.sum(jnp.sum(part[rows], axis=0, keepdims=True), axis=1, keepdims=True) for part in (left, right)]
        sums_ref[0, side : side + 1, :WIN] = near_sum
        lane = lax.broadcasted_iota(jnp.int32, (1, TILE), 1)
        sums_ref[0, side : side + 1, WIN:] = jnp.where(lane == 0, far[0], jnp.where(lane == 1, far[1], 0.0))


def attention_calls(length, width, heads, first=0, pairs=None, marks=0):
    total = heads // 2
    pairs = pairs or total
    tiles = length // TILE
    chunk_tiles = min(8, tiles)
    chunks = tiles // chunk_tiles
    wide = WIN + TILE
    lanes = width // total
    any_spec = pl.BlockSpec(memory_space=pl.ANY)
    own_spec = pl.BlockSpec(memory_space=pltpu.SMEM)
    q_spec = pl.BlockSpec((TILE, lanes), lambda p: (0, p + first))
    k_spec = pl.BlockSpec((length, lanes), lambda p: (0, p + first))
    dq_spec = pl.BlockSpec((TILE, lanes), lambda p: (0, p))
    dk_spec = pl.BlockSpec((length, lanes), lambda p: (0, p))
    qseg_spec = pl.BlockSpec((TILE, 1), lambda p: (0, 0))
    kseg_spec = pl.BlockSpec((tiles, TILE), lambda p: (0, 0))
    bias_spec = pl.BlockSpec((heads, wide), lambda p: (0, 0))
    lse_spec = pl.BlockSpec((2 * TILE, TILE), lambda p: (p + first, 0))
    sums_spec = pl.BlockSpec((1, 2, wide), lambda p: (p, 0, 0))
    scratch = [pltpu.VMEM((5, 2 * TILE, TILE), F32), pltpu.VMEM((2 * TILE, length), F32)]
    params = pltpu.CompilerParams(vmem_limit_bytes=(14 + length // 256) * MIB)

    def shape(dims, kind):
        return jax.ShapeDtypeStruct(dims, kind)

    forward = pl.pallas_call(
        functools.partial(attend_kernel, marks=marks, chunks=chunks, chunk_tiles=chunk_tiles),
        grid=(pairs,),
        in_specs=[own_spec, q_spec, k_spec, k_spec, qseg_spec, kseg_spec, bias_spec] + [any_spec] * marks,
        out_specs=[q_spec, q_spec, lse_spec],
        out_shape=[shape((TILE, width), F32), shape((TILE, width), BF16), shape((pairs * 2 * TILE, TILE), F32)],
        scratch_shapes=scratch,
        compiler_params=params,
        cost_estimate=pl.CostEstimate(flops=0, transcendentals=0, bytes_accessed=30 << 20),
        name="attend",
    )
    backward = pl.pallas_call(
        functools.partial(attend_back_kernel, first=first, marks=marks, chunks=chunks, chunk_tiles=chunk_tiles),
        grid=(pairs,),
        in_specs=[own_spec, q_spec, k_spec, k_spec, q_spec, q_spec, lse_spec, qseg_spec, kseg_spec, bias_spec]
        + [any_spec] * marks,
        out_specs=[dq_spec, dk_spec, dk_spec, sums_spec],
        out_shape=[
            shape((TILE, pairs * lanes), BF16),
            shape((length, pairs * lanes), BF16),
            shape((length, pairs * lanes), BF16),
            shape((pairs, 2, wide), F32),
        ],
        scratch_shapes=scratch + [pltpu.VMEM((4, 2 * TILE, TILE), F32)],
        compiler_params=params,
        cost_estimate=pl.CostEstimate(flops=0, transcendentals=0, bytes_accessed=48 << 20),
        name="attend_back",
    )
    return forward, backward


def normed(rows):
    scale = lax.rsqrt(jnp.mean(rows * rows, axis=-1, keepdims=True) + EPS)
    return rows * scale, scale


def norm_back(grad, gain, unit, scale):
    scaled = grad * gain
    return (scaled - unit * jnp.mean(scaled * unit, axis=-1, keepdims=True)) * scale


def bias_rows(rel_table):
    onehot = np.zeros((WIN + TILE, rel_table.shape[0]), np.float32)
    onehot[np.arange(WIN), bucket_np(window_offsets())] = 1.0
    onehot[WIN, 15] = 1.0
    onehot[WIN + 1, 31] = 1.0
    return lax.dot_general(
        rel_table, jnp.asarray(onehot, BF16), (((0,), (1,)), ((), ())), preferred_element_type=F32
    )


def table_grad(sums, heads, buckets):
    lane = np.arange(WIN)
    diagonal = np.zeros((WIN + TILE, buckets), np.float32)
    diagonal[lane, bucket_np(lane - (2 * TILE - 1))] = 1.0
    diagonal[WIN, 15] = 1.0
    diagonal[WIN + 1, 31] = 1.0
    table = lax.dot_general(
        jnp.asarray(diagonal),
        sums.reshape(heads, WIN + TILE),
        (((0,), (1,)), ((), ())),
        precision=lax.Precision.HIGHEST,
    )
    return jnp.pad(table, ((0, 0), (0, TILE - heads)))


def outputs_of(states, input_gradient_rows, reduced_qkv, reduced_mid, reduced_back, gain_grads, table, width, ff):
    return (
        states[None],
        input_gradient_rows[None],
        reduced_qkv[:, :width],
        reduced_qkv[:, width : 2 * width],
        reduced_qkv[:, 2 * width : 3 * width],
        reduced_mid[:, :width],
        reduced_mid[:, width : width + ff],
        reduced_back,
        reduced_mid[:, width + ff :],
        gain_grads[0],
        gain_grads[1],
        gain_grads[2],
        table,
    )


def general_body(inputs, segments, w_query, w_key, w_value, w_out, w_in, w_back, w_proj, gain_attn, gain_ffn, gain_final, rel_table, cotangent):
    links = Links()
    bits = links.bits
    tokens, width = inputs.shape[1:]
    ff = w_in.shape[1]
    proj = w_proj.shape[1]
    buckets, heads = rel_table.shape
    length = tokens * links.blocks
    rows = w_query.shape[0]
    own = lax.axis_index("blk").reshape(1).astype(jnp.int32)

    gains = jnp.stack([gain_attn, gain_ffn, gain_final], 1)
    gains = jnp.pad(gains, ((0, 0), (0, TILE - gains.shape[1])))
    pack_qkv = jnp.concatenate([w_query, w_key, w_value, gains], 1)
    pack_mid = jnp.concatenate([w_out, w_in, w_proj], 1)
    blk_down = [b for b in links.blk_bits if b > 1] + [1]
    order_a = blk_down + links.head_bits[::-1]
    own_rows = inputs[0]
    all_rows = gather_rows(links, own_rows, blk_down, links.blk_bits)
    seg_all = gather_rows(links, segments, blk_down, links.blk_bits)
    full_qkv = gather_rows(links, pack_qkv, order_a, bits)
    full_mid = gather_rows(links, pack_mid, order_a, bits)
    full_back = gather_rows(links, w_back, order_a, bits)
    full_query, full_key, full_value = (full_qkv[:, i * width : (i + 1) * width] for i in range(3))
    gain_rows = full_qkv[:, 3 * width :].astype(F32).T
    gain_one, gain_two, gain_three = gain_rows[0], gain_rows[1], gain_rows[2]
    full_out = full_mid[:, :width]
    full_in = full_mid[:, width : width + ff]
    full_proj = full_mid[:, width + ff :]

    bias = bias_rows(rel_table)

    states_in = own_rows.astype(F32)
    unit_all, scale_all = normed(all_rows.astype(F32))
    hidden_all = (unit_all * gain_one).astype(BF16)
    unit_one, scale_one = normed(states_in)
    hidden_one = (unit_one * gain_one).astype(BF16)
    query = dot(hidden_one, full_query).astype(BF16)
    key = dot(hidden_all, full_key).astype(BF16)
    value = dot(hidden_all, full_value).astype(BF16)
    attend, attend_back = attention_calls(length, width, heads)
    qseg = segments.reshape(tokens, 1)
    kseg = seg_all
    attended, attended_low, lse = attend(own, query, key, value, qseg, kseg, bias)
    resid_one = states_in + dot(attended_low, full_out)
    unit_two, scale_two = normed(resid_one)
    hidden_two = (unit_two * gain_two).astype(BF16)
    upward = dot(hidden_two, full_in)
    active, back_gelu = jax.vjp(lambda u: jax.nn.gelu(u, approximate=True), upward)
    active_low = active.astype(BF16)
    resid_two = resid_one + dot(active_low, full_back)
    unit_three, scale_three = normed(resid_two)
    final_low = (unit_three * gain_three).astype(BF16)
    states = dot(final_low, full_proj).astype(BF16)

    arriving = cotangent[0]
    grad_proj = dot_tn(final_low, arriving)
    grad_final = dot_nt(arriving, full_proj)
    grad_gain_three = jnp.sum(grad_final * unit_three, axis=0)
    grad_two = norm_back(grad_final, gain_three, unit_three, scale_three)
    grad_branch = grad_two.astype(BF16)
    grad_back = dot_tn(active_low, grad_branch)
    grad_up = back_gelu(dot_nt(grad_branch, full_back))[0].astype(BF16)
    grad_in = dot_tn(hidden_two, grad_up)
    grad_hidden_two = dot_nt(grad_up, full_in)
    grad_gain_two = jnp.sum(grad_hidden_two * unit_two, axis=0)
    grad_one = grad_two + norm_back(grad_hidden_two, gain_two, unit_two, scale_two)
    grad_attn = grad_one.astype(BF16)
    grad_out = dot_tn(attended_low, grad_attn)
    grad_attended = dot_nt(grad_attn, full_out).astype(BF16)
    grad_q, grad_k, grad_v, sums = attend_back(
        own, query, key, value, grad_attended, attended, lse, qseg, kseg, bias
    )
    grad_query = dot_tn(hidden_one, grad_q)
    grad_key = dot_tn(hidden_all, grad_k)
    grad_value = dot_tn(hidden_all, grad_v)
    grad_rows = dot_nt(grad_k, full_key) + dot_nt(grad_v, full_value)
    own_part = dot_nt(grad_q, full_query)
    first = lax.axis_index("blk") * tokens
    grad_rows = lax.dynamic_update_slice_in_dim(
        grad_rows, lax.dynamic_slice_in_dim(grad_rows, first, tokens, 0) + own_part, first, 0
    )
    grad_gain_one = jnp.sum(grad_rows * unit_all, axis=0)

    up_order = links.head_bits + [1] + [b for b in links.blk_bits if b > 1][::-1]
    blk_up = [1] + [b for b in links.blk_bits if b > 1][::-1]
    reduced_back = scatter_sum(links, grad_back, up_order, bits)
    reduced_mid = scatter_sum(links, jnp.concatenate([grad_out, grad_in, grad_proj], 1), up_order, bits)
    gain_grads = jnp.stack([grad_gain_one, grad_gain_two, grad_gain_three], 1)
    gain_grads = jnp.pad(gain_grads, ((0, 0), (0, TILE - 3)))
    reduced_qkv = scatter_sum(
        links, jnp.concatenate([grad_query, grad_key, grad_value, gain_grads], 1), up_order, bits
    )
    grad_hidden_one = scatter_sum(links, grad_rows, blk_up, links.blk_bits)
    input_gradient_rows = grad_one + norm_back(grad_hidden_one, gain_one, unit_one, scale_one)

    table = table_grad(sums, heads, rel_table.shape[0])
    for bit in bits:
        table = table + links.swap(table, bit)
    gain_grads = reduced_qkv[:, 3 * width :].T
    return outputs_of(
        states, input_gradient_rows, reduced_qkv, reduced_mid, reduced_back, gain_grads, table[:, :heads], width, ff
    )


X_BIT, CORE_BIT, Y_BIT = 16, 8, 1
NEAR_BIT, OVER_BIT = 2, 4
DEPTH = 4
PEERS = 32


def swap(value, mask, other_mask=None):
    masks = (mask, mask if other_mask is None else other_mask)
    return lax.ppermute(value, AXES, [(i, i ^ masks[(i // CORE_BIT) % 2]) for i in range(PEERS)])


def depth_mask(place, core):
    return (0, NEAR_BIT + core * (OVER_BIT - NEAR_BIT), OVER_BIT - core * (OVER_BIT - NEAR_BIT), NEAR_BIT | OVER_BIT)[place]


def side_masks(core):
    return Y_BIT + core * (X_BIT - Y_BIT), X_BIT - core * (X_BIT - Y_BIT)


def tied(value, *earlier):
    whole = functools.reduce(jnp.logical_and, [mark[(0,) * mark.ndim] == mark[(0,) * mark.ndim] for mark in earlier])
    return jnp.where(whole, value, jnp.zeros_like(value))


def gather_depth(own, first=None):
    first = swap(own, NEAR_BIT, OVER_BIT) if first is None else first
    pair = jnp.stack([own, first])
    return jnp.concatenate([pair, swap(pair, OVER_BIT, NEAR_BIT)], 0)


def gather_plane(column):
    half = jnp.concatenate([column, swap(column, Y_BIT, X_BIT)], 0)
    return half, swap(half, X_BIT, Y_BIT)


def y_pairs(half, rest):
    second = (lax.axis_index("head") % 2) == 1
    high = (lax.axis_index("blk") % 2) == 1
    pairs = (
        (half[:DEPTH], jnp.where(second, rest[:DEPTH], half[DEPTH:])),
        (jnp.where(second, half[DEPTH:], rest[:DEPTH]), rest[DEPTH:]),
    )
    return [
        jnp.where(high, jnp.concatenate([other, mine], 1), jnp.concatenate([mine, other], 1)) for mine, other in pairs
    ]


def gathered_items(core, paired):
    items = []
    for c in range(2):
        here = core if c == 0 else 1 - core
        first, second = side_masks(here)
        for b in range(2):
            for k in range(DEPTH):
                depth = depth_mask(k, here)
                if paired:
                    items.append((2 * c + b, k, (c * CORE_BIT + b * X_BIT) | depth))
                else:
                    items += [
                        (2 * c + b, a * DEPTH + k, (c * CORE_BIT) | (a * first) | (b * second) | depth) for a in range(2)
                    ]
    return items


def sent_items(core):
    items = []
    for c in range(2):
        here = core if c == 0 else 1 - core
        minor, major = side_masks(here)
        for a in range(2):
            for b in range(2):
                for k in range(DEPTH):
                    place = a * 2 * DEPTH + b * DEPTH + k
                    items.append((c, place, (c * CORE_BIT) | (a * major) | (b * minor) | depth_mask(k, here)))
    return items


def wide(value):
    return value.astype(F32)


def part_of(terms, first, last):
    return sum(wide(term[first:last]) for term in terms)


def next_sent(terms):
    half = terms[-1].shape[0] // 2
    return part_of(terms, half, 2 * half).astype(BF16)


def halved(terms, masks, sent=None):
    half = terms[-1].shape[0] // 2
    return [term[:half] for term in terms] + [swap(next_sent(terms) if sent is None else sent, *masks)]


FIRST_SIDE, SECOND_SIDE = (X_BIT, Y_BIT), (Y_BIT, X_BIT)
FIRST_DEPTH, SECOND_DEPTH = (OVER_BIT, NEAR_BIT), (NEAR_BIT, OVER_BIT)


ANY = pl.BlockSpec(memory_space=pl.ANY)
SMEM = pl.BlockSpec(memory_space=pltpu.SMEM)
WHOLE = pl.BlockSpec(memory_space=pltpu.VMEM)


def load_shards(parts, me, target, sems, rows, paired, lanes=None, first=0):
    copies = []
    rows = 2 * rows if paired else rows
    core = lax.rem(me // CORE_BIT, 2)
    for n, (buffer, place, relative) in enumerate(gathered_items(core, paired)):
        index = (me ^ relative) // 2 if paired else me ^ relative
        at = pl.multiple_of(index * rows, 16)
        part, span = parts[buffer].at[place], target.at[pl.ds(at, rows), :]
        if lanes is not None:
            part, span = part.at[:, lanes], target.at[pl.ds(at, rows), lanes]
        copies.append(pltpu.make_async_copy(part, span, sems.at[first + n]))
    for copy in copies:
        copy.start()
    return copies


def store_blocks(source, me, targets, sems, lanes=None):
    copies = []
    for n, (side, place, relative) in enumerate(sent_items(lax.rem(me // CORE_BIT, 2))):
        block, target = source.at[me ^ relative], targets[side].at[place]
        if lanes is not None:
            block, target = block.at[:, lanes], target.at[:, lanes]
        copies.append(pltpu.make_async_copy(block, target, sems.at[n]))
    for copy in copies:
        copy.start()
    return copies


def put_blocks(target, lanes, value):
    rows = target.shape[1]
    for p in range(PEERS):
        target[p, :, lanes] = value[p * rows : (p + 1) * rows, :].astype(BF16)


def wait_all(copies):
    for copy in copies:
        copy.wait()


def project_kernel(me_ref, *refs, blocks, rows):
    xs = refs[:2]
    parts = refs[2:6]
    h_ref, k_ref, v_ref, q_ref, gains_ref, seg_ref, w_ref, sems = refs[-8:]
    me = me_ref[0]
    own = lax.rem(me, blocks)
    copies = load_shards(parts, me, w_ref, sems, rows, True)
    width = h_ref.shape[1]
    wait_all(copies)
    gains_ref[...] = wide(w_ref[:, 3 * width :]).T[:8]
    gain = gains_ref[0:1, :]
    core = lax.rem(me // CORE_BIT, 2)
    for r in range(blocks):
        x_ref = xs[r // 4].at[r % 4]
        unit, scale = normed(wide(x_ref[:TILE, :]))
        hidden = (unit * gain).astype(BF16)
        block = own ^ ((r & 1) * Y_BIT | depth_mask(r >> 1, core))
        at = pl.multiple_of(block * TILE, TILE)
        h_ref[pl.ds(at, TILE), :] = hidden
        seg_ref[pl.ds(block, 1), :] = wide(x_ref[TILE : TILE + 1, :TILE])
        if r == 0:
            q_ref[...] = dot(hidden, w_ref[:, :width]).astype(BF16)
    step = 512
    for start in range(0, h_ref.shape[0], step):
        at = slice(start, start + step)
        k_ref[at, :] = dot(h_ref[at, :], w_ref[:, width : 2 * width]).astype(BF16)
        v_ref[at, :] = dot(h_ref[at, :], w_ref[:, 2 * width : 3 * width]).astype(BF16)


GELU_C = math.sqrt(2.0 / math.pi)


def ffn_kernel(me_ref, att_ref, x_ref, cot_ref, gains_ref, *refs, ff):
    mid_parts, back_parts = refs[:4], refs[4:8]
    states_ref, one_ref, do_ref, gain_grads_ref, back_keep, back_send, mid_keep, mid_send = refs[8:16]
    mid_ref, back_ref, dmid_ref, dback_ref, mid_sems, back_sems, mid_out_sems, back_out_sems, out_sems = refs[16:]
    me = me_ref[0]
    width = att_ref.shape[1]
    mid_rows = width // PEERS
    back_rows = ff // PEERS
    out_copies = load_shards(mid_parts, me, mid_ref, mid_sems, mid_rows, True, pl.ds(0, width))
    rest = pl.ds(width, mid_ref.shape[1] - width)
    mid_copies = load_shards(mid_parts, me, mid_ref, mid_sems, mid_rows, True, rest, len(out_copies))
    back_copies = load_shards(back_parts, me, back_ref, back_sems, back_rows, False)
    gain_two = gains_ref[1:2, :]
    gain_three = gains_ref[2:3, :]
    w_out = slice(0, width)
    w_in = slice(width, width + ff)
    w_proj = slice(width + ff, mid_ref.shape[1])
    wait_all(out_copies)
    resid_one = wide(x_ref[:TILE, :]) + dot(att_ref[...], mid_ref[:, w_out])
    unit_two, scale_two = normed(resid_one)
    hidden_two = (unit_two * gain_two).astype(BF16)
    wait_all(mid_copies)
    up = dot(hidden_two, mid_ref[:, w_in])
    inner = GELU_C * (up + 0.044715 * (up * up * up))
    bent = jnp.tanh(inner)
    active = (0.5 * up * (1.0 + bent)).astype(BF16)
    slope = 0.5 * (1.0 + bent) + 0.5 * up * (1.0 - bent * bent) * (GELU_C * (1.0 + 3.0 * 0.044715 * (up * up)))
    wait_all(back_copies)
    resid_two = resid_one + dot(active, back_ref[...])
    unit_three, scale_three = normed(resid_two)
    final = (unit_three * gain_three).astype(BF16)
    states_ref[...] = dot(final, mid_ref[:, w_proj]).astype(BF16)
    grad_final = dot_nt(cot_ref[...], mid_ref[:, w_proj])
    grad_two = norm_back(grad_final, gain_three, unit_three, scale_three)
    branch = grad_two.astype(BF16)
    put_blocks(dback_ref, slice(None), dot_tn(active, branch))
    back_out = store_blocks(dback_ref, me, (back_keep, back_send), back_out_sems)
    grad_up = (dot_nt(branch, back_ref[...]) * slope).astype(BF16)
    put_blocks(dmid_ref, w_in, dot_tn(hidden_two, grad_up))
    put_blocks(dmid_ref, w_proj, dot_tn(final, cot_ref[...]))
    mid_out = store_blocks(dmid_ref, me, (mid_keep, mid_send), mid_out_sems, pl.ds(width, ff + w_proj.stop - w_proj.start))
    grad_hidden = dot_nt(grad_up, mid_ref[:, w_in])
    grad_one = grad_two + norm_back(grad_hidden, gain_two, unit_two, scale_two)
    one_ref[...] = grad_one
    grad_attn = grad_one.astype(BF16)
    do_ref[...] = dot_nt(grad_attn, mid_ref[:, w_out]).astype(BF16)
    put_blocks(dmid_ref, w_out, dot_tn(att_ref[...], grad_attn))
    mid_out += store_blocks(dmid_ref, me, (mid_keep, mid_send), out_sems, pl.ds(0, width))
    gain_grads_ref[...] = jnp.zeros_like(gain_grads_ref)
    gain_grads_ref[1:2, :] = jnp.sum(grad_hidden * unit_two, axis=0, keepdims=True)
    gain_grads_ref[2:3, :] = jnp.sum(grad_final * unit_three, axis=0, keepdims=True)
    wait_all(back_out)
    wait_all(mid_out)


def rows_grad_kernel(me_ref, x_ref, rest_ref, *refs, blocks, rows):
    halves = [refs[3 * i : 3 * i + 3] for i in range(2)]
    parts = refs[6:10]
    *dh_refs, gain_grad_ref, w_ref, grad_ref, sems = refs[-6:]
    me = me_ref[0]
    own = lax.rem(me, blocks)
    width = grad_ref.shape[1]
    span = width // 2
    own_at = pl.ds(pl.multiple_of(own * TILE, TILE), TILE)
    loads = [
        load_shards(parts, me, w_ref, sems, rows, True, pl.ds(part * width, width), 16 * n) for n, part in enumerate((1, 2, 0))
    ]
    (dq_low, dk_low, dv_low), (dq_high, dk_high, dv_high) = halves
    wait_all(loads[0])
    low, high = slice(width, width + span), slice(width + span, 2 * width)
    grad_ref[...] = dot_nt(dk_low[...], w_ref[:, low]) + dot_nt(dk_high[...], w_ref[:, high])
    wait_all(loads[1])
    low, high = slice(2 * width, 2 * width + span), slice(2 * width + span, 3 * width)
    grad_ref[...] = grad_ref[...] + (dot_nt(dv_low[...], w_ref[:, low]) + dot_nt(dv_high[...], w_ref[:, high]))
    wait_all(loads[2])
    own_grad = dot_nt(dq_low[...], w_ref[:, :span]) + dot_nt(dq_high[...], w_ref[:, span:width])
    grad_ref[own_at, :] = grad_ref[own_at, :] + own_grad
    gain_grad = jnp.zeros((1, width), F32)
    core = lax.rem(me // CORE_BIT, 2)
    for r in range(blocks):
        block = own ^ ((r & 1) * Y_BIT | depth_mask(r >> 1, core))
        at = pl.ds(pl.multiple_of(block * TILE, TILE), TILE)
        grad = grad_ref[at, :]
        source = rest_ref if r // 4 else x_ref
        unit, scale = normed(wide(source[r % 4, :TILE, :]))
        gain_grad = gain_grad + jnp.sum(grad * unit, axis=0, keepdims=True)
        dh_refs[r & 1][r >> 1] = grad.astype(BF16)
    gain_grad_ref[...] = jnp.broadcast_to(gain_grad, gain_grad_ref.shape)


def qkv_grad_kernel(me_ref, h_ref, *refs, marks, blocks):
    halves = [refs[3 * i : 3 * i + 3] for i in range(2)]
    keep, send, dw_ref, out_sems = refs[6 + marks :]
    me = me_ref[0]
    own = lax.rem(me, blocks)
    width = h_ref.shape[1]
    span = width // 2
    own_at = pl.ds(pl.multiple_of(own * TILE, TILE), TILE)
    for i, (dq_ref, dk_ref, dv_ref) in enumerate(halves):
        put_blocks(dw_ref, slice(i * span, (i + 1) * span), dot_tn(h_ref[own_at, :], dq_ref[...]))
        put_blocks(dw_ref, slice(width + i * span, width + (i + 1) * span), dot_tn(h_ref[...], dk_ref[...]))
        put_blocks(dw_ref, slice(2 * width + i * span, 2 * width + (i + 1) * span), dot_tn(h_ref[...], dv_ref[...]))
    wait_all(store_blocks(dw_ref, me, (keep, send), out_sems))


def shaped(dims, kind):
    return jax.ShapeDtypeStruct(dims, kind)


def cube_body(inputs, segments, w_query, w_key, w_value, w_out, w_in, w_back, w_proj, gain_attn, gain_ffn, gain_final, rel_table, cotangent):
    blocks = lax.axis_size("blk")
    tokens, width = inputs.shape[1:]
    ff = w_in.shape[1]
    proj = w_proj.shape[1]
    heads = rel_table.shape[1]
    length = tokens * blocks
    rows = w_query.shape[0]
    back_rows = w_back.shape[0]
    own = lax.axis_index("blk").reshape(1).astype(jnp.int32)
    me = (lax.axis_index("head") * blocks + lax.axis_index("blk")).reshape(1).astype(jnp.int32)
    dma = pltpu.SemaphoreType.DMA((PEERS,))

    gains = jnp.stack([gain_attn, gain_ffn, gain_final], 1)
    gains = jnp.pad(gains, ((0, 0), (0, TILE - gains.shape[1])))
    pack_qkv = jnp.concatenate([w_query, w_key, w_value, gains], 1)
    pack_mid = jnp.concatenate([w_out, w_in, w_proj], 1)
    qkv_lanes = pack_qkv.shape[1]
    mid_lanes = pack_mid.shape[1]
    seg_row = jnp.pad(segments.astype(BF16), ((0, 7), (0, width - tokens)))
    own_x = jnp.concatenate([inputs[0], seg_row], 0)
    x_pair = jnp.stack([own_x, swap(own_x, Y_BIT)])
    qkv_first = swap(pack_qkv, NEAR_BIT, OVER_BIT)
    qkv_column = gather_depth(pack_qkv, qkv_first)
    x_half = jnp.concatenate([x_pair, swap(x_pair, NEAR_BIT, OVER_BIT)], 0)
    x_rest = swap(x_half, OVER_BIT, NEAR_BIT)
    qkv_parts = y_pairs(*gather_plane(qkv_column))
    qkv_parts = qkv_parts + [swap(part, CORE_BIT) for part in qkv_parts]
    pack_mid = tied(pack_mid, qkv_column)
    mid_first = swap(pack_mid, NEAR_BIT, OVER_BIT)
    mid_plane = gather_plane(gather_depth(pack_mid, mid_first))
    back_column = gather_depth(tied(w_back, mid_first))
    back_plane = gather_plane(back_column)
    hidden, key, value, query, gain_rows, kseg = pl.pallas_call(
        functools.partial(project_kernel, blocks=blocks, rows=rows),
        in_specs=[SMEM] + [WHOLE] * 2 + [ANY] * 6,
        out_specs=[WHOLE] * 6,
        out_shape=[
            shaped((length, width), BF16),
            shaped((length, width), BF16),
            shaped((length, width), BF16),
            shaped((tokens, width), BF16),
            shaped((8, width), F32),
            shaped((blocks, TILE), F32),
        ],
        scratch_shapes=[pltpu.VMEM((width, qkv_lanes), BF16), dma],
        compiler_params=pltpu.CompilerParams(vmem_limit_bytes=24 * MIB),
        cost_estimate=pl.CostEstimate(flops=2 * length * width * 2 * width, transcendentals=0, bytes_accessed=30 << 20),
        name="project",
    )(me, x_half, x_rest, *qkv_parts, mid_plane[0], back_column)
    bias = bias_rows(rel_table)
    attend, _ = attention_calls(length, width, heads, marks=1)
    qseg = segments.reshape(tokens, 1).astype(F32)
    attended, attended_low, lse = attend(own, query, key, value, qseg, kseg, bias, back_plane[0])
    mid_parts = y_pairs(*(tied(part, attended_low) for part in mid_plane))
    mid_parts = mid_parts + [swap(part, CORE_BIT) for part in mid_parts]
    back_parts = [*back_plane, *(swap(part, CORE_BIT) for part in back_plane)]
    states, grad_one, grad_attended, gain_grads, back_keep, back_send, mid_keep, mid_send = pl.pallas_call(
        functools.partial(ffn_kernel, ff=ff),
        in_specs=[SMEM] + [WHOLE] * 4 + [ANY] * 8,
        out_specs=[WHOLE] * 4 + [ANY] * 4,
        out_shape=[
            shaped((tokens, proj), BF16),
            shaped((tokens, width), F32),
            shaped((tokens, width), BF16),
            shaped((8, width), F32),
            shaped((PEERS // 2, back_rows, width), BF16),
            shaped((PEERS // 2, back_rows, width), BF16),
            shaped((PEERS // 2, rows, mid_lanes), BF16),
            shaped((PEERS // 2, rows, mid_lanes), BF16),
        ],
        scratch_shapes=[
            pltpu.VMEM((width, mid_lanes), BF16),
            pltpu.VMEM((ff, width), BF16),
            pltpu.VMEM((PEERS, rows, mid_lanes), BF16),
            pltpu.VMEM((PEERS, back_rows, width), BF16),
            dma,
            dma,
            dma,
            dma,
            dma,
        ],
        compiler_params=pltpu.CompilerParams(vmem_limit_bytes=56 * MIB),
        cost_estimate=pl.CostEstimate(flops=6 * 2 * tokens * width * (ff + width), transcendentals=0, bytes_accessed=70 << 20),
        name="ffn",
    )(me, attended_low, own_x, cotangent[0], gain_rows, *mid_parts, *back_parts)
    back_terms = [back_keep, swap(back_send, CORE_BIT)]
    mid_terms = [mid_keep, swap(mid_send, CORE_BIT)]
    common = (own, query, key, value, grad_attended, attended, lse, qseg, kseg, bias)
    _, attend_back = attention_calls(length, width, heads, 0, heads // 4)
    *first_grads, first_sums = attend_back(*common)
    back_sent, mid_sent = next_sent(back_terms), next_sent(mid_terms)
    _, attend_back = attention_calls(length, width, heads, heads // 4, heads // 4, marks=2)
    *second_grads, second_sums = attend_back(*common, back_sent, mid_sent)
    back_terms = halved(back_terms, FIRST_SIDE, back_sent)
    mid_terms = halved(mid_terms, FIRST_SIDE, mid_sent)
    back_sent = next_sent(back_terms)
    grad_parts = (*first_grads, *second_grads)
    lanes = 3 * width
    qkv_keep, qkv_send = pl.pallas_call(
        functools.partial(qkv_grad_kernel, marks=1, blocks=blocks),
        in_specs=[SMEM] + [WHOLE] * 7 + [ANY],
        out_specs=[ANY, ANY],
        out_shape=[shaped((PEERS // 2, rows, lanes), BF16), shaped((PEERS // 2, rows, lanes), BF16)],
        scratch_shapes=[pltpu.VMEM((PEERS, rows, lanes), BF16), dma],
        compiler_params=pltpu.CompilerParams(vmem_limit_bytes=26 * MIB),
        cost_estimate=pl.CostEstimate(flops=2 * 2 * length * width * width, transcendentals=0, bytes_accessed=30 << 20),
        name="qkv_grad",
    )(me, hidden, *grad_parts, back_sent)
    back_terms = halved(back_terms, SECOND_SIDE, back_sent)
    back_sent = next_sent(back_terms)
    qkv_terms = [qkv_keep, swap(qkv_send, CORE_BIT)]
    mid_sent = tied(next_sent(mid_terms), qkv_keep)
    qkv_sent = next_sent(qkv_terms)
    rows_keep, rows_send, gain_grad = pl.pallas_call(
        functools.partial(rows_grad_kernel, blocks=blocks, rows=rows),
        in_specs=[SMEM] + [WHOLE] * 8 + [ANY] * 7,
        out_specs=[WHOLE] * 3,
        out_shape=[shaped((blocks // 2, tokens, width), BF16)] * 2 + [shaped((8, width), F32)],
        scratch_shapes=[pltpu.VMEM((width, qkv_lanes), BF16), pltpu.VMEM((length, width), F32), pltpu.SemaphoreType.DMA((48,))],
        compiler_params=pltpu.CompilerParams(vmem_limit_bytes=30 * MIB),
        cost_estimate=pl.CostEstimate(flops=2 * 2 * length * width * width, transcendentals=0, bytes_accessed=30 << 20),
        name="rows_grad",
    )(me, x_half, x_rest, *grad_parts, *qkv_parts, back_sent, mid_sent, qkv_sent)
    qkv_terms = halved(qkv_terms, FIRST_SIDE, qkv_sent)
    mid_terms = halved(mid_terms, SECOND_SIDE, mid_sent)
    row_terms = [rows_keep, swap(rows_send, Y_BIT)]
    back_terms = halved(back_terms, FIRST_DEPTH, back_sent)
    mid_terms = halved(mid_terms, FIRST_DEPTH)
    qkv_sent = next_sent(qkv_terms)
    qkv_terms = halved(qkv_terms, SECOND_SIDE, qkv_sent)
    after_sides = qkv_sent
    row_terms = halved(row_terms, FIRST_DEPTH, tied(next_sent(row_terms), qkv_sent))
    back_terms = halved(back_terms, SECOND_DEPTH, tied(next_sent(back_terms), qkv_sent))
    mid_terms = halved(mid_terms, SECOND_DEPTH, tied(next_sent(mid_terms), qkv_sent))
    qkv_sent = next_sent(qkv_terms)
    qkv_terms = halved(qkv_terms, FIRST_DEPTH, qkv_sent)
    row_terms = halved(row_terms, SECOND_DEPTH)
    qkv_terms = halved(qkv_terms, SECOND_DEPTH)
    reduced_back, reduced_mid, reduced_qkv, grad_hidden = (
        part_of(terms, 0, 1)[0] for terms in (back_terms, mid_terms, qkv_terms, row_terms)
    )
    sums = jnp.concatenate([first_sums, second_sums], 0)
    unit, scale = normed(wide(inputs[0]))
    input_gradient_rows = grad_one + norm_back(grad_hidden, gain_rows[0], unit, scale)
    buckets = rel_table.shape[0]
    table = table_grad(sums, heads, buckets)[:, :heads].reshape(1, -1, TILE)
    gain_grads = jnp.stack([gain_grad[0], gain_grads[1], gain_grads[2]]).reshape(3, PEERS, rows)
    gain_grads = jnp.pad(gain_grads.transpose(1, 0, 2), ((0, 0), (0, 8 - 3 - table.shape[1]), (0, TILE - rows)))
    small = jnp.concatenate([jnp.broadcast_to(table, (PEERS,) + table.shape[1:]), gain_grads], 1)
    small = tied(small, after_sides)
    small = jnp.sum(lax.all_to_all(small, AXES, 0, 0), axis=0)
    first = table.shape[1]
    table = small[:first].reshape(buckets, heads)
    return outputs_of(
        states, input_gradient_rows, reduced_qkv, reduced_mid, reduced_back, small[first : first + 3, :rows], table, width, ff
    )


def body(*args):
    cube = lax.axis_size("head") == 4 and lax.axis_size("blk") == 8
    return (cube_body if cube else general_body)(*args)


def solution(mesh):
    rows = P(("head", "blk"), None)
    line = P(("head", "blk"))
    tokens = P("head", "blk", None)
    in_specs = (tokens, P("head", "blk")) + (rows,) * 7 + (line,) * 3 + (P(), tokens)
    out_specs = (tokens, tokens) + (rows,) * 7 + (line,) * 3 + (P(),)
    return jax.shard_map(body, mesh=mesh, in_specs=in_specs, out_specs=out_specs, check_vma=False)
```

```python
import functools
import math

import jax
import jax.numpy as jnp
import numpy as np
from jax import lax
from jax.experimental import pallas as pl
from jax.experimental.pallas import tpu as pltpu
from jax.sharding import PartitionSpec as P

BORDERS = (12, 16, 23, 32, 46, 64, 91)
MASKED = -1e30
EPS = 1e-6
TILE = 128
WIN = 512
BF16 = jnp.bfloat16
F32 = jnp.float32
AXES = ("head", "blk")
MIB = 1024 * 1024


def bucket_np(offset):
    distance = np.abs(offset)
    beyond = 8 + sum((distance >= border).astype(np.int64) for border in BORDERS)
    within = np.minimum(np.where(distance < 8, distance, beyond), 15)
    return within + 16 * (offset > 0)


def window_offsets():
    k = np.arange(WIN)
    return np.where(k < WIN - TILE, k - TILE, k - WIN - TILE)


def dot(a, b):
    return jnp.dot(a, b, preferred_element_type=F32)


def dot_nt(a, b):
    return lax.dot_general(a, b, (((1,), (1,)), ((), ())), preferred_element_type=F32)


def dot_tn(a, b):
    return lax.dot_general(a, b, (((0,), (0,)), ((), ())), preferred_element_type=F32)


class Links:
    def __init__(self):
        self.blocks = lax.axis_size("blk")
        self.total = lax.axis_size("head") * self.blocks
        self.me = lax.axis_index("head") * self.blocks + lax.axis_index("blk")
        self.bits = [1 << k for k in range(int(math.log2(self.total)))]
        self.blk_bits = [bit for bit in self.bits if bit < self.blocks]
        self.head_bits = [bit for bit in self.bits if bit >= self.blocks]

    def swap(self, value, bit):
        return lax.ppermute(value, AXES, [(i, i ^ bit) for i in range(self.total)])

    def mine(self, bit):
        return (self.me & bit) != 0


def gather_rows(links, shard, order, all_bits):
    high_first = sorted(all_bits, reverse=True)
    value = shard.reshape((1,) * len(high_first) + shard.shape)
    for bit in order:
        axis = high_first.index(bit)
        other = links.swap(value, bit)
        value = jnp.where(
            links.mine(bit),
            jnp.concatenate([other, value], axis),
            jnp.concatenate([value, other], axis),
        )
    return value.reshape((-1,) + shard.shape[1:])


def scatter_sum(links, whole, order, all_bits):
    high_first = sorted(all_bits, reverse=True)
    count = len(high_first)
    rows = whole.shape[0] >> count
    value = whole.reshape((2,) * count + (rows,) + whole.shape[1:])
    for bit in order:
        axis = high_first.index(bit)
        side = links.mine(bit).astype(jnp.int32)
        sent = lax.dynamic_slice_in_dim(value, 1 - side, 1, axis).astype(BF16)
        kept = lax.dynamic_slice_in_dim(value, side, 1, axis)
        value = kept.astype(F32) + links.swap(sent, bit).astype(F32)
    return value.reshape((rows,) + whole.shape[1:])


def bias_tiles(bias_ref, tiles_ref, head_row, side):
    row = bias_ref[pl.ds(head_row, 1), :]
    near = pltpu.roll(jnp.broadcast_to(row[:, :WIN], (TILE, WIN)), 0, 1, stride=1, stride_axis=0)
    rows = pl.ds(side * TILE, TILE)
    tiles_ref[0, rows, :] = jnp.broadcast_to(row[:, WIN : WIN + 1], (TILE, TILE))
    for t in range(3):
        tiles_ref[1 + t, rows, :] = near[:, t * TILE : (t + 1) * TILE]
    tiles_ref[4, rows, :] = jnp.broadcast_to(row[:, WIN + 1 : WIN + 2], (TILE, TILE))


def stacked(pair):
    lane = lax.broadcasted_iota(jnp.int32, pair.shape, 1)
    zero = jnp.zeros_like(pair)
    half = pair.shape[1] // 2
    return jnp.concatenate([jnp.where(lane < half, pair, zero), jnp.where(lane < half, zero, pair)], 0)


def unstacked(both):
    rows = both.shape[0] // 2
    lane = lax.broadcasted_iota(jnp.int32, (rows, both.shape[1]), 1)
    return jnp.where(lane < both.shape[1] // 2, both[:rows], both[rows:])


def tile_kind(key_tile, own_tile):
    return jnp.clip(key_tile - own_tile, -2, 2) + 2


def scores_into(chunk, chunk_tiles, own, q2, k_ref, qseg, kseg_ref, tiles_ref, s_ref):
    base = chunk * chunk_tiles * TILE
    raw = dot_nt(q2, k_ref[pl.ds(base, chunk_tiles * TILE), :])
    parts = []
    for t in range(chunk_tiles):
        at = base + t * TILE
        near = tiles_ref[tile_kind(chunk * chunk_tiles + t, own)]
        allowed = qseg == kseg_ref[pl.ds(chunk * chunk_tiles + t, 1), :]
        tile = jnp.where(allowed, raw[:, t * TILE : (t + 1) * TILE] + near, MASKED)
        s_ref[:, pl.ds(at, TILE)] = tile
        parts.append(tile)
    return parts


def attend_kernel(own_ref, q_ref, k_ref, v_ref, qseg_ref, kseg_ref, bias_ref, *refs, marks, chunks, chunk_tiles):
    o_ref, low_ref, lse_ref, tiles_ref, s_ref = refs[marks:]
    pair = pl.program_id(0)
    own = own_ref[0]
    for side in range(2):
        bias_tiles(bias_ref, tiles_ref, pair * 2 + side, side)
    q2 = stacked(q_ref[...])
    qseg = jnp.concatenate([qseg_ref[...], qseg_ref[...]], 0)

    def first(chunk, high):
        parts = scores_into(chunk, chunk_tiles, own, q2, k_ref, qseg, kseg_ref, tiles_ref, s_ref)
        return functools.reduce(jnp.maximum, parts, high)

    def second(chunk, total):
        for t in range(chunk_tiles):
            at = pl.ds((chunk * chunk_tiles + t) * TILE, TILE)
            powers = jnp.exp(s_ref[:, at] - high)
            s_ref[:, at] = powers
            total = total + powers
        return total

    def third(chunk, acc):
        base = chunk * chunk_tiles * TILE
        at = pl.ds(base, chunk_tiles * TILE)
        low = (s_ref[:, at] * inverse).astype(BF16)
        return acc + dot(low, v_ref[at, :])

    def loop(body, start):
        return body(0, start) if chunks == 1 else lax.fori_loop(0, chunks, body, start)

    high = loop(first, jnp.full((2 * TILE, TILE), MASKED, F32))
    high = jnp.max(high, axis=1, keepdims=True)
    total = jnp.sum(loop(second, jnp.zeros((2 * TILE, TILE), F32)), axis=1, keepdims=True)
    inverse = 1.0 / total
    out = unstacked(loop(third, jnp.zeros((2 * TILE, TILE), F32)))
    o_ref[...] = out
    low_ref[...] = out.astype(BF16)
    lse_ref[...] = jnp.broadcast_to(high + jnp.log(total), (2 * TILE, TILE))


def attend_back_kernel(own_ref, q_ref, k_ref, v_ref, do_ref, o_ref, lse_ref, qseg_ref, kseg_ref, bias_ref, *refs, first, marks, chunks, chunk_tiles):
    dq_ref, dk_ref, dv_ref, sums_ref, tiles_ref, s_ref, near_ref = refs[marks:]
    pair = pl.program_id(0) + first
    own = own_ref[0]
    for side in range(2):
        bias_tiles(bias_ref, tiles_ref, pair * 2 + side, side)
    q2 = stacked(q_ref[...])
    do2 = stacked(do_ref[...])
    delta = jnp.sum(stacked(do_ref[...].astype(F32) * o_ref[...]), axis=1, keepdims=True)
    lse = lse_ref[:, :1]
    qseg = jnp.concatenate([qseg_ref[...], qseg_ref[...]], 0)
    near_ref[...] = jnp.zeros_like(near_ref)

    def step(chunk, carried):
        acc, left, right = carried
        base = chunk * chunk_tiles * TILE
        at = pl.ds(base, chunk_tiles * TILE)
        scores_into(chunk, chunk_tiles, own, q2, k_ref, qseg, kseg_ref, tiles_ref, s_ref)
        probs = jnp.exp(s_ref[:, at] - lse)
        grad_probs = dot_nt(do2, v_ref[at, :])
        grads = (probs * (grad_probs - delta)).astype(BF16)
        acc = acc + dot(grads, k_ref[at, :])
        dk_ref[at, :] = dot_tn(grads, q2).astype(BF16)
        dv_ref[at, :] = dot_tn(probs.astype(BF16), do2).astype(BF16)
        wide = grads.astype(F32)
        for t in range(chunk_tiles):
            gap = chunk * chunk_tiles + t - own
            tile = wide[:, t * TILE : (t + 1) * TILE]
            left = left + jnp.where(gap < -1, tile, 0.0)
            right = right + jnp.where(gap > 1, tile, 0.0)

            @pl.when(jnp.abs(gap) <= 1)
            def _():
                near_ref[jnp.clip(gap + 1, 0, 2)] = tile

        return acc, left, right

    zero = jnp.zeros((2 * TILE, TILE), F32)
    start = (zero, zero, zero)
    acc, left, right = step(0, start) if chunks == 1 else lax.fori_loop(0, chunks, step, start)
    dq_ref[...] = unstacked(acc).astype(BF16)
    flip = (
        lax.broadcasted_iota(jnp.int32, (TILE, TILE), 0) + lax.broadcasted_iota(jnp.int32, (TILE, TILE), 1) == TILE - 1
    ).astype(BF16)
    for side in range(2):
        rows = slice(side * TILE, (side + 1) * TILE)
        window = jnp.concatenate([near_ref[t, rows, :] for t in range(4)], 1).astype(BF16)
        turned = pltpu.roll(dot(flip, window), 0, 1, stride=1, stride_axis=0)
        near_sum = jnp.sum(turned, axis=0, keepdims=True)
        far = [jnp.sum(jnp.sum(part[rows], axis=0, keepdims=True), axis=1, keepdims=True) for part in (left, right)]
        sums_ref[0, side : side + 1, :WIN] = near_sum
        lane = lax.broadcasted_iota(jnp.int32, (1, TILE), 1)
        sums_ref[0, side : side + 1, WIN:] = jnp.where(lane == 0, far[0], jnp.where(lane == 1, far[1], 0.0))


def attention_calls(length, width, heads, first=0, pairs=None, marks=0):
    total = heads // 2
    pairs = pairs or total
    tiles = length // TILE
    chunk_tiles = min(8, tiles)
    chunks = tiles // chunk_tiles
    wide = WIN + TILE
    lanes = width // total
    any_spec = pl.BlockSpec(memory_space=pl.ANY)
    own_spec = pl.BlockSpec(memory_space=pltpu.SMEM)
    q_spec = pl.BlockSpec((TILE, lanes), lambda p: (0, p + first))
    k_spec = pl.BlockSpec((length, lanes), lambda p: (0, p + first))
    dq_spec = pl.BlockSpec((TILE, lanes), lambda p: (0, p))
    dk_spec = pl.BlockSpec((length, lanes), lambda p: (0, p))
    qseg_spec = pl.BlockSpec((TILE, 1), lambda p: (0, 0))
    kseg_spec = pl.BlockSpec((tiles, TILE), lambda p: (0, 0))
    bias_spec = pl.BlockSpec((heads, wide), lambda p: (0, 0))
    lse_spec = pl.BlockSpec((2 * TILE, TILE), lambda p: (p + first, 0))
    sums_spec = pl.BlockSpec((1, 2, wide), lambda p: (p, 0, 0))
    scratch = [pltpu.VMEM((5, 2 * TILE, TILE), F32), pltpu.VMEM((2 * TILE, length), F32)]
    params = pltpu.CompilerParams(vmem_limit_bytes=(14 + length // 256) * MIB)

    def shape(dims, kind):
        return jax.ShapeDtypeStruct(dims, kind)

    forward = pl.pallas_call(
        functools.partial(attend_kernel, marks=marks, chunks=chunks, chunk_tiles=chunk_tiles),
        grid=(pairs,),
        in_specs=[own_spec, q_spec, k_spec, k_spec, qseg_spec, kseg_spec, bias_spec] + [any_spec] * marks,
        out_specs=[q_spec, q_spec, lse_spec],
        out_shape=[shape((TILE, width), F32), shape((TILE, width), BF16), shape((pairs * 2 * TILE, TILE), F32)],
        scratch_shapes=scratch,
        compiler_params=params,
        cost_estimate=pl.CostEstimate(flops=0, transcendentals=0, bytes_accessed=30 << 20),
        name="attend",
    )
    backward = pl.pallas_call(
        functools.partial(attend_back_kernel, first=first, marks=marks, chunks=chunks, chunk_tiles=chunk_tiles),
        grid=(pairs,),
        in_specs=[own_spec, q_spec, k_spec, k_spec, q_spec, q_spec, lse_spec, qseg_spec, kseg_spec, bias_spec]
        + [any_spec] * marks,
        out_specs=[dq_spec, dk_spec, dk_spec, sums_spec],
        out_shape=[
            shape((TILE, pairs * lanes), BF16),
            shape((length, pairs * lanes), BF16),
            shape((length, pairs * lanes), BF16),
            shape((pairs, 2, wide), F32),
        ],
        scratch_shapes=scratch + [pltpu.VMEM((4, 2 * TILE, TILE), F32)],
        compiler_params=params,
        cost_estimate=pl.CostEstimate(flops=0, transcendentals=0, bytes_accessed=48 << 20),
        name="attend_back",
    )
    return forward, backward


def normed(rows):
    scale = lax.rsqrt(jnp.mean(rows * rows, axis=-1, keepdims=True) + EPS)
    return rows * scale, scale


def norm_back(grad, gain, unit, scale):
    scaled = grad * gain
    return (scaled - unit * jnp.mean(scaled * unit, axis=-1, keepdims=True)) * scale


def bias_rows(rel_table):
    onehot = np.zeros((WIN + TILE, rel_table.shape[0]), np.float32)
    onehot[np.arange(WIN), bucket_np(window_offsets())] = 1.0
    onehot[WIN, 15] = 1.0
    onehot[WIN + 1, 31] = 1.0
    return lax.dot_general(
        rel_table, jnp.asarray(onehot, BF16), (((0,), (1,)), ((), ())), preferred_element_type=F32
    )


def table_grad(sums, heads, buckets):
    lane = np.arange(WIN)
    diagonal = np.zeros((WIN + TILE, buckets), np.float32)
    diagonal[lane, bucket_np(lane - (2 * TILE - 1))] = 1.0
    diagonal[WIN, 15] = 1.0
    diagonal[WIN + 1, 31] = 1.0
    table = lax.dot_general(
        jnp.asarray(diagonal),
        sums.reshape(heads, WIN + TILE),
        (((0,), (1,)), ((), ())),
        precision=lax.Precision.HIGHEST,
    )
    return jnp.pad(table, ((0, 0), (0, TILE - heads)))


def outputs_of(states, input_gradient_rows, reduced_qkv, reduced_mid, reduced_back, gain_grads, table, width, ff):
    return (
        states[None],
        input_gradient_rows[None],
        reduced_qkv[:, :width],
        reduced_qkv[:, width : 2 * width],
        reduced_qkv[:, 2 * width : 3 * width],
        reduced_mid[:, :width],
        reduced_mid[:, width : width + ff],
        reduced_back,
        reduced_mid[:, width + ff :],
        gain_grads[0],
        gain_grads[1],
        gain_grads[2],
        table,
    )


def general_body(inputs, segments, w_query, w_key, w_value, w_out, w_in, w_back, w_proj, gain_attn, gain_ffn, gain_final, rel_table, cotangent):
    links = Links()
    bits = links.bits
    tokens, width = inputs.shape[1:]
    ff = w_in.shape[1]
    proj = w_proj.shape[1]
    buckets, heads = rel_table.shape
    length = tokens * links.blocks
    rows = w_query.shape[0]
    own = lax.axis_index("blk").reshape(1).astype(jnp.int32)

    gains = jnp.stack([gain_attn, gain_ffn, gain_final], 1)
    gains = jnp.pad(gains, ((0, 0), (0, TILE - gains.shape[1])))
    pack_qkv = jnp.concatenate([w_query, w_key, w_value, gains], 1)
    pack_mid = jnp.concatenate([w_out, w_in, w_proj], 1)
    blk_down = [b for b in links.blk_bits if b > 1] + [1]
    order_a = blk_down + links.head_bits[::-1]
    own_rows = inputs[0]
    all_rows = gather_rows(links, own_rows, blk_down, links.blk_bits)
    seg_all = gather_rows(links, segments, blk_down, links.blk_bits)
    full_qkv = gather_rows(links, pack_qkv, order_a, bits)
    full_mid = gather_rows(links, pack_mid, order_a, bits)
    full_back = gather_rows(links, w_back, order_a, bits)
    full_query, full_key, full_value = (full_qkv[:, i * width : (i + 1) * width] for i in range(3))
    gain_rows = full_qkv[:, 3 * width :].astype(F32).T
    gain_one, gain_two, gain_three = gain_rows[0], gain_rows[1], gain_rows[2]
    full_out = full_mid[:, :width]
    full_in = full_mid[:, width : width + ff]
    full_proj = full_mid[:, width + ff :]

    bias = bias_rows(rel_table)

    states_in = own_rows.astype(F32)
    unit_all, scale_all = normed(all_rows.astype(F32))
    hidden_all = (unit_all * gain_one).astype(BF16)
    unit_one, scale_one = normed(states_in)
    hidden_one = (unit_one * gain_one).astype(BF16)
    query = dot(hidden_one, full_query).astype(BF16)
    key = dot(hidden_all, full_key).astype(BF16)
    value = dot(hidden_all, full_value).astype(BF16)
    attend, attend_back = attention_calls(length, width, heads)
    qseg = segments.reshape(tokens, 1)
    kseg = seg_all
    attended, attended_low, lse = attend(own, query, key, value, qseg, kseg, bias)
    resid_one = states_in + dot(attended_low, full_out)
    unit_two, scale_two = normed(resid_one)
    hidden_two = (unit_two * gain_two).astype(BF16)
    upward = dot(hidden_two, full_in)
    active, back_gelu = jax.vjp(lambda u: jax.nn.gelu(u, approximate=True), upward)
    active_low = active.astype(BF16)
    resid_two = resid_one + dot(active_low, full_back)
    unit_three, scale_three = normed(resid_two)
    final_low = (unit_three * gain_three).astype(BF16)
    states = dot(final_low, full_proj).astype(BF16)

    arriving = cotangent[0]
    grad_proj = dot_tn(final_low, arriving)
    grad_final = dot_nt(arriving, full_proj)
    grad_gain_three = jnp.sum(grad_final * unit_three, axis=0)
    grad_two = norm_back(grad_final, gain_three, unit_three, scale_three)
    grad_branch = grad_two.astype(BF16)
    grad_back = dot_tn(active_low, grad_branch)
    grad_up = back_gelu(dot_nt(grad_branch, full_back))[0].astype(BF16)
    grad_in = dot_tn(hidden_two, grad_up)
    grad_hidden_two = dot_nt(grad_up, full_in)
    grad_gain_two = jnp.sum(grad_hidden_two * unit_two, axis=0)
    grad_one = grad_two + norm_back(grad_hidden_two, gain_two, unit_two, scale_two)
    grad_attn = grad_one.astype(BF16)
    grad_out = dot_tn(attended_low, grad_attn)
    grad_attended = dot_nt(grad_attn, full_out).astype(BF16)
    grad_q, grad_k, grad_v, sums = attend_back(
        own, query, key, value, grad_attended, attended, lse, qseg, kseg, bias
    )
    grad_query = dot_tn(hidden_one, grad_q)
    grad_key = dot_tn(hidden_all, grad_k)
    grad_value = dot_tn(hidden_all, grad_v)
    grad_rows = dot_nt(grad_k, full_key) + dot_nt(grad_v, full_value)
    own_part = dot_nt(grad_q, full_query)
    first = lax.axis_index("blk") * tokens
    grad_rows = lax.dynamic_update_slice_in_dim(
        grad_rows, lax.dynamic_slice_in_dim(grad_rows, first, tokens, 0) + own_part, first, 0
    )
    grad_gain_one = jnp.sum(grad_rows * unit_all, axis=0)

    up_order = links.head_bits + [1] + [b for b in links.blk_bits if b > 1][::-1]
    blk_up = [1] + [b for b in links.blk_bits if b > 1][::-1]
    reduced_back = scatter_sum(links, grad_back, up_order, bits)
    reduced_mid = scatter_sum(links, jnp.concatenate([grad_out, grad_in, grad_proj], 1), up_order, bits)
    gain_grads = jnp.stack([grad_gain_one, grad_gain_two, grad_gain_three], 1)
    gain_grads = jnp.pad(gain_grads, ((0, 0), (0, TILE - 3)))
    reduced_qkv = scatter_sum(
        links, jnp.concatenate([grad_query, grad_key, grad_value, gain_grads], 1), up_order, bits
    )
    grad_hidden_one = scatter_sum(links, grad_rows, blk_up, links.blk_bits)
    input_gradient_rows = grad_one + norm_back(grad_hidden_one, gain_one, unit_one, scale_one)

    table = table_grad(sums, heads, rel_table.shape[0])
    for bit in bits:
        table = table + links.swap(table, bit)
    gain_grads = reduced_qkv[:, 3 * width :].T
    return outputs_of(
        states, input_gradient_rows, reduced_qkv, reduced_mid, reduced_back, gain_grads, table[:, :heads], width, ff
    )


X_BIT, CORE_BIT, Y_BIT = 16, 8, 1
NEAR_BIT, OVER_BIT = 2, 4
DEPTH = 4
PEERS = 32


def swap(value, mask, other_mask=None):
    masks = (mask, mask if other_mask is None else other_mask)
    return lax.ppermute(value, AXES, [(i, i ^ masks[(i // CORE_BIT) % 2]) for i in range(PEERS)])


def depth_mask(place, core):
    return (0, NEAR_BIT + core * (OVER_BIT - NEAR_BIT), OVER_BIT - core * (OVER_BIT - NEAR_BIT), NEAR_BIT | OVER_BIT)[place]


def side_masks(core):
    return Y_BIT + core * (X_BIT - Y_BIT), X_BIT - core * (X_BIT - Y_BIT)


def tied(value, *earlier):
    whole = functools.reduce(jnp.logical_and, [mark[(0,) * mark.ndim] == mark[(0,) * mark.ndim] for mark in earlier])
    return jnp.where(whole, value, jnp.zeros_like(value))


def gather_depth(own, first=None):
    first = swap(own, NEAR_BIT, OVER_BIT) if first is None else first
    pair = jnp.stack([own, first])
    return jnp.concatenate([pair, swap(pair, OVER_BIT, NEAR_BIT)], 0)


def gather_plane(column):
    half = jnp.concatenate([column, swap(column, Y_BIT, X_BIT)], 0)
    return half, swap(half, X_BIT, Y_BIT)


def y_pairs(half, rest):
    second = (lax.axis_index("head") % 2) == 1
    high = (lax.axis_index("blk") % 2) == 1
    pairs = (
        (half[:DEPTH], jnp.where(second, rest[:DEPTH], half[DEPTH:])),
        (jnp.where(second, half[DEPTH:], rest[:DEPTH]), rest[DEPTH:]),
    )
    return [
        jnp.where(high, jnp.concatenate([other, mine], 1), jnp.concatenate([mine, other], 1)) for mine, other in pairs
    ]


def gathered_items(core, paired):
    items = []
    for c in range(2):
        here = core if c == 0 else 1 - core
        first, second = side_masks(here)
        for b in range(2):
            for k in range(DEPTH):
                depth = depth_mask(k, here)
                if paired:
                    items.append((2 * c + b, k, (c * CORE_BIT + b * X_BIT) | depth))
                else:
                    items += [
                        (2 * c + b, a * DEPTH + k, (c * CORE_BIT) | (a * first) | (b * second) | depth) for a in range(2)
                    ]
    return items


def sent_items(core):
    items = []
    for c in range(2):
        here = core if c == 0 else 1 - core
        minor, major = side_masks(here)
        for a in range(2):
            for b in range(2):
                for k in range(DEPTH):
                    place = a * 2 * DEPTH + b * DEPTH + k
                    items.append((c, place, (c * CORE_BIT) | (a * major) | (b * minor) | depth_mask(k, here)))
    return items


def wide(value):
    return value.astype(F32)


def part_of(terms, first, last):
    return sum(wide(term[first:last]) for term in terms)


def next_sent(terms):
    half = terms[-1].shape[0] // 2
    return part_of(terms, half, 2 * half).astype(BF16)


def halved(terms, masks, sent=None):
    half = terms[-1].shape[0] // 2
    return [term[:half] for term in terms] + [swap(next_sent(terms) if sent is None else sent, *masks)]


FIRST_SIDE, SECOND_SIDE = (X_BIT, Y_BIT), (Y_BIT, X_BIT)
FIRST_DEPTH, SECOND_DEPTH = (OVER_BIT, NEAR_BIT), (NEAR_BIT, OVER_BIT)


ANY = pl.BlockSpec(memory_space=pl.ANY)
SMEM = pl.BlockSpec(memory_space=pltpu.SMEM)
WHOLE = pl.BlockSpec(memory_space=pltpu.VMEM)


def load_shards(parts, me, target, sems, rows, paired, lanes=None, first=0):
    copies = []
    rows = 2 * rows if paired else rows
    core = lax.rem(me // CORE_BIT, 2)
    for n, (buffer, place, relative) in enumerate(gathered_items(core, paired)):
        index = (me ^ relative) // 2 if paired else me ^ relative
        at = pl.multiple_of(index * rows, 16)
        part, span = parts[buffer].at[place], target.at[pl.ds(at, rows), :]
        if lanes is not None:
            part, span = part.at[:, lanes], target.at[pl.ds(at, rows), lanes]
        copies.append(pltpu.make_async_copy(part, span, sems.at[first + n]))
    for copy in copies:
        copy.start()
    return copies


def store_blocks(source, me, targets, sems, lanes=None):
    copies = []
    for n, (side, place, relative) in enumerate(sent_items(lax.rem(me // CORE_BIT, 2))):
        block, target = source.at[me ^ relative], targets[side].at[place]
        if lanes is not None:
            block, target = block.at[:, lanes], target.at[:, lanes]
        copies.append(pltpu.make_async_copy(block, target, sems.at[n]))
    for copy in copies:
        copy.start()
    return copies


def put_blocks(target, lanes, value):
    rows = target.shape[1]
    for p in range(PEERS):
        target[p, :, lanes] = value[p * rows : (p + 1) * rows, :].astype(BF16)


def wait_all(copies):
    for copy in copies:
        copy.wait()


def project_kernel(me_ref, *refs, blocks, rows):
    xs = refs[:2]
    parts = refs[2:6]
    h_ref, k_ref, v_ref, q_ref, gains_ref, seg_ref, w_ref, sems = refs[-8:]
    me = me_ref[0]
    own = lax.rem(me, blocks)
    copies = load_shards(parts, me, w_ref, sems, rows, True)
    width = h_ref.shape[1]
    wait_all(copies)
    gains_ref[...] = wide(w_ref[:, 3 * width :]).T[:8]
    gain = gains_ref[0:1, :]
    core = lax.rem(me // CORE_BIT, 2)
    for r in range(blocks):
        x_ref = xs[r // 4].at[r % 4]
        unit, scale = normed(wide(x_ref[:TILE, :]))
        hidden = (unit * gain).astype(BF16)
        block = own ^ ((r & 1) * Y_BIT | depth_mask(r >> 1, core))
        at = pl.multiple_of(block * TILE, TILE)
        h_ref[pl.ds(at, TILE), :] = hidden
        seg_ref[pl.ds(block, 1), :] = wide(x_ref[TILE : TILE + 1, :TILE])
        if r == 0:
            q_ref[...] = dot(hidden, w_ref[:, :width]).astype(BF16)
    step = 512
    for start in range(0, h_ref.shape[0], step):
        at = slice(start, start + step)
        k_ref[at, :] = dot(h_ref[at, :], w_ref[:, width : 2 * width]).astype(BF16)
        v_ref[at, :] = dot(h_ref[at, :], w_ref[:, 2 * width : 3 * width]).astype(BF16)


GELU_C = math.sqrt(2.0 / math.pi)


def ffn_kernel(me_ref, att_ref, x_ref, cot_ref, gains_ref, *refs, ff):
    mid_parts, back_parts = refs[:4], refs[4:8]
    states_ref, one_ref, do_ref, gain_grads_ref, back_keep, back_send, mid_keep, mid_send = refs[8:16]
    mid_ref, back_ref, dmid_ref, dback_ref, mid_sems, back_sems, mid_out_sems, back_out_sems, out_sems = refs[16:]
    me = me_ref[0]
    width = att_ref.shape[1]
    mid_rows = width // PEERS
    back_rows = ff // PEERS
    out_copies = load_shards(mid_parts, me, mid_ref, mid_sems, mid_rows, True, pl.ds(0, width))
    rest = pl.ds(width, mid_ref.shape[1] - width)
    mid_copies = load_shards(mid_parts, me, mid_ref, mid_sems, mid_rows, True, rest, len(out_copies))
    back_copies = load_shards(back_parts, me, back_ref, back_sems, back_rows, False)
    gain_two = gains_ref[1:2, :]
    gain_three = gains_ref[2:3, :]
    w_out = slice(0, width)
    w_in = slice(width, width + ff)
    w_proj = slice(width + ff, mid_ref.shape[1])
    wait_all(out_copies)
    resid_one = wide(x_ref[:TILE, :]) + dot(att_ref[...], mid_ref[:, w_out])
    unit_two, scale_two = normed(resid_one)
    hidden_two = (unit_two * gain_two).astype(BF16)
    wait_all(mid_copies)
    up = dot(hidden_two, mid_ref[:, w_in])
    inner = GELU_C * (up + 0.044715 * (up * up * up))
    bent = jnp.tanh(inner)
    active = (0.5 * up * (1.0 + bent)).astype(BF16)
    slope = 0.5 * (1.0 + bent) + 0.5 * up * (1.0 - bent * bent) * (GELU_C * (1.0 + 3.0 * 0.044715 * (up * up)))
    wait_all(back_copies)
    resid_two = resid_one + dot(active, back_ref[...])
    unit_three, scale_three = normed(resid_two)
    final = (unit_three * gain_three).astype(BF16)
    states_ref[...] = dot(final, mid_ref[:, w_proj]).astype(BF16)
    grad_final = dot_nt(cot_ref[...], mid_ref[:, w_proj])
    grad_two = norm_back(grad_final, gain_three, unit_three, scale_three)
    branch = grad_two.astype(BF16)
    put_blocks(dback_ref, slice(None), dot_tn(active, branch))
    back_out = store_blocks(dback_ref, me, (back_keep, back_send), back_out_sems)
    grad_up = (dot_nt(branch, back_ref[...]) * slope).astype(BF16)
    put_blocks(dmid_ref, w_in, dot_tn(hidden_two, grad_up))
    put_blocks(dmid_ref, w_proj, dot_tn(final, cot_ref[...]))
    mid_out = store_blocks(dmid_ref, me, (mid_keep, mid_send), mid_out_sems, pl.ds(width, ff + w_proj.stop - w_proj.start))
    grad_hidden = dot_nt(grad_up, mid_ref[:, w_in])
    grad_one = grad_two + norm_back(grad_hidden, gain_two, unit_two, scale_two)
    one_ref[...] = grad_one
    grad_attn = grad_one.astype(BF16)
    do_ref[...] = dot_nt(grad_attn, mid_ref[:, w_out]).astype(BF16)
    put_blocks(dmid_ref, w_out, dot_tn(att_ref[...], grad_attn))
    mid_out += store_blocks(dmid_ref, me, (mid_keep, mid_send), out_sems, pl.ds(0, width))
    gain_grads_ref[...] = jnp.zeros_like(gain_grads_ref)
    gain_grads_ref[1:2, :] = jnp.sum(grad_hidden * unit_two, axis=0, keepdims=True)
    gain_grads_ref[2:3, :] = jnp.sum(grad_final * unit_three, axis=0, keepdims=True)
    wait_all(back_out)
    wait_all(mid_out)


def rows_grad_kernel(me_ref, x_ref, rest_ref, *refs, blocks, rows):
    halves = [refs[3 * i : 3 * i + 3] for i in range(2)]
    parts = refs[6:10]
    *dh_refs, gain_grad_ref, w_ref, grad_ref, sems = refs[-6:]
    me = me_ref[0]
    own = lax.rem(me, blocks)
    width = grad_ref.shape[1]
    span = width // 2
    own_at = pl.ds(pl.multiple_of(own * TILE, TILE), TILE)
    loads = [
        load_shards(parts, me, w_ref, sems, rows, True, pl.ds(part * width, width), 16 * n) for n, part in enumerate((1, 2, 0))
    ]
    (dq_low, dk_low, dv_low), (dq_high, dk_high, dv_high) = halves
    wait_all(loads[0])
    low, high = slice(width, width + span), slice(width + span, 2 * width)
    grad_ref[...] = dot_nt(dk_low[...], w_ref[:, low]) + dot_nt(dk_high[...], w_ref[:, high])
    wait_all(loads[1])
    low, high = slice(2 * width, 2 * width + span), slice(2 * width + span, 3 * width)
    grad_ref[...] = grad_ref[...] + (dot_nt(dv_low[...], w_ref[:, low]) + dot_nt(dv_high[...], w_ref[:, high]))
    wait_all(loads[2])
    own_grad = dot_nt(dq_low[...], w_ref[:, :span]) + dot_nt(dq_high[...], w_ref[:, span:width])
    grad_ref[own_at, :] = grad_ref[own_at, :] + own_grad
    gain_grad = jnp.zeros((1, width), F32)
    core = lax.rem(me // CORE_BIT, 2)
    for r in range(blocks):
        block = own ^ ((r & 1) * Y_BIT | depth_mask(r >> 1, core))
        at = pl.ds(pl.multiple_of(block * TILE, TILE), TILE)
        grad = grad_ref[at, :]
        source = rest_ref if r // 4 else x_ref
        unit, scale = normed(wide(source[r % 4, :TILE, :]))
        gain_grad = gain_grad + jnp.sum(grad * unit, axis=0, keepdims=True)
        dh_refs[r & 1][r >> 1] = grad.astype(BF16)
    gain_grad_ref[...] = jnp.broadcast_to(gain_grad, gain_grad_ref.shape)


def qkv_grad_kernel(me_ref, h_ref, *refs, marks, blocks):
    halves = [refs[3 * i : 3 * i + 3] for i in range(2)]
    keep, send, dw_ref, first_sems, last_sems = refs[6 + marks :]
    me = me_ref[0]
    own = lax.rem(me, blocks)
    width = h_ref.shape[1]
    span = width // 2
    own_at = pl.ds(pl.multiple_of(own * TILE, TILE), TILE)
    for i, (dq_ref, dk_ref, dv_ref) in enumerate(halves):
        put_blocks(dw_ref, slice(i * span, (i + 1) * span), dot_tn(h_ref[own_at, :], dq_ref[...]))
        put_blocks(dw_ref, slice(width + i * span, width + (i + 1) * span), dot_tn(h_ref[...], dk_ref[...]))
    copies = store_blocks(dw_ref, me, (keep, send), first_sems, pl.ds(0, 2 * width))
    for i, (dq_ref, dk_ref, dv_ref) in enumerate(halves):
        put_blocks(dw_ref, slice(2 * width + i * span, 2 * width + (i + 1) * span), dot_tn(h_ref[...], dv_ref[...]))
    copies += store_blocks(dw_ref, me, (keep, send), last_sems, pl.ds(2 * width, width))
    wait_all(copies)


def shaped(dims, kind):
    return jax.ShapeDtypeStruct(dims, kind)


def cube_body(inputs, segments, w_query, w_key, w_value, w_out, w_in, w_back, w_proj, gain_attn, gain_ffn, gain_final, rel_table, cotangent):
    blocks = lax.axis_size("blk")
    tokens, width = inputs.shape[1:]
    ff = w_in.shape[1]
    proj = w_proj.shape[1]
    heads = rel_table.shape[1]
    length = tokens * blocks
    rows = w_query.shape[0]
    back_rows = w_back.shape[0]
    own = lax.axis_index("blk").reshape(1).astype(jnp.int32)
    me = (lax.axis_index("head") * blocks + lax.axis_index("blk")).reshape(1).astype(jnp.int32)
    dma = pltpu.SemaphoreType.DMA((PEERS,))

    gains = jnp.stack([gain_attn, gain_ffn, gain_final], 1)
    gains = jnp.pad(gains, ((0, 0), (0, TILE - gains.shape[1])))
    pack_qkv = jnp.concatenate([w_query, w_key, w_value, gains], 1)
    pack_mid = jnp.concatenate([w_out, w_in, w_proj], 1)
    qkv_lanes = pack_qkv.shape[1]
    mid_lanes = pack_mid.shape[1]
    seg_row = jnp.pad(segments.astype(BF16), ((0, 7), (0, width - tokens)))
    own_x = jnp.concatenate([inputs[0], seg_row], 0)
    x_pair = jnp.stack([own_x, swap(own_x, Y_BIT)])
    qkv_first = swap(pack_qkv, NEAR_BIT, OVER_BIT)
    qkv_column = gather_depth(pack_qkv, qkv_first)
    x_half = jnp.concatenate([x_pair, swap(x_pair, NEAR_BIT, OVER_BIT)], 0)
    x_rest = swap(x_half, OVER_BIT, NEAR_BIT)
    qkv_parts = y_pairs(*gather_plane(qkv_column))
    qkv_parts = qkv_parts + [swap(part, CORE_BIT) for part in qkv_parts]
    pack_mid = tied(pack_mid, qkv_column)
    mid_first = swap(pack_mid, NEAR_BIT, OVER_BIT)
    mid_plane = gather_plane(gather_depth(pack_mid, mid_first))
    back_column = gather_depth(tied(w_back, mid_first))
    back_plane = gather_plane(back_column)
    hidden, key, value, query, gain_rows, kseg = pl.pallas_call(
        functools.partial(project_kernel, blocks=blocks, rows=rows),
        in_specs=[SMEM] + [WHOLE] * 2 + [ANY] * 6,
        out_specs=[WHOLE] * 6,
        out_shape=[
            shaped((length, width), BF16),
            shaped((length, width), BF16),
            shaped((length, width), BF16),
            shaped((tokens, width), BF16),
            shaped((8, width), F32),
            shaped((blocks, TILE), F32),
        ],
        scratch_shapes=[pltpu.VMEM((width, qkv_lanes), BF16), dma],
        compiler_params=pltpu.CompilerParams(vmem_limit_bytes=24 * MIB),
        cost_estimate=pl.CostEstimate(flops=2 * length * width * 2 * width, transcendentals=0, bytes_accessed=30 << 20),
        name="project",
    )(me, x_half, x_rest, *qkv_parts, mid_plane[0], back_column)
    bias = bias_rows(rel_table)
    attend, _ = attention_calls(length, width, heads, marks=1)
    qseg = segments.reshape(tokens, 1).astype(F32)
    attended, attended_low, lse = attend(own, query, key, value, qseg, kseg, bias, back_plane[0])
    mid_parts = y_pairs(*(tied(part, attended_low) for part in mid_plane))
    mid_parts = mid_parts + [swap(part, CORE_BIT) for part in mid_parts]
    back_parts = [*back_plane, *(swap(part, CORE_BIT) for part in back_plane)]
    states, grad_one, grad_attended, gain_grads, back_keep, back_send, mid_keep, mid_send = pl.pallas_call(
        functools.partial(ffn_kernel, ff=ff),
        in_specs=[SMEM] + [WHOLE] * 4 + [ANY] * 8,
        out_specs=[WHOLE] * 4 + [ANY] * 4,
        out_shape=[
            shaped((tokens, proj), BF16),
            shaped((tokens, width), F32),
            shaped((tokens, width), BF16),
            shaped((8, width), F32),
            shaped((PEERS // 2, back_rows, width), BF16),
            shaped((PEERS // 2, back_rows, width), BF16),
            shaped((PEERS // 2, rows, mid_lanes), BF16),
            shaped((PEERS // 2, rows, mid_lanes), BF16),
        ],
        scratch_shapes=[
            pltpu.VMEM((width, mid_lanes), BF16),
            pltpu.VMEM((ff, width), BF16),
            pltpu.VMEM((PEERS, rows, mid_lanes), BF16),
            pltpu.VMEM((PEERS, back_rows, width), BF16),
            dma,
            dma,
            dma,
            dma,
            dma,
        ],
        compiler_params=pltpu.CompilerParams(vmem_limit_bytes=56 * MIB),
        cost_estimate=pl.CostEstimate(flops=6 * 2 * tokens * width * (ff + width), transcendentals=0, bytes_accessed=70 << 20),
        name="ffn",
    )(me, attended_low, own_x, cotangent[0], gain_rows, *mid_parts, *back_parts)
    back_terms = [back_keep, swap(back_send, CORE_BIT)]
    mid_terms = [mid_keep, swap(mid_send, CORE_BIT)]
    common = (own, query, key, value, grad_attended, attended, lse, qseg, kseg, bias)
    _, attend_back = attention_calls(length, width, heads, 0, heads // 4)
    *first_grads, first_sums = attend_back(*common)
    back_sent, mid_sent = next_sent(back_terms), next_sent(mid_terms)
    _, attend_back = attention_calls(length, width, heads, heads // 4, heads // 4, marks=2)
    *second_grads, second_sums = attend_back(*common, back_sent, mid_sent)
    back_terms = halved(back_terms, FIRST_SIDE, back_sent)
    mid_terms = halved(mid_terms, FIRST_SIDE, mid_sent)
    back_sent = next_sent(back_terms)
    grad_parts = (*first_grads, *second_grads)
    lanes = 3 * width
    qkv_keep, qkv_send = pl.pallas_call(
        functools.partial(qkv_grad_kernel, marks=1, blocks=blocks),
        in_specs=[SMEM] + [WHOLE] * 7 + [ANY],
        out_specs=[ANY, ANY],
        out_shape=[shaped((PEERS // 2, rows, lanes), BF16), shaped((PEERS // 2, rows, lanes), BF16)],
        scratch_shapes=[pltpu.VMEM((PEERS, rows, lanes), BF16), dma, dma],
        compiler_params=pltpu.CompilerParams(vmem_limit_bytes=26 * MIB),
        cost_estimate=pl.CostEstimate(flops=2 * 2 * length * width * width, transcendentals=0, bytes_accessed=30 << 20),
        name="qkv_grad",
    )(me, hidden, *grad_parts, back_sent)
    back_terms = halved(back_terms, SECOND_SIDE, back_sent)
    back_sent = next_sent(back_terms)
    qkv_terms = [qkv_keep, swap(qkv_send, CORE_BIT)]
    mid_sent = tied(next_sent(mid_terms), qkv_keep)
    qkv_sent = next_sent(qkv_terms)
    rows_keep, rows_send, gain_grad = pl.pallas_call(
        functools.partial(rows_grad_kernel, blocks=blocks, rows=rows),
        in_specs=[SMEM] + [WHOLE] * 8 + [ANY] * 7,
        out_specs=[WHOLE] * 3,
        out_shape=[shaped((blocks // 2, tokens, width), BF16)] * 2 + [shaped((8, width), F32)],
        scratch_shapes=[pltpu.VMEM((width, qkv_lanes), BF16), pltpu.VMEM((length, width), F32), pltpu.SemaphoreType.DMA((48,))],
        compiler_params=pltpu.CompilerParams(vmem_limit_bytes=30 * MIB),
        cost_estimate=pl.CostEstimate(flops=2 * 2 * length * width * width, transcendentals=0, bytes_accessed=30 << 20),
        name="rows_grad",
    )(me, x_half, x_rest, *grad_parts, *qkv_parts, back_sent, mid_sent, qkv_sent)
    qkv_terms = halved(qkv_terms, FIRST_SIDE, qkv_sent)
    mid_terms = halved(mid_terms, SECOND_SIDE, mid_sent)
    row_terms = [rows_keep, swap(rows_send, Y_BIT)]
    back_terms = halved(back_terms, FIRST_DEPTH, back_sent)
    mid_terms = halved(mid_terms, FIRST_DEPTH)
    qkv_sent = next_sent(qkv_terms)
    qkv_terms = halved(qkv_terms, SECOND_SIDE, qkv_sent)
    after_sides = qkv_sent
    row_terms = halved(row_terms, FIRST_DEPTH, tied(next_sent(row_terms), qkv_sent))
    back_terms = halved(back_terms, SECOND_DEPTH, tied(next_sent(back_terms), qkv_sent))
    mid_terms = halved(mid_terms, SECOND_DEPTH, tied(next_sent(mid_terms), qkv_sent))
    qkv_sent = next_sent(qkv_terms)
    qkv_terms = halved(qkv_terms, FIRST_DEPTH, qkv_sent)
    row_terms = halved(row_terms, SECOND_DEPTH)
    qkv_terms = halved(qkv_terms, SECOND_DEPTH)
    reduced_back, reduced_mid, reduced_qkv, grad_hidden = (
        part_of(terms, 0, 1)[0] for terms in (back_terms, mid_terms, qkv_terms, row_terms)
    )
    sums = jnp.concatenate([first_sums, second_sums], 0)
    unit, scale = normed(wide(inputs[0]))
    input_gradient_rows = grad_one + norm_back(grad_hidden, gain_rows[0], unit, scale)
    buckets = rel_table.shape[0]
    table = table_grad(sums, heads, buckets)[:, :heads].reshape(1, -1, TILE)
    gain_grads = jnp.stack([gain_grad[0], gain_grads[1], gain_grads[2]]).reshape(3, PEERS, rows)
    gain_grads = jnp.pad(gain_grads.transpose(1, 0, 2), ((0, 0), (0, 8 - 3 - table.shape[1]), (0, TILE - rows)))
    small = jnp.concatenate([jnp.broadcast_to(table, (PEERS,) + table.shape[1:]), gain_grads], 1)
    small = tied(small, after_sides)
    small = jnp.sum(lax.all_to_all(small, AXES, 0, 0), axis=0)
    first = table.shape[1]
    table = small[:first].reshape(buckets, heads)
    return outputs_of(
        states, input_gradient_rows, reduced_qkv, reduced_mid, reduced_back, small[first : first + 3, :rows], table, width, ff
    )


def body(*args):
    cube = lax.axis_size("head") == 4 and lax.axis_size("blk") == 8
    return (cube_body if cube else general_body)(*args)


def solution(mesh):
    rows = P(("head", "blk"), None)
    line = P(("head", "blk"))
    tokens = P("head", "blk", None)
    in_specs = (tokens, P("head", "blk")) + (rows,) * 7 + (line,) * 3 + (P(), tokens)
    out_specs = (tokens, tokens) + (rows,) * 7 + (line,) * 3 + (P(),)
    return jax.shard_map(body, mesh=mesh, in_specs=in_specs, out_specs=out_specs, check_vma=False)
```
